32 devices in a mesh: seq: 4 (over y, x), head: 8 (over z, core).
Axes of the slice: x: 2, y: 2, z: 4, core: 2. Of those that a mesh axis runs over, the one named last changes fastest.
Arguments:
- inputs: bfloat16 [4096, 6144], P('seq', 'head'), may hold values from -6 to 6
- projection: bfloat16 [6144, 3, 4096], P('seq', None, 'head'), may hold values from -0.078125 to 0.078125
- cotangent: bfloat16 [4096, 4096], P('seq', 'head'), may hold values from -0.3125 to 0.3125
- log_decay: float32 [32, 4096], P('head', 'seq'), may hold values from -0.7 to 0
- document_starts: int32 [4], replicated, may hold values from 0 to 3328, as said below
Outputs:
- input_gradient: bfloat16 [4096, 6144], P('seq', 'head')
- weight_gradient: bfloat16 [6144, 3, 4096], P('seq', None, 'head')
The draws below stay inside these ranges and needn't reach their ends.
Inputs may be any that keep to these rules, and one draw needn't show every extreme that they name: `document_starts`: strictly increasing; the first is 0 and the last is (3) * 1024 + 256.
All inputs are finite; a program needn't handle non-finite values.
Results may differ from the reference program's by a relative error of at most 0.02.
Values may be sent and summed in bfloat16 or wider, within the bound.
A program may use at most 192 MiB of HBM per device.

```python
import jax
import jax.numpy as jnp
from jax import lax

D = 6144
LOCAL_HEADS = 32
HEAD_DIM = 128
BLOCK = 256
TOK_DEV = 1024
PACKED_TOKENS = 4096
NDOC = 4
N_SEQ = 4
N_HEAD = 8


def draw_log_decay(key, part):
    parallel_flows = jax.random.split(jax.random.fold_in(key, 11), 7)
    strong_share = 0.5
    strong = jax.random.uniform(parallel_flows[0], (LOCAL_HEADS, 1, 1)) < strong_share
    fast_rate = jnp.exp(jax.random.uniform(parallel_flows[1], (LOCAL_HEADS, 1, 1), jnp.float32, jnp.log(1.0 / 50.0), jnp.log(1.0 / 30.0)))
    slow_rate = jnp.exp(jax.random.uniform(parallel_flows[2], (LOCAL_HEADS, 1, 1), jnp.float32, jnp.log(0.05), jnp.log(0.4))) / PACKED_TOKENS
    rate = jnp.where(strong, fast_rate, slow_rate)
    blocks = PACKED_TOKENS // BLOCK
    block_factor = jnp.exp(jax.random.uniform(parallel_flows[3], (LOCAL_HEADS, blocks, 1), jnp.float32, jnp.log(0.5), jnp.log(2.0)))
    jitter = jax.random.uniform(parallel_flows[4], (LOCAL_HEADS, blocks, BLOCK), jnp.float32, 0.5, 2.0)
    constant_level = -(rate * block_factor * jitter).reshape(LOCAL_HEADS, PACKED_TOKENS)
    sudden_spike = jax.random.uniform(parallel_flows[5], (LOCAL_HEADS, PACKED_TOKENS)) < 3.0 / PACKED_TOKENS
    nesting_level = jnp.log(jax.random.uniform(parallel_flows[6], (LOCAL_HEADS, PACKED_TOKENS), jnp.float32, 0.5, 0.8))
    return jnp.where(sudden_spike, nesting_level, constant_level).astype(jnp.float32)


def draw_document_starts(key, part):
    parallel_flows = jax.random.split(jax.random.fold_in(key, 23), 2)
    span = PACKED_TOKENS // NDOC
    jitter = span // 4
    offsets = jax.random.randint(parallel_flows[0], (NDOC,), -jitter, jitter + 1)
    aligned_flag = jax.random.randint(parallel_flows[1], (NDOC,), 0, 2)
    order = jnp.arange(NDOC, dtype=jnp.int32)
    base = order * span + offsets
    aligned = base // BLOCK * BLOCK
    starts = jnp.where(aligned_flag == 1, aligned, base)
    starts = jnp.where(order == 0, 0, starts)
    starts = jnp.where(order == NDOC - 1, (NDOC - 1) * span + jitter, starts)
    return starts.astype(jnp.int32)


def block_scale(own_key, shape, cuts, low, largest):
    loudness, own = 1.0, jax.random.fold_in(own_key, 6)
    for dim, blocks in cuts:
        heights = jnp.exp(jax.random.uniform(jax.random.fold_in(own, dim), (blocks,), jnp.float32, low / len(cuts), largest / len(cuts)))
        loudness = loudness * jnp.repeat(heights, shape[dim] // blocks).reshape([-1 if axis == dim else 1 for axis in range(len(shape))])
    return loudness


def normal_values(rng, dims, deviation, most, shards=(), kind=jnp.bfloat16):
    entries = deviation * jax.random.normal(rng, dims, jnp.float32)
    if shards:
        entries = entries * block_scale(rng, dims, shards, -0.22, 0.18)
    return jnp.clip(entries, -most, most).astype(kind)


def setup_inputs(seed: int = 0) -> dict:
    seeds = jax.random.split(jax.random.key(seed), 6)
    return {
        "inputs": normal_values(seeds[0], (PACKED_TOKENS, D), 1.0, 6.0, ((0, 4), (1, 8))),
        "projection": normal_values(seeds[1], (D, 3, LOCAL_HEADS * HEAD_DIM), D ** -0.5, 0.078125, ((0, 4), (2, 8))),
        "cotangent": normal_values(seeds[2], (PACKED_TOKENS, LOCAL_HEADS * HEAD_DIM), 0.05, 0.3125, ((0, 4), (1, 8))),
        "log_decay": draw_log_decay(jax.random.fold_in(seeds[5], 71), 0),
        "document_starts": draw_document_starts(jax.random.fold_in(seeds[5], 71), 0),
    }


def silu_slope(point):
    sigma = jax.nn.sigmoid(point)
    return sigma * (1.0 + point * (1.0 - sigma))


def block_factors(decay_sum, doc_index, doc_begin):
    inside = jnp.arange(doc_index.shape[-1], dtype=jnp.int32)
    causal = inside[:, None] >= inside[None, :]
    same_doc = (doc_index[:, :, None] == doc_index[:, None, :]) & causal[None]
    spread = jnp.minimum(decay_sum[..., :, None] - decay_sum[..., None, :], 0.0)
    pair_weight = jnp.where(same_doc[None], jnp.exp(spread), 0.0)
    to_end = jnp.where((doc_index == doc_index[:, -1:])[None], jnp.exp(decay_sum[..., -1:] - decay_sum), 0.0)
    began_flag = doc_index == (doc_index[:, :1] - doc_begin[:, :1].astype(jnp.int32))
    from_start = jnp.where(began_flag[None], jnp.exp(decay_sum), 0.0)
    return pair_weight, to_end, from_start, from_start[..., -1]


def reference(inputs, projection, cotangent, log_decay, document_starts):
    columns = LOCAL_HEADS * HEAD_DIM
    blocks = PACKED_TOKENS // BLOCK
    query_scale = HEAD_DIM ** -0.5
    flat_weight = projection.reshape(D, 3 * columns)
    projected = jnp.dot(inputs, flat_weight, preferred_element_type=jnp.float32).reshape(PACKED_TOKENS, 3, columns)
    queries = (jax.nn.silu(projected[:, 0]) * query_scale).astype(jnp.bfloat16)
    keys = jax.nn.silu(projected[:, 1]).astype(jnp.bfloat16)
    values = projected[:, 2].astype(jnp.bfloat16)

    def split_blocks(table):
        return table.reshape(blocks, BLOCK, LOCAL_HEADS, HEAD_DIM).transpose(2, 0, 1, 3).astype(jnp.float32)

    def merge_blocks(table):
        return table.transpose(1, 2, 0, 3).reshape(PACKED_TOKENS, columns)

    queries_b = split_blocks(queries)
    keys_b = split_blocks(keys)
    values_b = split_blocks(values)
    upstream = split_blocks(cotangent)
    positions = jnp.arange(PACKED_TOKENS, dtype=jnp.int32)
    doc_index = jnp.sum((document_starts[None, :] <= positions[:, None]).astype(jnp.int32), axis=1) - 1
    doc_begin = jnp.any(document_starts[None, :] == positions[:, None], axis=1).astype(jnp.int32)
    decay_sum = jnp.cumsum(log_decay.reshape(LOCAL_HEADS, blocks, BLOCK), axis=-1)
    pair_weight, to_end, from_start, block_decay = block_factors(
        decay_sum, doc_index.reshape(blocks, BLOCK), doc_begin.reshape(blocks, BLOCK))
    keys_weighted = (keys_b * to_end[..., None]).astype(jnp.bfloat16).astype(jnp.float32)
    queries_weighted = (queries_b * from_start[..., None]).astype(jnp.bfloat16).astype(jnp.float32)
    key_state = jnp.einsum("hbse,hbsf->hbef", keys_weighted, values_b)
    query_state = jnp.einsum("hbte,hbtf->hbef", queries_weighted, upstream)

    def advance(state, item):
        decay_now, added = item
        return decay_now[:, None, None] * state + added, state

    empty = jnp.zeros((LOCAL_HEADS, HEAD_DIM, HEAD_DIM), jnp.float32)
    unused, before = lax.scan(advance, empty, (block_decay.T, key_state.swapaxes(0, 1)))
    unused, after = lax.scan(advance, empty, (block_decay.T, query_state.swapaxes(0, 1)), reverse=True)
    state_before = before.swapaxes(0, 1).astype(jnp.bfloat16).astype(jnp.float32)
    state_after = after.swapaxes(0, 1).astype(jnp.bfloat16).astype(jnp.float32)
    query_key = (jnp.einsum("hbte,hbse->hbts", queries_b, keys_b) * pair_weight).astype(jnp.bfloat16).astype(jnp.float32)
    value_score = (jnp.einsum("hbtf,hbsf->hbts", upstream, values_b) * pair_weight).astype(jnp.bfloat16).astype(jnp.float32)
    query_gradient = jnp.einsum("hbts,hbse->hbte", value_score, keys_b) + from_start[..., None] * jnp.einsum("hbtf,hbef->hbte", upstream, state_before)
    key_gradient = jnp.einsum("hbts,hbte->hbse", value_score, queries_b) + to_end[..., None] * jnp.einsum("hbsf,hbef->hbse", values_b, state_after)
    value_gradient = jnp.einsum("hbts,hbtf->hbsf", query_key, upstream) + to_end[..., None] * jnp.einsum("hbse,hbef->hbsf", keys_b, state_after)
    project_gradient = jnp.stack([
        merge_blocks(query_gradient) * silu_slope(projected[:, 0]) * query_scale,
        merge_blocks(key_gradient) * silu_slope(projected[:, 1]),
        merge_blocks(value_gradient)], axis=1).astype(jnp.bfloat16)
    group_cols = columns // N_HEAD
    grad_groups = project_gradient.reshape(PACKED_TOKENS, 3, N_HEAD, group_cols).transpose(2, 0, 1, 3)
    weight_groups = projection.reshape(D, 3, N_HEAD, group_cols).transpose(2, 0, 1, 3)

    def add_head_group(total, item):
        group_grad, group_weight = item
        head_partial = jnp.einsum("tkc,dkc->td", group_grad.astype(jnp.float32), group_weight.astype(jnp.float32))
        rounded = lax.optimization_barrier(head_partial.astype(jnp.bfloat16))
        return total + rounded.astype(jnp.float32), None

    summed, unused = lax.scan(add_head_group, jnp.zeros((PACKED_TOKENS, D), jnp.float32), (grad_groups, weight_groups))
    input_gradient = summed.astype(jnp.bfloat16)
    flat_gradient = project_gradient.reshape(PACKED_TOKENS, 3 * columns)
    grouped_inputs = inputs.reshape(N_SEQ, TOK_DEV, D)
    grouped_gradient = flat_gradient.reshape(N_SEQ, TOK_DEV, 3 * columns)

    def add_group(total, item):
        group_inputs, group_gradient = item
        partial_value = lax.dot_general(group_inputs, group_gradient, (((0,), (0,)), ((), ())),
                                  preferred_element_type=jnp.float32)
        rounded = lax.optimization_barrier(partial_value.astype(jnp.bfloat16))
        return total + rounded.astype(jnp.float32), None

    total, unused = lax.scan(add_group, jnp.zeros((D, 3 * columns), jnp.float32), (grouped_inputs, grouped_gradient))
    weight_gradient = total.astype(jnp.bfloat16).reshape(D, 3, columns)
    return input_gradient, weight_gradient
```

```python
import jax
import jax.numpy as jnp
from jax import lax
from jax.experimental import pallas as pl
from jax.experimental.layout import Layout, with_layout_constraint
from jax.experimental.pallas import tpu as pltpu
from jax.sharding import PartitionSpec as P

HEAD_DIM = 128
BLOCK = 256


def hop(array, axis, flip):
    return lax.ppermute(array, axis, [(i, i ^ flip) for i in range(lax.axis_size(axis))])


def gather_states(packed, axis):
    length, place = (lax.axis_size(axis), lax.axis_index(axis))
    if length != 4:
        whole = lax.all_gather(packed, axis)
        return [whole[k] for k in range(length)], jnp.arange(length, dtype=jnp.int32)
    parts = [packed] + [hop(packed, axis, flip) for flip in range(1, length)]
    return parts, place ^ jnp.arange(length, dtype=jnp.int32)


def device_weights(device_decay, owners, axis):
    length, place = (lax.axis_size(axis), lax.axis_index(axis))
    if length == 4:
        slab = jnp.broadcast_to(device_decay[:, None], (device_decay.shape[0], HEAD_DIM))
        hops = [slab] + [hop(slab, axis, flip) for flip in range(1, length)]
        arrived = jnp.stack([part[:, 0] for part in hops])
        mine = owners[None, :] == jnp.arange(length, dtype=jnp.int32)[:, None]
        decays = jnp.sum(jnp.where(mine[:, :, None], arrived[None], 0.0), axis=1)
    else:
        decays = lax.all_gather(device_decay, axis)
    at, other = owners[:, None], jnp.arange(length, dtype=jnp.int32)[None]
    before = (other > at) & (other < place)
    after = (other < at) & (other > place)
    weights = []
    for between, counts in ((before, owners < place), (after, owners > place)):
        product = jnp.prod(jnp.where(between[:, :, None], decays[None], 1.0), axis=1)
        weights.append(jnp.where(counts[:, None], product, 0.0))
    return jnp.stack(weights)


def gather_rows(part, axis):
    length, place, rows = (lax.axis_size(axis), lax.axis_index(axis), part.shape[1])
    if length != 4:
        whole = lax.all_gather(part, axis, axis=1, tiled=True)
        return [(0, 0, whole)]
    half = rows // 2
    low, high = part[:, :half], part[:, half:]
    x_high = hop(high, axis, 1)
    y_low = hop(low, axis, 2)
    x_low = hop(low, axis, 1)
    y_high = hop(high, axis, 2)
    d_low = hop(y_low, axis, 1)
    d_high = hop(x_high, axis, 2)
    return [
        (place, 0, low),
        (place, half, high),
        (place ^ 1, half, x_high),
        (place ^ 2, 0, y_low),
        (place ^ 1, 0, x_low),
        (place ^ 2, half, y_high),
        (place ^ 3, 0, d_low),
        (place ^ 3, half, d_high),
    ]


def scatter_rows(partial, between, source, axis, rows):
    length, place = (lax.axis_size(axis), lax.axis_index(axis))
    if length != 4:
        whole = partial(source, 0, 0, rows * length)
        return [between(source, 0, 1)], lax.psum_scatter(whole, axis, scatter_dimension=1, tiled=True)
    half = rows // 2

    def add(*terms):
        return sum(term.astype(jnp.float32) for term in terms).astype(jnp.bfloat16)

    far_low, far_high = partial(source, place ^ 3, 0, half), partial(source, place ^ 3, half, half)
    source, far_low, far_high = lax.optimization_barrier((source, far_low, far_high))
    far_low, far_high = hop(far_low, axis, 1), hop(far_high, axis, 2)
    beside = between(source, 0, 1)
    source, beside = lax.optimization_barrier((source, beside))
    x_low, y_high = partial(source, place ^ 1, 0, half), partial(source, place ^ 2, half, half)
    source, x_low, y_high = lax.optimization_barrier((source, x_low, y_high))
    x_low, y_high = hop(x_low, axis, 1), hop(y_high, axis, 2)
    x_high = hop(add(partial(source, place ^ 1, half, half), far_high), axis, 1)
    y_low = hop(add(partial(source, place ^ 2, 0, half), far_low), axis, 2)
    own_low, own_high = partial(source, place, 0, half), partial(source, place, half, half)
    whole = jnp.concatenate([add(own_low, x_low, y_low), add(own_high, x_high, y_high)], axis=1)
    return [beside], whole


def running_sum(values):
    inside = jnp.arange(values.shape[-1], dtype=jnp.int32)
    triangle = (inside[:, None] <= inside[None, :]).astype(jnp.float32)
    return jnp.einsum("hbu,ut->hbt", values, triangle, precision=lax.Precision.HIGHEST)


def block_factors(decay_sum, doc_index, doc_begin):
    inside = jnp.arange(doc_index.shape[-1], dtype=jnp.int32)
    causal = inside[:, None] >= inside[None, :]
    same_doc = (doc_index[:, :, None] == doc_index[:, None, :]) & causal[None]
    spread = jnp.minimum(decay_sum[..., :, None] - decay_sum[..., None, :], 0.0)
    pair_weight = jnp.where(same_doc[None], jnp.exp(spread), 0.0)
    to_end = jnp.where(
        (doc_index == doc_index[:, -1:])[None], jnp.exp(decay_sum[..., -1:] - decay_sum), 0.0
    )
    began_flag = doc_index == doc_index[:, :1] - doc_begin[:, :1]
    from_start = jnp.where(began_flag[None], jnp.exp(decay_sum), 0.0)
    return (pair_weight, to_end, from_start, from_start[..., -1])


def dot(left, right, contract):
    return lax.dot_general(
        left, right, ((contract[:1], contract[1:]), ((), ())), preferred_element_type=jnp.float32
    )


def projections(proj_ref, span):
    point_q, point_k = proj_ref[0, span], proj_ref[1, span]
    gate_q, gate_k = jax.nn.sigmoid(point_q), jax.nn.sigmoid(point_k)
    queries = (point_q * gate_q * HEAD_DIM ** (-0.5)).astype(jnp.bfloat16)
    keys = (point_k * gate_k).astype(jnp.bfloat16)
    values = proj_ref[2, span].astype(jnp.bfloat16)
    return (point_q, gate_q, queries), (point_k, gate_k, keys), values


def state_kernel(proj_ref, up_ref, start_ref, end_ref, key_ref, query_ref, total_ref):
    blocks = key_ref.shape[1]
    forward = jnp.zeros((HEAD_DIM, HEAD_DIM), jnp.float32)
    query_states, decays = [], []
    for b in range(blocks):
        span = pl.ds(b * BLOCK, BLOCK)
        (_, _, queries), (_, _, keys), values = projections(proj_ref, span)
        keys_weighted = (keys.astype(jnp.float32) * end_ref[0, span]).astype(jnp.bfloat16)
        queries_weighted = (queries.astype(jnp.float32) * start_ref[0, span]).astype(jnp.bfloat16)
        key_state = dot(keys_weighted, values, (0, 0))
        query_state = dot(queries_weighted, up_ref[span], (0, 0))
        key_ref[0, b] = key_state
        query_ref[0, b] = query_state
        decay = start_ref[0, pl.ds(b * BLOCK + BLOCK - 1, 1)]
        forward = decay * forward + key_state
        query_states.append(query_state)
        decays.append(decay)
    backward = jnp.zeros((HEAD_DIM, HEAD_DIM), jnp.float32)
    for b in reversed(range(blocks)):
        backward = decays[b] * backward + query_states[b]
    total_ref[0, 0] = forward.astype(jnp.bfloat16)
    total_ref[1, 0] = backward.astype(jnp.bfloat16)


def gradient_kernel(
    weight_ref, proj_ref, up_ref, start_ref, end_ref, pair_ref, key_ref, query_ref, *rest
):
    totals, out_ref = rest[:-1], rest[-1]
    blocks = key_ref.shape[1]
    head = pl.program_id(0)
    state = jnp.zeros((HEAD_DIM, HEAD_DIM), jnp.float32)
    reverse = jnp.zeros((HEAD_DIM, HEAD_DIM), jnp.float32)
    for k, total in enumerate(totals):
        state = state + weight_ref[0, k, head] * total[0, 0].astype(jnp.float32)
        reverse = reverse + weight_ref[1, k, head] * total[1, 0].astype(jnp.float32)
    decays = [start_ref[0, pl.ds(b * BLOCK + BLOCK - 1, 1)] for b in range(blocks)]
    after = [None] * blocks
    for b in reversed(range(blocks)):
        after[b] = reverse.astype(jnp.bfloat16)
        reverse = decays[b] * reverse + query_ref[0, b]
    for b in range(blocks):
        before = state.astype(jnp.bfloat16)
        state = decays[b] * state + key_ref[0, b]
        span = pl.ds(b * BLOCK, BLOCK)
        (point_q, gate_q, queries), (point_k, gate_k, keys), values = projections(proj_ref, span)
        upstream = up_ref[span]
        from_start, to_end, pair = start_ref[0, span], end_ref[0, span], pair_ref[0, b]
        query_key = (dot(queries, keys, (1, 1)) * pair).astype(jnp.bfloat16)
        value_score = (dot(upstream, values, (1, 1)) * pair).astype(jnp.bfloat16)
        query_gradient = dot(value_score, keys, (1, 0)) + from_start * dot(
            upstream, before, (1, 1)
        )
        key_gradient = dot(value_score, queries, (0, 0)) + to_end * dot(values, after[b], (1, 1))
        value_gradient = dot(query_key, upstream, (0, 0)) + to_end * dot(keys, after[b], (1, 0))
        slope_q = gate_q * (1.0 + point_q * (1.0 - gate_q)) * HEAD_DIM ** (-0.5)
        slope_k = gate_k * (1.0 + point_k * (1.0 - gate_k))
        out_ref[0, span] = (query_gradient * slope_q).astype(jnp.bfloat16)
        out_ref[1, span] = (key_gradient * slope_k).astype(jnp.bfloat16)
        out_ref[2, span] = value_gradient.astype(jnp.bfloat16)


def input_kernel(gradient_ref, weight_ref, out_ref):
    for first in range(0, out_ref.shape[0], BLOCK):
        span = pl.ds(first, BLOCK)
        total = dot(gradient_ref[0, span], weight_ref[0], (1, 1))
        for k in (1, 2):
            total = total + dot(gradient_ref[k, span], weight_ref[k], (1, 1))
        out_ref[span] = total.astype(jnp.bfloat16)


def general_body(inputs, projection, cotangent, log_decay, document_starts):
    tokens = inputs.shape[0]
    heads_here = log_decay.shape[0]
    local_cols = cotangent.shape[1]
    blocks = tokens // BLOCK
    features = lax.all_gather(inputs, "head", axis=1, tiled=True)
    rows = projection.shape[0]
    blocks_w = gather_rows(projection.transpose(1, 0, 2), "seq")

    def feature_rows(owner, first, count):
        return lax.dynamic_slice_in_dim(features, owner * rows + first, count, axis=1)

    offset = lax.axis_index("seq") * tokens
    positions = offset + jnp.arange(tokens, dtype=jnp.int32)
    doc_index = (
        jnp.sum((document_starts[None, :] <= positions[:, None]).astype(jnp.int32), axis=1) - 1
    )
    doc_begin = jnp.any(document_starts[None, :] == positions[:, None], axis=1).astype(jnp.int32)
    decay_sum = running_sum(log_decay.reshape(heads_here, blocks, BLOCK))
    pair_weight, to_end, from_start, block_decay = block_factors(
        decay_sum, doc_index.reshape(blocks, BLOCK), doc_begin.reshape(blocks, BLOCK)
    )
    lanes = (heads_here, tokens, HEAD_DIM)
    to_end = jnp.broadcast_to(to_end.reshape(heads_here, tokens)[..., None], lanes)
    from_start = jnp.broadcast_to(from_start.reshape(heads_here, tokens)[..., None], lanes)
    device_decay = jnp.prod(block_decay, axis=1)

    zero = jnp.zeros((), jnp.bfloat16)
    if len(blocks_w) > 2:
        owner, first, block = blocks_w[2]
        zero, block = lax.optimization_barrier((zero, block))
        blocks_w[2] = (owner, first, block)
    weights_all = jnp.broadcast_to(zero, (3, features.shape[1], local_cols))

    def place_rows(whole, some):
        for owner, first, block in some:
            whole = lax.dynamic_update_slice_in_dim(whole, block, owner * rows + first, axis=1)
        return whole

    early, late = blocks_w[:6], blocks_w[6:]
    weights_all = place_rows(weights_all, early)
    features, weights_all, from_start, to_end, pair_weight = lax.optimization_barrier(
        (features, weights_all, from_start, to_end, pair_weight)
    )
    projected = None
    for k, (owner, first, block) in enumerate(blocks_w):
        piece = jnp.einsum(
            "td,kdc->ktc",
            feature_rows(owner, first, block.shape[1]),
            block,
            preferred_element_type=jnp.float32,
        )
        projected = piece if projected is None else lax.optimization_barrier(projected) + piece
        if k == min(5, len(blocks_w) - 1):
            projected, device_decay = lax.optimization_barrier((projected, device_decay))
    weights_all = place_rows(weights_all, late)

    proj_spec = pl.BlockSpec((3, tokens, HEAD_DIM), lambda h: (0, 0, h))
    up_spec = pl.BlockSpec((tokens, HEAD_DIM), lambda h: (0, h))
    lane_spec = pl.BlockSpec((1, tokens, HEAD_DIM), lambda h: (h, 0, 0))
    state_spec = pl.BlockSpec((1, blocks, HEAD_DIM, HEAD_DIM), lambda h: (h, 0, 0, 0))
    total_spec = pl.BlockSpec((2, 1, HEAD_DIM, HEAD_DIM), lambda h: (0, h, 0, 0))
    pair_spec = pl.BlockSpec((1, blocks, BLOCK, BLOCK), lambda h: (h, 0, 0, 0))
    states = jax.ShapeDtypeStruct((heads_here, blocks, HEAD_DIM, HEAD_DIM), jnp.float32)
    key_state, query_state, totals = pl.pallas_call(
        state_kernel,
        grid=(heads_here,),
        in_specs=[proj_spec, up_spec, lane_spec, lane_spec],
        out_specs=[state_spec, state_spec, total_spec],
        out_shape=[
            states,
            states,
            jax.ShapeDtypeStruct((2, heads_here, HEAD_DIM, HEAD_DIM), jnp.bfloat16),
        ],
    )(projected, cotangent, from_start, to_end)
    parts, owners = gather_states(totals, "seq")
    weights = device_weights(device_decay, owners, "seq")
    project_gradient = pl.pallas_call(
        gradient_kernel,
        grid=(heads_here,),
        in_specs=[pl.BlockSpec(memory_space=pltpu.SMEM)]
        + [proj_spec, up_spec, lane_spec, lane_spec, pair_spec, state_spec, state_spec]
        + [total_spec] * len(parts),
        out_specs=proj_spec,
        out_shape=jax.ShapeDtypeStruct(projected.shape, jnp.bfloat16),
    )(weights, projected, cotangent, from_start, to_end, pair_weight, key_state, query_state, *parts)

    def weight_partial(gradient, owner, first, count):
        term = jnp.einsum(
            "td,ktc->kdc",
            feature_rows(owner, first, count),
            gradient,
            preferred_element_type=jnp.float32,
        ).astype(jnp.bfloat16)
        return with_layout_constraint(term, Layout(major_to_minor=(0, 1, 2)))

    def input_partial(gradient, part, of):
        columns = features.shape[1]
        tile, count = columns // 8, tokens // of
        return pl.pallas_call(
            input_kernel,
            grid=(columns // tile,),
            in_specs=[
                pl.BlockSpec((3, count, local_cols), lambda i: (0, part, 0)),
                pl.BlockSpec((3, tile, local_cols), lambda i: (0, i, 0)),
            ],
            out_specs=pl.BlockSpec((count, tile), lambda i: (0, i)),
            out_shape=jax.ShapeDtypeStruct((count, columns), jnp.bfloat16),
            cost_estimate=pl.CostEstimate(flops=1, bytes_accessed=1, transcendentals=0),
            compiler_params=pltpu.CompilerParams(vmem_limit_bytes=40 << 20),
        )(gradient, weights_all)

    input_partials, weight_gradient = scatter_rows(
        weight_partial, input_partial, project_gradient, "seq", rows
    )
    input_gradient = lax.psum_scatter(
        input_partials[0], "head", scatter_dimension=1, tiled=True
    )
    weight_gradient = weight_gradient.transpose(1, 0, 2)
    return (input_gradient, weight_gradient)


MESH = pl.DeviceIdType.MESH


def remote_maker(send, recv):
    def remote(index, source, target, device):
        return pltpu.make_async_remote_copy(
            src_ref=source,
            dst_ref=target,
            send_sem=send.at[index],
            recv_sem=recv.at[index],
            device_id=device,
            device_id_type=MESH,
        )

    return remote


def greet(others):
    barrier = pltpu.get_barrier_semaphore()
    for other in others:
        pl.semaphore_signal(barrier, inc=1, device_id=other, device_id_type=MESH)
    pl.semaphore_wait(barrier, len(others))


def gather_kernel(
    x_ref, w_ref, feats_out, wall_out, total_out, swap, feats, wall, total, send, recv, local
):
    place, head = lax.axis_index("seq"), lax.axis_index("head")
    z, core = head // 2, head % 2
    tokens, cols = x_ref.shape
    rows = w_ref.shape[1]
    half, near, chunk = tokens // 2, rows // 2, tokens // 8
    x_id, y_id, far_id = (place ^ 1, head), (place ^ 2, head), (place ^ 3, head)
    next_id, last_id = (place, (head + 2) % 8), (place, (head + 6) % 8)
    twin_id = (place, head ^ 1)
    mine = pl.ds(pl.multiple_of(core * cols, cols), cols)
    remote = remote_maker(send, recv)

    own_w = pltpu.make_async_copy(w_ref, wall.at[place], local.at[0])
    own_x = pltpu.make_async_copy(x_ref, feats.at[z, :, mine], local.at[1])
    own_w.start()
    own_x.start()

    def block(step, part):
        return feats.at[(z + 4 - step) % 4, pl.ds(part * half, half), mine]

    def x_part(step, part):
        return x_ref.at[pl.ds(part * half, half)] if step == 0 else block(step, part)

    ring = [
        [remote(2 * k + p, x_part(k, p), block(k, p), next_id) for p in range(2)] for k in range(3)
    ]
    twin = [
        [remote(6 + 2 * k + p, x_part(k, p), block(k, p), twin_id) for p in range(2)]
        for k in range(4)
    ]
    low, high = pl.ds(0, near), pl.ds(near, near)
    side = [
        remote(14 + i, w_ref.at[:, part], wall.at[place, :, part], device)
        for i, (part, device) in enumerate(((high, x_id), (low, y_id), (low, x_id), (high, y_id)))
    ]

    def quarter(owner, part):
        return wall.at[owner, :, pl.ds(part * (near // 2), near // 2)]

    far = [
        [
            remote(18 + 2 * i, quarter(place ^ 2, i), quarter(place ^ 2, i), x_id),
            remote(19 + 2 * i, quarter(place ^ 1, 2 + i), quarter(place ^ 1, 2 + i), y_id),
        ]
        for i in range(2)
    ]

    def share(who):
        return pl.ds(pl.multiple_of(who * chunk, chunk), chunk)

    mix = [
        remote(21 + flip, feats.at[place ^ flip, share(head)], swap.at[flip - 1, share(head)], device)
        for flip, device in ((1, x_id), (2, y_id), (3, far_id))
    ]

    def shared(step):
        return swap.at[:, share((head + 8 - 2 * step) % 8)]

    spread = [remote(25 + k, shared(k), shared(k), next_id) for k in range(2)]
    spread_twin = [remote(27 + k, shared(k), shared(k), twin_id) for k in range(3)]

    greet((x_id, y_id, far_id, next_id, last_id, twin_id))
    ring[0][0].start()
    side[0].start()
    side[1].start()
    ring[0][1].start()
    twin[0][0].start()
    twin[0][1].start()

    def arrived(step, part):
        ring[step][part].wait_recv()
        if step < 2:
            ring[step + 1][part].start()
        twin[step + 1][part].start()

    def multiply(owner, begin, top, count):
        @pl.loop(0, 6)
        def _(i):
            k, span = i // 2, pl.ds(pl.multiple_of(i % 2 * half, half), half)
            term = jnp.dot(
                feats[owner, span, pl.ds(top, count)],
                wall[owner, k, pl.ds(top, count), :],
                preferred_element_type=jnp.float32,
            )
            total[k, span, :] = term if begin else total[k, span, :] + term

    arrived(0, 0)
    arrived(0, 1)
    arrived(1, 0)
    side[0].wait_recv()
    side[1].wait_recv()
    side[2].start()
    side[3].start()
    arrived(1, 1)
    own_w.wait()
    own_x.wait()
    arrived(2, 0)
    arrived(2, 1)
    for pair in twin:
        for move in pair:
            move.wait_recv()
    for move in mix:
        move.start()
    side[2].wait_recv()
    far[0][0].start()
    far[1][0].start()
    side[3].wait_recv()
    far[0][1].start()
    far[1][1].start()
    feats_copy = pltpu.make_async_copy(feats, feats_out, local.at[2])
    feats_copy.start()
    multiply(place, True, 0, rows)
    for move in mix:
        move.wait_recv()
    spread[0].start()
    spread_twin[0].start()
    multiply(place ^ 1, False, 0, rows)
    multiply(place ^ 2, False, 0, rows)
    near_copies = [
        pltpu.make_async_copy(wall.at[place ^ f], wall_out.at[place ^ f], local.at[3 + f])
        for f in range(3)
    ]
    for move in near_copies:
        move.start()
    spread[0].wait_recv()
    spread[1].start()
    spread_twin[1].start()
    for i in range(2):
        for move in far[i]:
            move.wait_recv()
        multiply(place ^ 3, False, i * (near // 2), near // 2)
        multiply(place ^ 3, False, near + i * (near // 2), near // 2)
    far_copy = pltpu.make_async_copy(wall.at[place ^ 3], wall_out.at[place ^ 3], local.at[6])
    far_copy.start()
    total_copy = pltpu.make_async_copy(total, total_out, local.at[7])
    total_copy.start()
    spread[1].wait_recv()
    spread_twin[2].start()
    for move in spread_twin:
        move.wait_recv()
    for move in (feats_copy, *near_copies, far_copy, total_copy):
        move.wait()
    for move in (*ring[0], *ring[1], *ring[2], *side, *far[0], *far[1], *mix, *spread, *spread_twin):
        move.wait_send()
    for pair in twin:
        for move in pair:
            move.wait_send()


def gather_call(inputs, weights):
    (tokens, cols), (_, rows, local_cols) = inputs.shape, weights.shape
    bf16, f32 = jnp.bfloat16, jnp.float32
    shapes = [
        ((4, tokens, 2 * cols), bf16),
        ((4, 3, rows, local_cols), bf16),
        ((3, tokens, local_cols), f32),
        ((3, tokens, 2 * cols), bf16),
    ]
    anywhere = pl.BlockSpec(memory_space=pl.ANY)
    return pl.pallas_call(
        gather_kernel,
        in_specs=[anywhere] * 2,
        out_specs=[anywhere] * 4,
        out_shape=[jax.ShapeDtypeStruct(*shape) for shape in shapes],
        scratch_shapes=[pltpu.VMEM(*shape) for shape in shapes[:3]]
        + [
            pltpu.SemaphoreType.DMA((30,)),
            pltpu.SemaphoreType.DMA((30,)),
            pltpu.SemaphoreType.DMA((8,)),
        ],
        compiler_params=pltpu.CompilerParams(
            collective_id=0, has_side_effects=True, vmem_limit_bytes=48 << 20
        ),
        name="gather",
    )(inputs, weights)


def finish_kernel(
    grad_ref, feats_ref, wall_ref, swap_ref, late_ref, twin_late_ref, input_out, weight_out,
    grads, tokens_buf, rows_buf, total, keep, twin_out, twin_in, ring_out, ring_in,
    send, recv, local,
):
    place, head = lax.axis_index("seq"), lax.axis_index("head")
    z, core = head // 2, head % 2
    _, tokens, local_cols = grad_ref.shape
    rows, cols = total.shape[1], keep.shape[1]
    half, chunk = tokens // 2, tokens // 8
    x_id, y_id = (place ^ 1, head), (place ^ 2, head)
    next_id, last_id = (place, (head + 2) % 8), (place, (head + 6) % 8)
    twin_id = (place, head ^ 1)
    remote = remote_maker(send, recv)
    low, high = pl.ds(0, half), pl.ds(half, half)

    def fetch_rows(turn, part):
        owner = (z + 7 - turn) % 4
        side = pl.multiple_of((core if part else 1 - core) * cols, cols)
        return pltpu.make_async_copy(
            wall_ref.at[owner, :, pl.ds(side, cols)], rows_buf.at[part], local.at[part]
        )

    def fetch_tokens(flip):
        slot = flip % 2
        if flip == 0:
            return [
                pltpu.make_async_copy(feats_ref.at[place], tokens_buf.at[slot], local.at[2])
            ]
        copies = []
        for i in range(3):
            top = pl.multiple_of((z + 2 + i) % 4 * (2 * chunk), 2 * chunk)
            copies.append(
                pltpu.make_async_copy(
                    swap_ref.at[flip - 1, pl.ds(top, 2 * chunk)],
                    tokens_buf.at[slot, pl.ds(top, 2 * chunk)],
                    local.at[3 + 5 * flip + i],
                )
            )
        for i, (ref, who) in enumerate(
            ((late_ref, (head + 2) % 8), (twin_late_ref, (head + 2) % 8 + 1 - 2 * core))
        ):
            top = pl.multiple_of(who * chunk, chunk)
            copies.append(
                pltpu.make_async_copy(
                    ref.at[flip - 1],
                    tokens_buf.at[slot, pl.ds(top, chunk)],
                    local.at[6 + 5 * flip + i],
                )
            )
        return copies

    own = pltpu.make_async_copy(grad_ref, grads.at[0], local.at[23])
    own.start()
    fetched_rows = [fetch_rows(0, 0), fetch_rows(0, 1)]
    for move in fetched_rows:
        move.start()
    fetched = [fetch_tokens(0), fetch_tokens(1)]
    for moves in fetched:
        for move in moves:
            move.start()
    side = [
        remote(i, grad_ref.at[:, part], grads.at[flip, :, part], device)
        for i, (part, flip, device) in enumerate(
            ((high, 1, x_id), (low, 2, y_id), (low, 1, x_id), (high, 2, y_id))
        )
    ]
    far = [
        remote(4, grads.at[2, :, low], grads.at[3, :, low], x_id),
        remote(5, grads.at[1, :, high], grads.at[3, :, high], y_id),
    ]
    twin = [remote(6 + k, twin_out.at[k % 2], twin_in.at[k], twin_id) for k in range(4)]
    ring = [
        [
            remote(10 + 2 * k + p, ring_out.at[k, part], ring_in.at[k, part], next_id)
            for p, part in enumerate((low, high))
        ]
        for k in range(3)
    ]
    greet((x_id, y_id, next_id, last_id, twin_id))
    for move in side:
        move.start()
    own.wait()

    def back(part, target):
        fetched_rows[part].wait()

        @pl.loop(0, 4)
        def _(i):
            span = pl.ds(pl.multiple_of(i * (tokens // 4), tokens // 4), tokens // 4)
            term = None
            for k in range(3):
                piece = dot(grads[0, k, span, :], rows_buf[part, k], (1, 1))
                term = piece if term is None else term + piece
            target[span, :] = term.astype(target.dtype)

    def input_block(turn):
        if turn >= 2:
            twin[turn - 2].wait_send()
        back(0, twin_out.at[turn % 2])
        twin[turn].start()
        if turn < 3:
            fetched_rows[0] = fetch_rows(turn + 1, 0)
            fetched_rows[0].start()
        back(1, keep)
        if turn < 3:
            fetched_rows[1] = fetch_rows(turn + 1, 1)
            fetched_rows[1].start()
        twin[turn].wait_recv()

    def pass_on(turn):
        for p, part in enumerate((low, high)):
            if turn > 0:
                ring[turn - 1][p].wait_recv()

            @pl.loop(0, 2)
            def _(i):
                quarter = tokens // 4
                span = pl.ds(pl.multiple_of(p * half + i * quarter, quarter), quarter)
                sum_ = keep[span, :] + twin_in[turn, span, :].astype(jnp.float32)
                if turn > 0:
                    sum_ = sum_ + ring_in[turn - 1, span, :].astype(jnp.float32)
                target = ring_out.at[turn] if turn < 3 else twin_out.at[0]
                target[span, :] = sum_.astype(jnp.bfloat16)

            if turn < 3:
                ring[turn][p].start()

    def weight_block(flip):
        slot = flip % 2
        for move in fetched[slot]:
            move.wait()

        @pl.loop(0, rows // BLOCK)
        def _(i):
            span = pl.ds(pl.multiple_of(i * BLOCK, BLOCK), BLOCK)
            turned = tokens_buf[slot, :, span].T
            for k in range(3):
                term = jnp.dot(turned, grads[flip, k], preferred_element_type=jnp.float32)
                total[k, span, :] = term if flip == 0 else total[k, span, :] + term

        if flip < 2:
            fetched[slot] = fetch_tokens(flip + 2)
            for move in fetched[slot]:
                move.start()

    input_block(0)
    pass_on(0)
    input_block(1)
    weight_block(0)
    side[0].wait_recv()
    far[1].start()
    side[1].wait_recv()
    far[0].start()
    pass_on(1)
    input_block(2)
    side[2].wait_recv()
    weight_block(1)
    pass_on(2)
    input_block(3)
    side[3].wait_recv()
    weight_block(2)
    for move in far:
        move.wait_recv()
    weight_block(3)
    stores = []
    for part in range(2):
        span = pl.ds(part * (rows // 2), rows // 2)
        for k in range(3):
            rows_buf[part, k] = total[k, span, :].astype(jnp.bfloat16)
        stores.append(
            pltpu.make_async_copy(rows_buf.at[part], weight_out.at[:, span], local.at[part])
        )
        stores[-1].start()
    twin[2].wait_send()
    twin[3].wait_send()
    pass_on(3)
    stores.append(pltpu.make_async_copy(twin_out.at[0], input_out, local.at[23]))
    stores[-1].start()
    for move in stores:
        move.wait()
    for move in (*side, *far, *ring[0], *ring[1], *ring[2]):
        move.wait_send()


def finish_call(gradient, feats, wall, swap, late, twin_late):
    _, tokens, local_cols = gradient.shape
    rows = wall.shape[2]
    cols = rows // 2
    bf16, f32 = jnp.bfloat16, jnp.float32
    anywhere = pl.BlockSpec(memory_space=pl.ANY)
    return pl.pallas_call(
        finish_kernel,
        in_specs=[anywhere] * 6,
        out_specs=[anywhere] * 2,
        out_shape=[
            jax.ShapeDtypeStruct((tokens, cols), bf16),
            jax.ShapeDtypeStruct((3, rows, local_cols), bf16),
        ],
        scratch_shapes=[
            pltpu.VMEM((4, 3, tokens, local_cols), bf16),
            pltpu.VMEM((2, tokens, rows), bf16),
            pltpu.VMEM((2, 3, cols, local_cols), bf16),
            pltpu.VMEM((3, rows, local_cols), f32),
            pltpu.VMEM((tokens, cols), f32),
            pltpu.VMEM((2, tokens, cols), bf16),
            pltpu.VMEM((4, tokens, cols), bf16),
            pltpu.VMEM((3, tokens, cols), bf16),
            pltpu.VMEM((3, tokens, cols), bf16),
            pltpu.SemaphoreType.DMA((16,)),
            pltpu.SemaphoreType.DMA((16,)),
            pltpu.SemaphoreType.DMA((24,)),
        ],
        compiler_params=pltpu.CompilerParams(
            collective_id=1, has_side_effects=True, vmem_limit_bytes=60 << 20
        ),
        name="finish",
    )(gradient, feats, wall, swap, late, twin_late)


def fast_body(inputs, projection, cotangent, log_decay, document_starts):
    tokens = inputs.shape[0]
    heads_here = log_decay.shape[0]
    blocks = tokens // BLOCK
    place, head = lax.axis_index("seq"), lax.axis_index("head")
    feats, wall, projected, swap = gather_call(inputs, projection.transpose(1, 0, 2))
    chunk = tokens // 8
    late = lax.dynamic_slice_in_dim(swap, (head + 4) % 8 * chunk, chunk, axis=1)
    late = lax.ppermute(late, "head", [(i, (i + 2) % 8) for i in range(8)])
    twin_late = lax.ppermute(late, "head", [(i, i ^ 1) for i in range(8)])

    positions = place * tokens + jnp.arange(tokens, dtype=jnp.int32)
    doc_index = (
        jnp.sum((document_starts[None, :] <= positions[:, None]).astype(jnp.int32), axis=1) - 1
    )
    doc_begin = jnp.any(document_starts[None, :] == positions[:, None], axis=1).astype(jnp.int32)
    decay_sum = running_sum(log_decay.reshape(heads_here, blocks, BLOCK))
    pair_weight, to_end, from_start, block_decay = block_factors(
        decay_sum, doc_index.reshape(blocks, BLOCK), doc_begin.reshape(blocks, BLOCK)
    )
    lanes = (heads_here, tokens, HEAD_DIM)
    to_end = jnp.broadcast_to(to_end.reshape(heads_here, tokens)[..., None], lanes)
    from_start = jnp.broadcast_to(from_start.reshape(heads_here, tokens)[..., None], lanes)
    device_decay = jnp.prod(block_decay, axis=1)
    owners = place ^ jnp.arange(4, dtype=jnp.int32)
    weights = device_weights(device_decay, owners, "seq")

    proj_spec = pl.BlockSpec((3, tokens, HEAD_DIM), lambda h: (0, 0, h))
    up_spec = pl.BlockSpec((tokens, HEAD_DIM), lambda h: (0, h))
    lane_spec = pl.BlockSpec((1, tokens, HEAD_DIM), lambda h: (h, 0, 0))
    state_spec = pl.BlockSpec((1, blocks, HEAD_DIM, HEAD_DIM), lambda h: (h, 0, 0, 0))
    total_spec = pl.BlockSpec((2, 1, HEAD_DIM, HEAD_DIM), lambda h: (0, h, 0, 0))
    pair_spec = pl.BlockSpec((1, blocks, BLOCK, BLOCK), lambda h: (h, 0, 0, 0))
    states = jax.ShapeDtypeStruct((heads_here, blocks, HEAD_DIM, HEAD_DIM), jnp.float32)
    key_state, query_state, totals = pl.pallas_call(
        state_kernel,
        grid=(heads_here,),
        in_specs=[proj_spec, up_spec, lane_spec, lane_spec],
        out_specs=[state_spec, state_spec, total_spec],
        out_shape=[
            states,
            states,
            jax.ShapeDtypeStruct((2, heads_here, HEAD_DIM, HEAD_DIM), jnp.bfloat16),
        ],
    )(projected, cotangent, from_start, to_end)
    parts = [totals] + [hop(totals, "seq", flip) for flip in (1, 2, 3)]
    gradient = pl.pallas_call(
        gradient_kernel,
        grid=(heads_here,),
        in_specs=[pl.BlockSpec(memory_space=pltpu.SMEM)]
        + [proj_spec, up_spec, lane_spec, lane_spec, pair_spec, state_spec, state_spec]
        + [total_spec] * len(parts),
        out_specs=proj_spec,
        out_shape=jax.ShapeDtypeStruct(projected.shape, jnp.bfloat16),
    )(weights, projected, cotangent, from_start, to_end, pair_weight, key_state, query_state, *parts)
    input_gradient, weight_gradient = finish_call(gradient, feats, wall, swap, late, twin_late)
    return (input_gradient, weight_gradient.transpose(1, 0, 2))


def solution(mesh):
    fast = (mesh.shape["seq"], mesh.shape["head"]) == (4, 8)
    placed = (P("seq", "head"), P("seq", None, "head"), P("seq", "head"), P("head", "seq"), P())
    return jax.shard_map(
        fast_body if fast else general_body,
        mesh=mesh,
        in_specs=placed,
        out_specs=(P("seq", "head"), P("seq", None, "head")),
        check_vma=False,
    )
```

```python
import jax
import jax.numpy as jnp
from jax import lax
from jax.experimental import pallas as pl
from jax.experimental.layout import Layout, with_layout_constraint
from jax.experimental.pallas import tpu as pltpu
from jax.sharding import PartitionSpec as P

HEAD_DIM = 128
BLOCK = 256


def hop(array, axis, flip):
    return lax.ppermute(array, axis, [(i, i ^ flip) for i in range(lax.axis_size(axis))])


def gather_states(packed, axis):
    length, place = (lax.axis_size(axis), lax.axis_index(axis))
    if length != 4:
        whole = lax.all_gather(packed, axis)
        return [whole[k] for k in range(length)], jnp.arange(length, dtype=jnp.int32)
    parts = [packed] + [hop(packed, axis, flip) for flip in range(1, length)]
    return parts, place ^ jnp.arange(length, dtype=jnp.int32)


def device_weights(device_decay, owners, axis):
    length, place = (lax.axis_size(axis), lax.axis_index(axis))
    if length == 4:
        slab = jnp.broadcast_to(device_decay[:, None], (device_decay.shape[0], HEAD_DIM))
        hops = [slab] + [hop(slab, axis, flip) for flip in range(1, length)]
        arrived = jnp.stack([part[:, 0] for part in hops])
        mine = owners[None, :] == jnp.arange(length, dtype=jnp.int32)[:, None]
        decays = jnp.sum(jnp.where(mine[:, :, None], arrived[None], 0.0), axis=1)
    else:
        decays = lax.all_gather(device_decay, axis)
    at, other = owners[:, None], jnp.arange(length, dtype=jnp.int32)[None]
    before = (other > at) & (other < place)
    after = (other < at) & (other > place)
    weights = []
    for between, counts in ((before, owners < place), (after, owners > place)):
        product = jnp.prod(jnp.where(between[:, :, None], decays[None], 1.0), axis=1)
        weights.append(jnp.where(counts[:, None], product, 0.0))
    return jnp.stack(weights)


def gather_rows(part, axis):
    length, place, rows = (lax.axis_size(axis), lax.axis_index(axis), part.shape[1])
    if length != 4:
        whole = lax.all_gather(part, axis, axis=1, tiled=True)
        return [(0, 0, whole)]
    half = rows // 2
    low, high = part[:, :half], part[:, half:]
    x_high = hop(high, axis, 1)
    y_low = hop(low, axis, 2)
    x_low = hop(low, axis, 1)
    y_high = hop(high, axis, 2)
    d_low = hop(y_low, axis, 1)
    d_high = hop(x_high, axis, 2)
    return [
        (place, 0, low),
        (place, half, high),
        (place ^ 1, half, x_high),
        (place ^ 2, 0, y_low),
        (place ^ 1, 0, x_low),
        (place ^ 2, half, y_high),
        (place ^ 3, 0, d_low),
        (place ^ 3, half, d_high),
    ]


def scatter_rows(partial, between, source, axis, rows):
    length, place = (lax.axis_size(axis), lax.axis_index(axis))
    if length != 4:
        whole = partial(source, 0, 0, rows * length)
        return [between(source, 0, 1)], lax.psum_scatter(whole, axis, scatter_dimension=1, tiled=True)
    half = rows // 2

    def add(*terms):
        return sum(term.astype(jnp.float32) for term in terms).astype(jnp.bfloat16)

    far_low, far_high = partial(source, place ^ 3, 0, half), partial(source, place ^ 3, half, half)
    source, far_low, far_high = lax.optimization_barrier((source, far_low, far_high))
    far_low, far_high = hop(far_low, axis, 1), hop(far_high, axis, 2)
    beside = between(source, 0, 1)
    source, beside = lax.optimization_barrier((source, beside))
    x_low, y_high = partial(source, place ^ 1, 0, half), partial(source, place ^ 2, half, half)
    source, x_low, y_high = lax.optimization_barrier((source, x_low, y_high))
    x_low, y_high = hop(x_low, axis, 1), hop(y_high, axis, 2)
    x_high = hop(add(partial(source, place ^ 1, half, half), far_high), axis, 1)
    y_low = hop(add(partial(source, place ^ 2, 0, half), far_low), axis, 2)
    own_low, own_high = partial(source, place, 0, half), partial(source, place, half, half)
    whole = jnp.concatenate([add(own_low, x_low, y_low), add(own_high, x_high, y_high)], axis=1)
    return [beside], whole


def running_sum(values):
    inside = jnp.arange(values.shape[-1], dtype=jnp.int32)
    triangle = (inside[:, None] <= inside[None, :]).astype(jnp.float32)
    return jnp.einsum("hbu,ut->hbt", values, triangle, precision=lax.Precision.HIGHEST)


def block_factors(decay_sum, doc_index, doc_begin):
    inside = jnp.arange(doc_index.shape[-1], dtype=jnp.int32)
    causal = inside[:, None] >= inside[None, :]
    same_doc = (doc_index[:, :, None] == doc_index[:, None, :]) & causal[None]
    spread = jnp.minimum(decay_sum[..., :, None] - decay_sum[..., None, :], 0.0)
    pair_weight = jnp.where(same_doc[None], jnp.exp(spread), 0.0)
    to_end = jnp.where(
        (doc_index == doc_index[:, -1:])[None], jnp.exp(decay_sum[..., -1:] - decay_sum), 0.0
    )
    began_flag = doc_index == doc_index[:, :1] - doc_begin[:, :1]
    from_start = jnp.where(began_flag[None], jnp.exp(decay_sum), 0.0)
    return (pair_weight, to_end, from_start, from_start[..., -1])


def dot(left, right, contract):
    return lax.dot_general(
        left, right, ((contract[:1], contract[1:]), ((), ())), preferred_element_type=jnp.float32
    )


def projections(proj_ref, span):
    point_q, point_k = proj_ref[0, span], proj_ref[1, span]
    gate_q, gate_k = jax.nn.sigmoid(point_q), jax.nn.sigmoid(point_k)
    queries = (point_q * gate_q * HEAD_DIM ** (-0.5)).astype(jnp.bfloat16)
    keys = (point_k * gate_k).astype(jnp.bfloat16)
    values = proj_ref[2, span].astype(jnp.bfloat16)
    return (point_q, gate_q, queries), (point_k, gate_k, keys), values


def state_kernel(proj_ref, up_ref, start_ref, end_ref, key_ref, query_ref, total_ref):
    blocks = key_ref.shape[1]
    forward = jnp.zeros((HEAD_DIM, HEAD_DIM), jnp.float32)
    query_states, decays = [], []
    for b in range(blocks):
        span = pl.ds(b * BLOCK, BLOCK)
        (_, _, queries), (_, _, keys), values = projections(proj_ref, span)
        keys_weighted = (keys.astype(jnp.float32) * end_ref[0, span]).astype(jnp.bfloat16)
        queries_weighted = (queries.astype(jnp.float32) * start_ref[0, span]).astype(jnp.bfloat16)
        key_state = dot(keys_weighted, values, (0, 0))
        query_state = dot(queries_weighted, up_ref[span], (0, 0))
        key_ref[0, b] = key_state
        query_ref[0, b] = query_state
        decay = start_ref[0, pl.ds(b * BLOCK + BLOCK - 1, 1)]
        forward = decay * forward + key_state
        query_states.append(query_state)
        decays.append(decay)
    backward = jnp.zeros((HEAD_DIM, HEAD_DIM), jnp.float32)
    for b in reversed(range(blocks)):
        backward = decays[b] * backward + query_states[b]
    total_ref[0, 0] = forward.astype(jnp.bfloat16)
    total_ref[1, 0] = backward.astype(jnp.bfloat16)


def gradient_kernel(
    weight_ref, proj_ref, up_ref, start_ref, end_ref, pair_ref, key_ref, query_ref, *rest
):
    totals, out_ref = rest[:-1], rest[-1]
    blocks = key_ref.shape[1]
    head = pl.program_id(0)
    state = jnp.zeros((HEAD_DIM, HEAD_DIM), jnp.float32)
    reverse = jnp.zeros((HEAD_DIM, HEAD_DIM), jnp.float32)
    for k, total in enumerate(totals):
        state = state + weight_ref[0, k, head] * total[0, 0].astype(jnp.float32)
        reverse = reverse + weight_ref[1, k, head] * total[1, 0].astype(jnp.float32)
    decays = [start_ref[0, pl.ds(b * BLOCK + BLOCK - 1, 1)] for b in range(blocks)]
    after = [None] * blocks
    for b in reversed(range(blocks)):
        after[b] = reverse.astype(jnp.bfloat16)
        reverse = decays[b] * reverse + query_ref[0, b]
    for b in range(blocks):
        before = state.astype(jnp.bfloat16)
        state = decays[b] * state + key_ref[0, b]
        span = pl.ds(b * BLOCK, BLOCK)
        (point_q, gate_q, queries), (point_k, gate_k, keys), values = projections(proj_ref, span)
        upstream = up_ref[span]
        from_start, to_end, pair = start_ref[0, span], end_ref[0, span], pair_ref[0, b]
        query_key = (dot(queries, keys, (1, 1)) * pair).astype(jnp.bfloat16)
        value_score = (dot(upstream, values, (1, 1)) * pair).astype(jnp.bfloat16)
        query_gradient = dot(value_score, keys, (1, 0)) + from_start * dot(
            upstream, before, (1, 1)
        )
        key_gradient = dot(value_score, queries, (0, 0)) + to_end * dot(values, after[b], (1, 1))
        value_gradient = dot(query_key, upstream, (0, 0)) + to_end * dot(keys, after[b], (1, 0))
        slope_q = gate_q * (1.0 + point_q * (1.0 - gate_q)) * HEAD_DIM ** (-0.5)
        slope_k = gate_k * (1.0 + point_k * (1.0 - gate_k))
        out_ref[0, span] = (query_gradient * slope_q).astype(jnp.bfloat16)
        out_ref[1, span] = (key_gradient * slope_k).astype(jnp.bfloat16)
        out_ref[2, span] = value_gradient.astype(jnp.bfloat16)


def input_kernel(gradient_ref, weight_ref, out_ref):
    for first in range(0, out_ref.shape[0], BLOCK):
        span = pl.ds(first, BLOCK)
        total = dot(gradient_ref[0, span], weight_ref[0], (1, 1))
        for k in (1, 2):
            total = total + dot(gradient_ref[k, span], weight_ref[k], (1, 1))
        out_ref[span] = total.astype(jnp.bfloat16)


def general_body(inputs, projection, cotangent, log_decay, document_starts):
    tokens = inputs.shape[0]
    heads_here = log_decay.shape[0]
    local_cols = cotangent.shape[1]
    blocks = tokens // BLOCK
    features = lax.all_gather(inputs, "head", axis=1, tiled=True)
    rows = projection.shape[0]
    blocks_w = gather_rows(projection.transpose(1, 0, 2), "seq")

    def feature_rows(owner, first, count):
        return lax.dynamic_slice_in_dim(features, owner * rows + first, count, axis=1)

    offset = lax.axis_index("seq") * tokens
    positions = offset + jnp.arange(tokens, dtype=jnp.int32)
    doc_index = (
        jnp.sum((document_starts[None, :] <= positions[:, None]).astype(jnp.int32), axis=1) - 1
    )
    doc_begin = jnp.any(document_starts[None, :] == positions[:, None], axis=1).astype(jnp.int32)
    decay_sum = running_sum(log_decay.reshape(heads_here, blocks, BLOCK))
    pair_weight, to_end, from_start, block_decay = block_factors(
        decay_sum, doc_index.reshape(blocks, BLOCK), doc_begin.reshape(blocks, BLOCK)
    )
    lanes = (heads_here, tokens, HEAD_DIM)
    to_end = jnp.broadcast_to(to_end.reshape(heads_here, tokens)[..., None], lanes)
    from_start = jnp.broadcast_to(from_start.reshape(heads_here, tokens)[..., None], lanes)
    device_decay = jnp.prod(block_decay, axis=1)

    zero = jnp.zeros((), jnp.bfloat16)
    if len(blocks_w) > 2:
        owner, first, block = blocks_w[2]
        zero, block = lax.optimization_barrier((zero, block))
        blocks_w[2] = (owner, first, block)
    weights_all = jnp.broadcast_to(zero, (3, features.shape[1], local_cols))

    def place_rows(whole, some):
        for owner, first, block in some:
            whole = lax.dynamic_update_slice_in_dim(whole, block, owner * rows + first, axis=1)
        return whole

    early, late = blocks_w[:6], blocks_w[6:]
    weights_all = place_rows(weights_all, early)
    features, weights_all, from_start, to_end, pair_weight = lax.optimization_barrier(
        (features, weights_all, from_start, to_end, pair_weight)
    )
    projected = None
    for k, (owner, first, block) in enumerate(blocks_w):
        piece = jnp.einsum(
            "td,kdc->ktc",
            feature_rows(owner, first, block.shape[1]),
            block,
            preferred_element_type=jnp.float32,
        )
        projected = piece if projected is None else lax.optimization_barrier(projected) + piece
        if k == min(5, len(blocks_w) - 1):
            projected, device_decay = lax.optimization_barrier((projected, device_decay))
    weights_all = place_rows(weights_all, late)

    proj_spec = pl.BlockSpec((3, tokens, HEAD_DIM), lambda h: (0, 0, h))
    up_spec = pl.BlockSpec((tokens, HEAD_DIM), lambda h: (0, h))
    lane_spec = pl.BlockSpec((1, tokens, HEAD_DIM), lambda h: (h, 0, 0))
    state_spec = pl.BlockSpec((1, blocks, HEAD_DIM, HEAD_DIM), lambda h: (h, 0, 0, 0))
    total_spec = pl.BlockSpec((2, 1, HEAD_DIM, HEAD_DIM), lambda h: (0, h, 0, 0))
    pair_spec = pl.BlockSpec((1, blocks, BLOCK, BLOCK), lambda h: (h, 0, 0, 0))
    states = jax.ShapeDtypeStruct((heads_here, blocks, HEAD_DIM, HEAD_DIM), jnp.float32)
    key_state, query_state, totals = pl.pallas_call(
        state_kernel,
        grid=(heads_here,),
        in_specs=[proj_spec, up_spec, lane_spec, lane_spec],
        out_specs=[state_spec, state_spec, total_spec],
        out_shape=[
            states,
            states,
            jax.ShapeDtypeStruct((2, heads_here, HEAD_DIM, HEAD_DIM), jnp.bfloat16),
        ],
    )(projected, cotangent, from_start, to_end)
    parts, owners = gather_states(totals, "seq")
    weights = device_weights(device_decay, owners, "seq")
    project_gradient = pl.pallas_call(
        gradient_kernel,
        grid=(heads_here,),
        in_specs=[pl.BlockSpec(memory_space=pltpu.SMEM)]
        + [proj_spec, up_spec, lane_spec, lane_spec, pair_spec, state_spec, state_spec]
        + [total_spec] * len(parts),
        out_specs=proj_spec,
        out_shape=jax.ShapeDtypeStruct(projected.shape, jnp.bfloat16),
    )(weights, projected, cotangent, from_start, to_end, pair_weight, key_state, query_state, *parts)

    def weight_partial(gradient, owner, first, count):
        term = jnp.einsum(
            "td,ktc->kdc",
            feature_rows(owner, first, count),
            gradient,
            preferred_element_type=jnp.float32,
        ).astype(jnp.bfloat16)
        return with_layout_constraint(term, Layout(major_to_minor=(0, 1, 2)))

    def input_partial(gradient, part, of):
        columns = features.shape[1]
        tile, count = columns // 8, tokens // of
        return pl.pallas_call(
            input_kernel,
            grid=(columns // tile,),
            in_specs=[
                pl.BlockSpec((3, count, local_cols), lambda i: (0, part, 0)),
                pl.BlockSpec((3, tile, local_cols), lambda i: (0, i, 0)),
            ],
            out_specs=pl.BlockSpec((count, tile), lambda i: (0, i)),
            out_shape=jax.ShapeDtypeStruct((count, columns), jnp.bfloat16),
            cost_estimate=pl.CostEstimate(flops=1, bytes_accessed=1, transcendentals=0),
            compiler_params=pltpu.CompilerParams(vmem_limit_bytes=40 << 20),
        )(gradient, weights_all)

    input_partials, weight_gradient = scatter_rows(
        weight_partial, input_partial, project_gradient, "seq", rows
    )
    input_gradient = lax.psum_scatter(
        input_partials[0], "head", scatter_dimension=1, tiled=True
    )
    weight_gradient = weight_gradient.transpose(1, 0, 2)
    return (input_gradient, weight_gradient)


MESH = pl.DeviceIdType.MESH


def remote_maker(send, recv):
    def remote(index, source, target, device):
        return pltpu.make_async_remote_copy(
            src_ref=source,
            dst_ref=target,
            send_sem=send.at[index],
            recv_sem=recv.at[index],
            device_id=device,
            device_id_type=MESH,
        )

    return remote


def greet(others):
    barrier = pltpu.get_barrier_semaphore()
    for other in others:
        pl.semaphore_signal(barrier, inc=1, device_id=other, device_id_type=MESH)
    pl.semaphore_wait(barrier, len(others))


def gather_kernel(
    x_ref, w_ref, feats_out, wall_out, total_out, swap, feats, wall, total, send, recv, local
):
    place, head = lax.axis_index("seq"), lax.axis_index("head")
    z, core = head // 2, head % 2
    tokens, cols = x_ref.shape
    rows = w_ref.shape[1]
    half, near, chunk = tokens // 2, rows // 2, tokens // 8
    x_id, y_id, far_id = (place ^ 1, head), (place ^ 2, head), (place ^ 3, head)
    next_id, last_id = (place, (head + 2) % 8), (place, (head + 6) % 8)
    twin_id = (place, head ^ 1)
    mine = pl.ds(pl.multiple_of(core * cols, cols), cols)
    remote = remote_maker(send, recv)

    own_w = pltpu.make_async_copy(w_ref, wall.at[place], local.at[0])
    own_x = pltpu.make_async_copy(x_ref, feats.at[z, :, mine], local.at[1])
    own_w.start()
    own_x.start()

    def block(step, part):
        return feats.at[(z + 4 - step) % 4, pl.ds(part * half, half), mine]

    def x_part(step, part):
        return x_ref.at[pl.ds(part * half, half)] if step == 0 else block(step, part)

    ring = [
        [remote(2 * k + p, x_part(k, p), block(k, p), next_id) for p in range(2)] for k in range(3)
    ]
    twin = [
        [remote(6 + 2 * k + p, x_part(k, p), block(k, p), twin_id) for p in range(2)]
        for k in range(4)
    ]
    low, high = pl.ds(0, near), pl.ds(near, near)
    side = [
        remote(14 + i, w_ref.at[:, part], wall.at[place, :, part], device)
        for i, (part, device) in enumerate(((high, x_id), (low, y_id), (low, x_id), (high, y_id)))
    ]

    def quarter(owner, part):
        return wall.at[owner, :, pl.ds(part * (near // 2), near // 2)]

    far = [
        [
            remote(18 + 2 * i, quarter(place ^ 2, i), quarter(place ^ 2, i), x_id),
            remote(19 + 2 * i, quarter(place ^ 1, 2 + i), quarter(place ^ 1, 2 + i), y_id),
        ]
        for i in range(2)
    ]

    def share(who):
        return pl.ds(pl.multiple_of(who * chunk, chunk), chunk)

    mix = [
        remote(21 + flip, feats.at[place ^ flip, share(head)], swap.at[flip - 1, share(head)], device)
        for flip, device in ((1, x_id), (2, y_id), (3, far_id))
    ]

    def shared(step):
        return swap.at[:, share((head + 8 - 2 * step) % 8)]

    spread = [remote(25 + k, shared(k), shared(k), next_id) for k in range(2)]
    spread_twin = [remote(27 + k, shared(k), shared(k), twin_id) for k in range(3)]

    greet((x_id, y_id, far_id, next_id, last_id, twin_id))
    ring[0][0].start()
    side[0].start()
    side[1].start()
    ring[0][1].start()
    twin[0][0].start()
    twin[0][1].start()

    def arrived(step, part):
        ring[step][part].wait_recv()
        if step < 2:
            ring[step + 1][part].start()
        twin[step + 1][part].start()

    def multiply(owner, begin, top, count):
        @pl.loop(0, 6)
        def _(i):
            k, span = i // 2, pl.ds(pl.multiple_of(i % 2 * half, half), half)
            term = jnp.dot(
                feats[owner, span, pl.ds(top, count)],
                wall[owner, k, pl.ds(top, count), :],
                preferred_element_type=jnp.float32,
            )
            total[k, span, :] = term if begin else total[k, span, :] + term

    arrived(0, 0)
    arrived(0, 1)
    arrived(1, 0)
    side[0].wait_recv()
    side[1].wait_recv()
    side[2].start()
    side[3].start()
    arrived(1, 1)
    own_w.wait()
    own_x.wait()
    arrived(2, 0)
    arrived(2, 1)
    for pair in twin:
        for move in pair:
            move.wait_recv()
    for move in mix:
        move.start()
    side[2].wait_recv()
    far[0][0].start()
    far[1][0].start()
    side[3].wait_recv()
    far[0][1].start()
    far[1][1].start()
    feats_copy = pltpu.make_async_copy(feats, feats_out, local.at[2])
    feats_copy.start()
    multiply(place, True, 0, rows)
    for move in mix:
        move.wait_recv()
    spread[0].start()
    spread_twin[0].start()
    multiply(place ^ 1, False, 0, rows)
    multiply(place ^ 2, False, 0, rows)
    near_copies = [
        pltpu.make_async_copy(wall.at[place ^ f], wall_out.at[place ^ f], local.at[3 + f])
        for f in range(3)
    ]
    for move in near_copies:
        move.start()
    spread[0].wait_recv()
    spread[1].start()
    spread_twin[1].start()
    for i in range(2):
        for move in far[i]:
            move.wait_recv()
        multiply(place ^ 3, False, i * (near // 2), near // 2)
        multiply(place ^ 3, False, near + i * (near // 2), near // 2)
    far_copy = pltpu.make_async_copy(wall.at[place ^ 3], wall_out.at[place ^ 3], local.at[6])
    far_copy.start()
    total_copy = pltpu.make_async_copy(total, total_out, local.at[7])
    total_copy.start()
    spread[1].wait_recv()
    spread_twin[2].start()
    for move in spread_twin:
        move.wait_recv()
    for move in (feats_copy, *near_copies, far_copy, total_copy):
        move.wait()
    for move in (*ring[0], *ring[1], *ring[2], *side, *far[0], *far[1], *mix, *spread, *spread_twin):
        move.wait_send()
    for pair in twin:
        for move in pair:
            move.wait_send()


def gather_call(inputs, weights):
    (tokens, cols), (_, rows, local_cols) = inputs.shape, weights.shape
    bf16, f32 = jnp.bfloat16, jnp.float32
    shapes = [
        ((4, tokens, 2 * cols), bf16),
        ((4, 3, rows, local_cols), bf16),
        ((3, tokens, local_cols), f32),
        ((3, tokens, 2 * cols), bf16),
    ]
    anywhere = pl.BlockSpec(memory_space=pl.ANY)
    return pl.pallas_call(
        gather_kernel,
        in_specs=[anywhere] * 2,
        out_specs=[anywhere] * 4,
        out_shape=[jax.ShapeDtypeStruct(*shape) for shape in shapes],
        scratch_shapes=[pltpu.VMEM(*shape) for shape in shapes[:3]]
        + [
            pltpu.SemaphoreType.DMA((30,)),
            pltpu.SemaphoreType.DMA((30,)),
            pltpu.SemaphoreType.DMA((8,)),
        ],
        compiler_params=pltpu.CompilerParams(
            collective_id=0, has_side_effects=True, vmem_limit_bytes=48 << 20
        ),
        name="gather",
    )(inputs, weights)


def finish_kernel(
    share_ref, marks_ref, proj_ref, up_ref, feats_ref, wall_ref, swap_ref, input_out, weight_out,
    grads, tokens_buf, rows_buf, total, keep, twin_out, twin_in, ring_out, ring_in,
    late, sums_out, sums_in, send, recv, local,
):
    place, head = lax.axis_index("seq"), lax.axis_index("head")
    z, core = head // 2, head % 2
    _, tokens, local_cols = proj_ref.shape
    blocks, pair_cols = tokens // BLOCK, local_cols // 2
    rows, cols = total.shape[1], keep.shape[1]
    half, chunk = tokens // 2, tokens // 8
    x_id, y_id, far_id = (place ^ 1, head), (place ^ 2, head), (place ^ 3, head)
    next_id, last_id = (place, (head + 2) % 8), (place, (head + 6) % 8)
    twin_id = (place, head ^ 1)
    remote = remote_maker(send, recv)
    low, high = pl.ds(0, half), pl.ds(half, half)

    def fetch_rows(turn, part):
        owner = (z + 7 - turn) % 4
        side = pl.multiple_of((core if part else 1 - core) * cols, cols)
        return pltpu.make_async_copy(
            wall_ref.at[owner, :, pl.ds(side, cols)], rows_buf.at[part], local.at[part]
        )

    def fetch_tokens(flip):
        slot = flip % 2
        if flip == 0:
            return [
                pltpu.make_async_copy(feats_ref.at[place], tokens_buf.at[slot], local.at[2])
            ]
        copies = []
        for i in range(3):
            top = pl.multiple_of((z + 2 + i) % 4 * (2 * chunk), 2 * chunk)
            copies.append(
                pltpu.make_async_copy(
                    swap_ref.at[flip - 1, pl.ds(top, 2 * chunk)],
                    tokens_buf.at[slot, pl.ds(top, 2 * chunk)],
                    local.at[3 + 5 * flip + i],
                )
            )
        for i, who in enumerate(((head + 2) % 8, (head + 2) % 8 + 1 - 2 * core)):
            top = pl.multiple_of(who * chunk, chunk)
            copies.append(
                pltpu.make_async_copy(
                    late.at[i, flip - 1],
                    tokens_buf.at[slot, pl.ds(top, chunk)],
                    local.at[6 + 5 * flip + i],
                )
            )
        return copies

    own = [
        pltpu.make_async_copy(proj_ref, total.at[:, pl.ds(0, tokens)], local.at[23]),
        pltpu.make_async_copy(up_ref, twin_out.at[1, :, pl.ds(0, local_cols)], local.at[24]),
    ]
    for move in own:
        move.start()
    fetched_rows = [fetch_rows(0, 0), fetch_rows(0, 1)]
    for move in fetched_rows:
        move.start()

    def columns(pair):
        return pl.ds(pair * pair_cols, pair_cols)

    side = [
        [
            remote(
                4 * pair + i, grads.at[0, :, part, columns(pair)],
                grads.at[flip, :, part, columns(pair)], device,
            )
            for i, (part, flip, device) in enumerate(
                ((high, 1, x_id), (low, 2, y_id), (low, 1, x_id), (high, 2, y_id))
            )
        ]
        for pair in range(2)
    ]
    far = [
        [
            remote(
                8 + 2 * pair + i, grads.at[flip, :, part, columns(pair)],
                grads.at[3, :, part, columns(pair)], device,
            )
            for i, (part, flip, device) in enumerate(((low, 2, x_id), (high, 1, y_id)))
        ]
        for pair in range(2)
    ]
    twin = [remote(12 + k, twin_out.at[k % 2], twin_in.at[k], twin_id) for k in range(4)]
    ring = [
        [
            remote(16 + 2 * k + p, ring_out.at[k, part], ring_in.at[k, part], next_id)
            for p, part in enumerate((low, high))
        ]
        for k in range(3)
    ]
    last_rows = pl.ds(pl.multiple_of((head + 4) % 8 * chunk, chunk), chunk)
    late_ring = remote(22, swap_ref.at[:, last_rows], late.at[0], next_id)
    late_twin = remote(23, late.at[0], late.at[1], twin_id)
    upper = (place % 2, place // 2, place // 2)
    sums = [
        [
            remote(
                24 + 3 * pair + flip - 1,
                sums_out.at[upper[flip - 1], pl.ds(2 * pair, 2)],
                sums_in.at[flip - 1, pl.ds(2 * pair, 2)], device,
            )
            for flip, device in ((1, x_id), (2, y_id), (3, far_id))
        ]
        for pair in range(2)
    ]
    greet((x_id, y_id, far_id, next_id, last_id, twin_id))
    late_ring.start()
    for b in range(blocks):
        span = pl.ds(b * BLOCK, BLOCK)
        for row in range(5):
            wide = jnp.broadcast_to(marks_ref[pl.ds(row, 1), span], (HEAD_DIM, BLOCK))
            keep[span, pl.ds(row * HEAD_DIM, HEAD_DIM)] = wide.T
    for move in own:
        move.wait()

    def factors(b, lane):
        span = pl.ds(b * BLOCK, BLOCK)
        decay, doc = keep[span, lane], keep[span, pl.ds(4 * HEAD_DIM, HEAD_DIM)]
        one = pl.ds(b * BLOCK, HEAD_DIM)
        last = keep[pl.ds(b * BLOCK + BLOCK - 1, 1), lane]
        from_start = jnp.where(doc == marks_ref[pl.ds(5, 1), one], jnp.exp(decay), 0.0)
        to_end = jnp.where(doc == marks_ref[pl.ds(6, 1), one], jnp.exp(last - decay), 0.0)
        return decay, doc, from_start, to_end

    def project(b, lane):
        span = pl.ds(b * BLOCK, BLOCK)
        point_q, point_k = total[0, span, lane], total[1, span, lane]
        gate_q, gate_k = jax.nn.sigmoid(point_q), jax.nn.sigmoid(point_k)
        queries = (point_q * gate_q * HEAD_DIM ** (-0.5)).astype(jnp.bfloat16)
        keys = (point_k * gate_k).astype(jnp.bfloat16)
        values = total[2, span, lane].astype(jnp.bfloat16)
        return (point_q, gate_q, queries), (point_k, gate_k, keys), values

    def state_rows(b):
        return pl.ds(tokens + b * HEAD_DIM, HEAD_DIM)

    def summarize(pair):
        @pl.loop(0, 2)
        def _(i):
            h = 2 * pair + i
            lane = pl.ds(pl.multiple_of(h * HEAD_DIM, HEAD_DIM), HEAD_DIM)
            forward = jnp.zeros((HEAD_DIM, HEAD_DIM), jnp.float32)
            query_states, decays = [], []
            for b in range(blocks):
                _, _, from_start, to_end = factors(b, lane)
                (_, _, queries), (_, _, keys), values = project(b, lane)
                weighted = (keys.astype(jnp.float32) * to_end).astype(jnp.bfloat16)
                key_state = dot(weighted, values, (0, 0))
                weighted = (queries.astype(jnp.float32) * from_start).astype(jnp.bfloat16)
                upstream = twin_out[1, pl.ds(b * BLOCK, BLOCK), lane]
                query_state = dot(weighted, upstream, (0, 0))
                total[0, state_rows(b), lane] = key_state
                total[1, state_rows(b), lane] = query_state
                decay = from_start[BLOCK - 1 :]
                forward = decay * forward + key_state
                query_states.append(query_state)
                decays.append(decay)
            backward = jnp.zeros((HEAD_DIM, HEAD_DIM), jnp.float32)
            for b in reversed(range(blocks)):
                backward = decays[b] * backward + query_states[b]
            sums_out[0, h] = forward.astype(jnp.bfloat16)
            sums_out[1, h] = backward.astype(jnp.bfloat16)

        for move in sums[pair]:
            move.start()

    def differentiate(pair):
        for move in sums[pair]:
            move.wait_recv()

        @pl.loop(0, 2)
        def _(i):
            h = 2 * pair + i
            lane = pl.ds(pl.multiple_of(h * HEAD_DIM, HEAD_DIM), HEAD_DIM)
            state = jnp.zeros((HEAD_DIM, HEAD_DIM), jnp.float32)
            reverse = jnp.zeros((HEAD_DIM, HEAD_DIM), jnp.float32)
            for k in range(3):
                arrived = sums_in[k, h].astype(jnp.float32)
                state = state + share_ref[0, k + 1, h] * arrived
                reverse = reverse + share_ref[1, k + 1, h] * arrived
            decays = [factors(b, lane)[2][BLOCK - 1 :] for b in range(blocks)]
            behind = [None] * blocks
            for b in reversed(range(blocks)):
                behind[b] = reverse.astype(jnp.bfloat16)
                reverse = decays[b] * reverse + total[1, state_rows(b), lane]
            for b in range(blocks):
                before = state.astype(jnp.bfloat16)
                state = decays[b] * state + total[0, state_rows(b), lane]
                span = pl.ds(b * BLOCK, BLOCK)
                decay, doc, from_start, to_end = factors(b, lane)
                spread = jnp.minimum(
                    jnp.concatenate([decay, decay], axis=1) - marks_ref[pl.ds(h, 1), span], 0.0
                )
                rows_at = lax.broadcasted_iota(jnp.int32, (BLOCK, BLOCK), 0)
                cols_at = lax.broadcasted_iota(jnp.int32, (BLOCK, BLOCK), 1)
                same = jnp.concatenate([doc, doc], axis=1) == marks_ref[pl.ds(4, 1), span]
                pair_weight = jnp.where(same & (rows_at >= cols_at), jnp.exp(spread), 0.0)
                (point_q, gate_q, queries), (point_k, gate_k, keys), values = project(b, lane)
                upstream = twin_out[1, span, lane]
                query_key = (dot(queries, keys, (1, 1)) * pair_weight).astype(jnp.bfloat16)
                value_score = (dot(upstream, values, (1, 1)) * pair_weight).astype(jnp.bfloat16)
                query_gradient = dot(value_score, keys, (1, 0)) + from_start * dot(
                    upstream, before, (1, 1)
                )
                key_gradient = dot(value_score, queries, (0, 0)) + to_end * dot(
                    values, behind[b], (1, 1)
                )
                value_gradient = dot(query_key, upstream, (0, 0)) + to_end * dot(
                    keys, behind[b], (1, 0)
                )
                slope_q = gate_q * (1.0 + point_q * (1.0 - gate_q)) * HEAD_DIM ** (-0.5)
                slope_k = gate_k * (1.0 + point_k * (1.0 - gate_k))
                grads[0, 0, span, lane] = (query_gradient * slope_q).astype(jnp.bfloat16)
                grads[0, 1, span, lane] = (key_gradient * slope_k).astype(jnp.bfloat16)
                grads[0, 2, span, lane] = value_gradient.astype(jnp.bfloat16)

        for move in side[pair]:
            move.start()

    summarize(0)
    summarize(1)
    differentiate(0)
    differentiate(1)
    late_ring.wait_recv()
    late_twin.start()

    def back(part, target):
        fetched_rows[part].wait()

        @pl.loop(0, 4)
        def _(i):
            span = pl.ds(pl.multiple_of(i * (tokens // 4), tokens // 4), tokens // 4)
            term = None
            for k in range(3):
                piece = dot(grads[0, k, span, :], rows_buf[part, k], (1, 1))
                term = piece if term is None else term + piece
            target[span, :] = term.astype(target.dtype)

    def input_block(turn):
        if turn >= 2:
            twin[turn - 2].wait_send()
        back(0, twin_out.at[turn % 2])
        twin[turn].start()
        if turn < 3:
            fetched_rows[0] = fetch_rows(turn + 1, 0)
            fetched_rows[0].start()
        back(1, keep)
        if turn < 3:
            fetched_rows[1] = fetch_rows(turn + 1, 1)
            fetched_rows[1].start()
        twin[turn].wait_recv()

    def pass_on(turn):
        for p, part in enumerate((low, high)):
            if turn > 0:
                ring[turn - 1][p].wait_recv()

            @pl.loop(0, 2)
            def _(i):
                quarter = tokens // 4
                span = pl.ds(pl.multiple_of(p * half + i * quarter, quarter), quarter)
                sum_ = keep[span, :] + twin_in[turn, span, :].astype(jnp.float32)
                if turn > 0:
                    sum_ = sum_ + ring_in[turn - 1, span, :].astype(jnp.float32)
                target = ring_out.at[turn] if turn < 3 else twin_out.at[0]
                target[span, :] = sum_.astype(jnp.bfloat16)

            if turn < 3:
                ring[turn][p].start()

    def weight_block(flip):
        slot = flip % 2
        for move in fetched[slot]:
            move.wait()

        @pl.loop(0, rows // BLOCK)
        def _(i):
            span = pl.ds(pl.multiple_of(i * BLOCK, BLOCK), BLOCK)
            turned = tokens_buf[slot, :, span].T
            for k in range(3):
                term = jnp.dot(turned, grads[flip, k], preferred_element_type=jnp.float32)
                total[k, span, :] = term if flip == 0 else total[k, span, :] + term

        if flip < 2:
            fetched[slot] = fetch_tokens(flip + 2)
            for move in fetched[slot]:
                move.start()

    input_block(0)
    pass_on(0)
    late_twin.wait_recv()
    fetched = [fetch_tokens(0), fetch_tokens(1)]
    for moves in fetched:
        for move in moves:
            move.start()
    input_block(1)
    weight_block(0)
    for pair in range(2):
        side[pair][0].wait_recv()
        far[pair][1].start()
        side[pair][1].wait_recv()
        far[pair][0].start()
    pass_on(1)
    input_block(2)
    for pair in range(2):
        side[pair][2].wait_recv()
    weight_block(1)
    pass_on(2)
    input_block(3)
    for pair in range(2):
        side[pair][3].wait_recv()
    weight_block(2)
    for moves in far:
        for move in moves:
            move.wait_recv()
    weight_block(3)
    stores = []
    for part in range(2):
        span = pl.ds(part * (rows // 2), rows // 2)
        for k in range(3):
            rows_buf[part, k] = total[k, span, :].astype(jnp.bfloat16)
        stores.append(
            pltpu.make_async_copy(rows_buf.at[part], weight_out.at[:, span], local.at[part])
        )
        stores[-1].start()
    twin[2].wait_send()
    twin[3].wait_send()
    pass_on(3)
    stores.append(pltpu.make_async_copy(twin_out.at[0], input_out, local.at[23]))
    stores[-1].start()
    for move in stores:
        move.wait()
    for move in (*side[0], *side[1], *far[0], *far[1], *ring[0], *ring[1], *ring[2], *sums[0], *sums[1], late_ring, late_twin):
        move.wait_send()


def finish_call(share, marks, projected, cotangent, feats, wall, swap):
    _, tokens, local_cols = projected.shape
    rows = wall.shape[2]
    cols = rows // 2
    bf16, f32 = jnp.bfloat16, jnp.float32
    anywhere = pl.BlockSpec(memory_space=pl.ANY)
    return pl.pallas_call(
        finish_kernel,
        in_specs=[pl.BlockSpec(memory_space=pltpu.SMEM), pl.BlockSpec(memory_space=pltpu.VMEM)]
        + [anywhere] * 5,
        out_specs=[anywhere] * 2,
        out_shape=[
            jax.ShapeDtypeStruct((tokens, cols), bf16),
            jax.ShapeDtypeStruct((3, rows, local_cols), bf16),
        ],
        scratch_shapes=[
            pltpu.VMEM((4, 3, tokens, local_cols), bf16),
            pltpu.VMEM((2, tokens, rows), bf16),
            pltpu.VMEM((2, 3, cols, local_cols), bf16),
            pltpu.VMEM((3, rows, local_cols), f32),
            pltpu.VMEM((tokens, cols), f32),
            pltpu.VMEM((2, tokens, cols), bf16),
            pltpu.VMEM((4, tokens, cols), bf16),
            pltpu.VMEM((3, tokens, cols), bf16),
            pltpu.VMEM((3, tokens, cols), bf16),
            pltpu.VMEM((2, 3, tokens // 8, rows), bf16),
            pltpu.VMEM((2, 4, HEAD_DIM, HEAD_DIM), bf16),
            pltpu.VMEM((3, 4, HEAD_DIM, HEAD_DIM), bf16),
            pltpu.SemaphoreType.DMA((30,)),
            pltpu.SemaphoreType.DMA((30,)),
            pltpu.SemaphoreType.DMA((25,)),
        ],
        compiler_params=pltpu.CompilerParams(
            collective_id=1, has_side_effects=True, vmem_limit_bytes=62 << 20
        ),
        name="finish",
    )(share, marks, projected, cotangent, feats, wall, swap)


def fast_body(inputs, projection, cotangent, log_decay, document_starts):
    tokens = inputs.shape[0]
    heads_here = log_decay.shape[0]
    blocks = tokens // BLOCK
    place = lax.axis_index("seq")
    feats, wall, projected, swap = gather_call(inputs, projection.transpose(1, 0, 2))

    positions = place * tokens + jnp.arange(tokens, dtype=jnp.int32)
    doc_index = (
        jnp.sum((document_starts[None, :] <= positions[:, None]).astype(jnp.int32), axis=1) - 1
    )
    doc_begin = jnp.any(document_starts[None, :] == positions[:, None], axis=1).astype(jnp.int32)
    decay_sum = running_sum(log_decay.reshape(heads_here, blocks, BLOCK))
    doc_index, doc_begin = doc_index.reshape(blocks, BLOCK), doc_begin.reshape(blocks, BLOCK)
    began = doc_index == doc_index[:, :1] - doc_begin[:, :1]
    block_decay = jnp.where(began[None, :, -1], jnp.exp(decay_sum[..., -1]), 0.0)
    owners = place ^ jnp.arange(4, dtype=jnp.int32)
    share = device_weights(jnp.prod(block_decay, axis=1), owners, "seq")
    first = jnp.broadcast_to(doc_index[:, :1] - doc_begin[:, :1], doc_index.shape)
    last = jnp.broadcast_to(doc_index[:, -1:], doc_index.shape)
    documents = jnp.stack([doc_index, first, last, last]).reshape(4, tokens).astype(jnp.float32)
    marks = jnp.concatenate([decay_sum.reshape(heads_here, tokens), documents])
    input_gradient, weight_gradient = finish_call(
        share, marks, projected, cotangent, feats, wall, swap
    )
    return (input_gradient, weight_gradient.transpose(1, 0, 2))


def solution(mesh):
    fast = (mesh.shape["seq"], mesh.shape["head"]) == (4, 8)
    placed = (P("seq", "head"), P("seq", None, "head"), P("seq", "head"), P("head", "seq"), P())
    return jax.shard_map(
        fast_body if fast else general_body,
        mesh=mesh,
        in_specs=placed,
        out_specs=(P("seq", "head"), P("seq", None, "head")),
        check_vma=False,
    )
```

```python
import jax
import jax.numpy as jnp
from jax import lax
from jax.experimental import pallas as pl
from jax.experimental.layout import Layout, with_layout_constraint
from jax.experimental.pallas import tpu as pltpu
from jax.sharding import PartitionSpec as P

HEAD_DIM = 128
BLOCK = 256


def hop(array, axis, flip):
    return lax.ppermute(array, axis, [(i, i ^ flip) for i in range(lax.axis_size(axis))])


def gather_states(packed, axis):
    length, place = (lax.axis_size(axis), lax.axis_index(axis))
    if length != 4:
        whole = lax.all_gather(packed, axis)
        return [whole[k] for k in range(length)], jnp.arange(length, dtype=jnp.int32)
    parts = [packed] + [hop(packed, axis, flip) for flip in range(1, length)]
    return parts, place ^ jnp.arange(length, dtype=jnp.int32)


def device_weights(device_decay, owners, axis):
    length, place = (lax.axis_size(axis), lax.axis_index(axis))
    if length == 4:
        slab = jnp.broadcast_to(device_decay[:, None], (device_decay.shape[0], HEAD_DIM))
        hops = [slab] + [hop(slab, axis, flip) for flip in range(1, length)]
        arrived = jnp.stack([part[:, 0] for part in hops])
        mine = owners[None, :] == jnp.arange(length, dtype=jnp.int32)[:, None]
        decays = jnp.sum(jnp.where(mine[:, :, None], arrived[None], 0.0), axis=1)
    else:
        decays = lax.all_gather(device_decay, axis)
    at, other = owners[:, None], jnp.arange(length, dtype=jnp.int32)[None]
    before = (other > at) & (other < place)
    after = (other < at) & (other > place)
    weights = []
    for between, counts in ((before, owners < place), (after, owners > place)):
        product = jnp.prod(jnp.where(between[:, :, None], decays[None], 1.0), axis=1)
        weights.append(jnp.where(counts[:, None], product, 0.0))
    return jnp.stack(weights)


def gather_rows(part, axis):
    length, place, rows = (lax.axis_size(axis), lax.axis_index(axis), part.shape[1])
    if length != 4:
        whole = lax.all_gather(part, axis, axis=1, tiled=True)
        return [(0, 0, whole)]
    half = rows // 2
    low, high = part[:, :half], part[:, half:]
    x_high = hop(high, axis, 1)
    y_low = hop(low, axis, 2)
    x_low = hop(low, axis, 1)
    y_high = hop(high, axis, 2)
    d_low = hop(y_low, axis, 1)
    d_high = hop(x_high, axis, 2)
    return [
        (place, 0, low),
        (place, half, high),
        (place ^ 1, half, x_high),
        (place ^ 2, 0, y_low),
        (place ^ 1, 0, x_low),
        (place ^ 2, half, y_high),
        (place ^ 3, 0, d_low),
        (place ^ 3, half, d_high),
    ]


def scatter_rows(partial, between, source, axis, rows):
    length, place = (lax.axis_size(axis), lax.axis_index(axis))
    if length != 4:
        whole = partial(source, 0, 0, rows * length)
        return [between(source, 0, 1)], lax.psum_scatter(whole, axis, scatter_dimension=1, tiled=True)
    half = rows // 2

    def add(*terms):
        return sum(term.astype(jnp.float32) for term in terms).astype(jnp.bfloat16)

    far_low, far_high = partial(source, place ^ 3, 0, half), partial(source, place ^ 3, half, half)
    source, far_low, far_high = lax.optimization_barrier((source, far_low, far_high))
    far_low, far_high = hop(far_low, axis, 1), hop(far_high, axis, 2)
    beside = between(source, 0, 1)
    source, beside = lax.optimization_barrier((source, beside))
    x_low, y_high = partial(source, place ^ 1, 0, half), partial(source, place ^ 2, half, half)
    source, x_low, y_high = lax.optimization_barrier((source, x_low, y_high))
    x_low, y_high = hop(x_low, axis, 1), hop(y_high, axis, 2)
    x_high = hop(add(partial(source, place ^ 1, half, half), far_high), axis, 1)
    y_low = hop(add(partial(source, place ^ 2, 0, half), far_low), axis, 2)
    own_low, own_high = partial(source, place, 0, half), partial(source, place, half, half)
    whole = jnp.concatenate([add(own_low, x_low, y_low), add(own_high, x_high, y_high)], axis=1)
    return [beside], whole


def running_sum(values):
    inside = jnp.arange(values.shape[-1], dtype=jnp.int32)
    triangle = (inside[:, None] <= inside[None, :]).astype(jnp.float32)
    return jnp.einsum("hbu,ut->hbt", values, triangle, precision=lax.Precision.HIGHEST)


def block_factors(decay_sum, doc_index, doc_begin):
    inside = jnp.arange(doc_index.shape[-1], dtype=jnp.int32)
    causal = inside[:, None] >= inside[None, :]
    same_doc = (doc_index[:, :, None] == doc_index[:, None, :]) & causal[None]
    spread = jnp.minimum(decay_sum[..., :, None] - decay_sum[..., None, :], 0.0)
    pair_weight = jnp.where(same_doc[None], jnp.exp(spread), 0.0)
    to_end = jnp.where(
        (doc_index == doc_index[:, -1:])[None], jnp.exp(decay_sum[..., -1:] - decay_sum), 0.0
    )
    began_flag = doc_index == doc_index[:, :1] - doc_begin[:, :1]
    from_start = jnp.where(began_flag[None], jnp.exp(decay_sum), 0.0)
    return (pair_weight, to_end, from_start, from_start[..., -1])


def dot(left, right, contract):
    return lax.dot_general(
        left, right, ((contract[:1], contract[1:]), ((), ())), preferred_element_type=jnp.float32
    )


def projections(proj_ref, span):
    point_q, point_k = proj_ref[0, span], proj_ref[1, span]
    gate_q, gate_k = jax.nn.sigmoid(point_q), jax.nn.sigmoid(point_k)
    queries = (point_q * gate_q * HEAD_DIM ** (-0.5)).astype(jnp.bfloat16)
    keys = (point_k * gate_k).astype(jnp.bfloat16)
    values = proj_ref[2, span].astype(jnp.bfloat16)
    return (point_q, gate_q, queries), (point_k, gate_k, keys), values


def state_kernel(proj_ref, up_ref, start_ref, end_ref, key_ref, query_ref, total_ref):
    blocks = key_ref.shape[1]
    forward = jnp.zeros((HEAD_DIM, HEAD_DIM), jnp.float32)
    query_states, decays = [], []
    for b in range(blocks):
        span = pl.ds(b * BLOCK, BLOCK)
        (_, _, queries), (_, _, keys), values = projections(proj_ref, span)
        keys_weighted = (keys.astype(jnp.float32) * end_ref[0, span]).astype(jnp.bfloat16)
        queries_weighted = (queries.astype(jnp.float32) * start_ref[0, span]).astype(jnp.bfloat16)
        key_state = dot(keys_weighted, values, (0, 0))
        query_state = dot(queries_weighted, up_ref[span], (0, 0))
        key_ref[0, b] = key_state
        query_ref[0, b] = query_state
        decay = start_ref[0, pl.ds(b * BLOCK + BLOCK - 1, 1)]
        forward = decay * forward + key_state
        query_states.append(query_state)
        decays.append(decay)
    backward = jnp.zeros((HEAD_DIM, HEAD_DIM), jnp.float32)
    for b in reversed(range(blocks)):
        backward = decays[b] * backward + query_states[b]
    total_ref[0, 0] = forward.astype(jnp.bfloat16)
    total_ref[1, 0] = backward.astype(jnp.bfloat16)


def gradient_kernel(
    weight_ref, proj_ref, up_ref, start_ref, end_ref, pair_ref, key_ref, query_ref, *rest
):
    totals, out_ref = rest[:-1], rest[-1]
    blocks = key_ref.shape[1]
    head = pl.program_id(0)
    state = jnp.zeros((HEAD_DIM, HEAD_DIM), jnp.float32)
    reverse = jnp.zeros((HEAD_DIM, HEAD_DIM), jnp.float32)
    for k, total in enumerate(totals):
        state = state + weight_ref[0, k, head] * total[0, 0].astype(jnp.float32)
        reverse = reverse + weight_ref[1, k, head] * total[1, 0].astype(jnp.float32)
    decays = [start_ref[0, pl.ds(b * BLOCK + BLOCK - 1, 1)] for b in range(blocks)]
    after = [None] * blocks
    for b in reversed(range(blocks)):
        after[b] = reverse.astype(jnp.bfloat16)
        reverse = decays[b] * reverse + query_ref[0, b]
    for b in range(blocks):
        before = state.astype(jnp.bfloat16)
        state = decays[b] * state + key_ref[0, b]
        span = pl.ds(b * BLOCK, BLOCK)
        (point_q, gate_q, queries), (point_k, gate_k, keys), values = projections(proj_ref, span)
        upstream = up_ref[span]
        from_start, to_end, pair = start_ref[0, span], end_ref[0, span], pair_ref[0, b]
        query_key = (dot(queries, keys, (1, 1)) * pair).astype(jnp.bfloat16)
        value_score = (dot(upstream, values, (1, 1)) * pair).astype(jnp.bfloat16)
        query_gradient = dot(value_score, keys, (1, 0)) + from_start * dot(
            upstream, before, (1, 1)
        )
        key_gradient = dot(value_score, queries, (0, 0)) + to_end * dot(values, after[b], (1, 1))
        value_gradient = dot(query_key, upstream, (0, 0)) + to_end * dot(keys, after[b], (1, 0))
        slope_q = gate_q * (1.0 + point_q * (1.0 - gate_q)) * HEAD_DIM ** (-0.5)
        slope_k = gate_k * (1.0 + point_k * (1.0 - gate_k))
        out_ref[0, span] = (query_gradient * slope_q).astype(jnp.bfloat16)
        out_ref[1, span] = (key_gradient * slope_k).astype(jnp.bfloat16)
        out_ref[2, span] = value_gradient.astype(jnp.bfloat16)


def input_kernel(gradient_ref, weight_ref, out_ref):
    for first in range(0, out_ref.shape[0], BLOCK):
        span = pl.ds(first, BLOCK)
        total = dot(gradient_ref[0, span], weight_ref[0], (1, 1))
        for k in (1, 2):
            total = total + dot(gradient_ref[k, span], weight_ref[k], (1, 1))
        out_ref[span] = total.astype(jnp.bfloat16)


def general_body(inputs, projection, cotangent, log_decay, document_starts):
    tokens = inputs.shape[0]
    heads_here = log_decay.shape[0]
    local_cols = cotangent.shape[1]
    blocks = tokens // BLOCK
    features = lax.all_gather(inputs, "head", axis=1, tiled=True)
    rows = projection.shape[0]
    blocks_w = gather_rows(projection.transpose(1, 0, 2), "seq")

    def feature_rows(owner, first, count):
        return lax.dynamic_slice_in_dim(features, owner * rows + first, count, axis=1)

    offset = lax.axis_index("seq") * tokens
    positions = offset + jnp.arange(tokens, dtype=jnp.int32)
    doc_index = (
        jnp.sum((document_starts[None, :] <= positions[:, None]).astype(jnp.int32), axis=1) - 1
    )
    doc_begin = jnp.any(document_starts[None, :] == positions[:, None], axis=1).astype(jnp.int32)
    decay_sum = running_sum(log_decay.reshape(heads_here, blocks, BLOCK))
    pair_weight, to_end, from_start, block_decay = block_factors(
        decay_sum, doc_index.reshape(blocks, BLOCK), doc_begin.reshape(blocks, BLOCK)
    )
    lanes = (heads_here, tokens, HEAD_DIM)
    to_end = jnp.broadcast_to(to_end.reshape(heads_here, tokens)[..., None], lanes)
    from_start = jnp.broadcast_to(from_start.reshape(heads_here, tokens)[..., None], lanes)
    device_decay = jnp.prod(block_decay, axis=1)

    zero = jnp.zeros((), jnp.bfloat16)
    if len(blocks_w) > 2:
        owner, first, block = blocks_w[2]
        zero, block = lax.optimization_barrier((zero, block))
        blocks_w[2] = (owner, first, block)
    weights_all = jnp.broadcast_to(zero, (3, features.shape[1], local_cols))

    def place_rows(whole, some):
        for owner, first, block in some:
            whole = lax.dynamic_update_slice_in_dim(whole, block, owner * rows + first, axis=1)
        return whole

    early, late = blocks_w[:6], blocks_w[6:]
    weights_all = place_rows(weights_all, early)
    features, weights_all, from_start, to_end, pair_weight = lax.optimization_barrier(
        (features, weights_all, from_start, to_end, pair_weight)
    )
    projected = None
    for k, (owner, first, block) in enumerate(blocks_w):
        piece = jnp.einsum(
            "td,kdc->ktc",
            feature_rows(owner, first, block.shape[1]),
            block,
            preferred_element_type=jnp.float32,
        )
        projected = piece if projected is None else lax.optimization_barrier(projected) + piece
        if k == min(5, len(blocks_w) - 1):
            projected, device_decay = lax.optimization_barrier((projected, device_decay))
    weights_all = place_rows(weights_all, late)

    proj_spec = pl.BlockSpec((3, tokens, HEAD_DIM), lambda h: (0, 0, h))
    up_spec = pl.BlockSpec((tokens, HEAD_DIM), lambda h: (0, h))
    lane_spec = pl.BlockSpec((1, tokens, HEAD_DIM), lambda h: (h, 0, 0))
    state_spec = pl.BlockSpec((1, blocks, HEAD_DIM, HEAD_DIM), lambda h: (h, 0, 0, 0))
    total_spec = pl.BlockSpec((2, 1, HEAD_DIM, HEAD_DIM), lambda h: (0, h, 0, 0))
    pair_spec = pl.BlockSpec((1, blocks, BLOCK, BLOCK), lambda h: (h, 0, 0, 0))
    states = jax.ShapeDtypeStruct((heads_here, blocks, HEAD_DIM, HEAD_DIM), jnp.float32)
    key_state, query_state, totals = pl.pallas_call(
        state_kernel,
        grid=(heads_here,),
        in_specs=[proj_spec, up_spec, lane_spec, lane_spec],
        out_specs=[state_spec, state_spec, total_spec],
        out_shape=[
            states,
            states,
            jax.ShapeDtypeStruct((2, heads_here, HEAD_DIM, HEAD_DIM), jnp.bfloat16),
        ],
    )(projected, cotangent, from_start, to_end)
    parts, owners = gather_states(totals, "seq")
    weights = device_weights(device_decay, owners, "seq")
    project_gradient = pl.pallas_call(
        gradient_kernel,
        grid=(heads_here,),
        in_specs=[pl.BlockSpec(memory_space=pltpu.SMEM)]
        + [proj_spec, up_spec, lane_spec, lane_spec, pair_spec, state_spec, state_spec]
        + [total_spec] * len(parts),
        out_specs=proj_spec,
        out_shape=jax.ShapeDtypeStruct(projected.shape, jnp.bfloat16),
    )(weights, projected, cotangent, from_start, to_end, pair_weight, key_state, query_state, *parts)

    def weight_partial(gradient, owner, first, count):
        term = jnp.einsum(
            "td,ktc->kdc",
            feature_rows(owner, first, count),
            gradient,
            preferred_element_type=jnp.float32,
        ).astype(jnp.bfloat16)
        return with_layout_constraint(term, Layout(major_to_minor=(0, 1, 2)))

    def input_partial(gradient, part, of):
        columns = features.shape[1]
        tile, count = columns // 8, tokens // of
        return pl.pallas_call(
            input_kernel,
            grid=(columns // tile,),
            in_specs=[
                pl.BlockSpec((3, count, local_cols), lambda i: (0, part, 0)),
                pl.BlockSpec((3, tile, local_cols), lambda i: (0, i, 0)),
            ],
            out_specs=pl.BlockSpec((count, tile), lambda i: (0, i)),
            out_shape=jax.ShapeDtypeStruct((count, columns), jnp.bfloat16),
            cost_estimate=pl.CostEstimate(flops=1, bytes_accessed=1, transcendentals=0),
            compiler_params=pltpu.CompilerParams(vmem_limit_bytes=40 << 20),
        )(gradient, weights_all)

    input_partials, weight_gradient = scatter_rows(
        weight_partial, input_partial, project_gradient, "seq", rows
    )
    input_gradient = lax.psum_scatter(
        input_partials[0], "head", scatter_dimension=1, tiled=True
    )
    weight_gradient = weight_gradient.transpose(1, 0, 2)
    return (input_gradient, weight_gradient)


MESH = pl.DeviceIdType.MESH
PAIR = 2 * HEAD_DIM


def remote_maker(send, recv):
    def remote(index, source, target, device):
        return pltpu.make_async_remote_copy(
            src_ref=source,
            dst_ref=target,
            send_sem=send.at[index],
            recv_sem=recv.at[index],
            device_id=device,
            device_id_type=MESH,
        )

    return remote


def greet(others):
    barrier = pltpu.get_barrier_semaphore()
    for other in others:
        pl.semaphore_signal(barrier, inc=1, device_id=other, device_id_type=MESH)
    pl.semaphore_wait(barrier, len(others))


def gather_kernel(
    starts_ref, log_ref, x_ref, w_ref, up_ref, feats_out, wall_out, grads_out, swap,
    feats, wall, total, grads, upper, decay_rows, decay_cols, decays_out, decays_in, states,
    sums_out, sums_in, send, recv, local,
):
    place, head = lax.axis_index("seq"), lax.axis_index("head")
    z, core = head // 2, head % 2
    tokens, cols = x_ref.shape
    rows = w_ref.shape[1]
    half, near, chunk = tokens // 2, rows // 2, tokens // 8
    blocks = tokens // BLOCK
    x_id, y_id, far_id = (place ^ 1, head), (place ^ 2, head), (place ^ 3, head)
    next_id, last_id = (place, (head + 2) % 8), (place, (head + 6) % 8)
    twin_id = (place, head ^ 1)
    mine = pl.ds(pl.multiple_of(core * cols, cols), cols)
    remote = remote_maker(send, recv)

    own_w = pltpu.make_async_copy(w_ref, wall.at[place], local.at[0])
    own_x = pltpu.make_async_copy(x_ref, feats.at[z, :, mine], local.at[1])
    own_up = pltpu.make_async_copy(up_ref, upper, local.at[8])
    own_w.start()
    own_x.start()
    own_up.start()

    def block(step, part):
        return feats.at[(z + 4 - step) % 4, pl.ds(part * half, half), mine]

    def x_part(step, part):
        return x_ref.at[pl.ds(part * half, half)] if step == 0 else block(step, part)

    ring = [
        [remote(2 * k + p, x_part(k, p), block(k, p), next_id) for p in range(2)] for k in range(3)
    ]
    twin = [
        [remote(6 + 2 * k + p, x_part(k, p), block(k, p), twin_id) for p in range(2)]
        for k in range(4)
    ]
    low, high = pl.ds(0, near), pl.ds(near, near)
    side = [
        remote(14 + i, w_ref.at[:, part], wall.at[place, :, part], device)
        for i, (part, device) in enumerate(((high, x_id), (low, y_id), (low, x_id), (high, y_id)))
    ]

    def patch(owner, top, count, pair):
        return wall.at[owner, :, pl.ds(top, count), pl.ds(pair * PAIR, PAIR)]

    def forward(index, top, count, pair):
        first, second = patch(place ^ 2, top, count, pair), patch(place ^ 1, near + top, count, pair)
        return [remote(index, first, first, x_id), remote(index + 1, second, second, y_id)]

    part = near // 2
    far = [forward(18, 0, near, 0), forward(20, 0, part, 1), forward(22, part, part, 1)]

    def share(who):
        return pl.ds(pl.multiple_of(who * chunk, chunk), chunk)

    others = ((1, x_id), (2, y_id), (3, far_id))
    mix = [
        remote(23 + flip, feats.at[place ^ flip, share(head)], swap.at[flip - 1, share(head)], device)
        for flip, device in others
    ]

    def shared(step):
        return swap.at[:, share((head + 8 - 2 * step) % 8)]

    def half_share(who, part):
        return pl.ds(pl.multiple_of(who * chunk + part * (chunk // 2), chunk // 2), chunk // 2)

    spread = [remote(27 + k, shared(k), shared(k), next_id) for k in range(2)]
    last_half = swap.at[:, half_share((head + 4) % 8, 0)]
    spread.append(remote(29, last_half, last_half, next_id))
    spread_twin = [remote(30 + k, shared(k), shared(k), twin_id) for k in range(4)]
    direct_rows = half_share((head + 2) % 8, 1)
    direct = [
        remote(33 + flip, feats.at[place ^ flip, direct_rows], swap.at[flip - 1, direct_rows], device)
        for flip, device in others
    ]
    decays = [
        remote(36 + flip, decays_out, decays_in.at[flip - 1], device) for flip, device in others
    ]
    way = (place % 2, place // 2, place // 2)
    sums = [
        [
            remote(
                39 + 3 * pair + flip, sums_out.at[way[flip - 1], pl.ds(2 * pair, 2)],
                sums_in.at[flip - 1, pl.ds(2 * pair, 2)], device,
            )
            for flip, device in others
        ]
        for pair in range(2)
    ]

    greet((x_id, y_id, far_id, next_id, last_id, twin_id))
    ring[0][0].start()
    side[0].start()
    side[1].start()
    ring[0][1].start()
    twin[0][0].start()
    twin[0][1].start()

    def arrived(step, part):
        ring[step][part].wait_recv()
        if step < 2:
            ring[step + 1][part].start()
        twin[step + 1][part].start()

    def multiply(owner, pair, begin, top, count):
        columns = pl.ds(pair * PAIR, PAIR)

        @pl.loop(0, 6)
        def _(i):
            k, span = i // 2, pl.ds(pl.multiple_of(i % 2 * half, half), half)
            term = jnp.dot(
                feats[owner, span, pl.ds(top, count)],
                wall[owner, k, pl.ds(top, count), columns],
                preferred_element_type=jnp.float32,
            )
            total[k, span, columns] = term if begin else total[k, span, columns] + term

    def documents(b, shape, axis):
        at = lax.broadcasted_iota(jnp.int32, shape, axis) + (place * tokens + b * BLOCK)
        return sum((starts_ref[i] <= at).astype(jnp.int32) for i in range(starts_ref.shape[0]))

    def factors(b, lane):
        span = pl.ds(b * BLOCK, BLOCK)
        decay, doc = decay_cols[span, lane], documents(b, (BLOCK, HEAD_DIM), 0)
        last = decay_cols[pl.ds(b * BLOCK + BLOCK - 1, 1), lane]
        first, final = 0, 0
        top = place * tokens + b * BLOCK
        for i in range(starts_ref.shape[0]):
            first = first + (starts_ref[i] < top).astype(jnp.int32)
            final = final + (starts_ref[i] <= top + (BLOCK - 1)).astype(jnp.int32)
        from_start = jnp.where(doc == first, jnp.exp(decay), 0.0)
        to_end = jnp.where(doc == final, jnp.exp(last - decay), 0.0)
        return decay, doc, from_start, to_end

    def project(b, lane):
        span = pl.ds(b * BLOCK, BLOCK)
        point_q, point_k = total[0, span, lane], total[1, span, lane]
        gate_q, gate_k = jax.nn.sigmoid(point_q), jax.nn.sigmoid(point_k)
        queries = (point_q * gate_q * HEAD_DIM ** (-0.5)).astype(jnp.bfloat16)
        keys = (point_k * gate_k).astype(jnp.bfloat16)
        values = total[2, span, lane].astype(jnp.bfloat16)
        return (point_q, gate_q, queries), (point_k, gate_k, keys), values

    def summarize(pair):
        @pl.loop(0, 2)
        def _(i):
            h = 2 * pair + i
            lane = pl.ds(pl.multiple_of(h * HEAD_DIM, HEAD_DIM), HEAD_DIM)
            forward = jnp.zeros((HEAD_DIM, HEAD_DIM), jnp.float32)
            query_states, decays = [], []
            for b in range(blocks):
                _, _, from_start, to_end = factors(b, lane)
                (_, _, queries), (_, _, keys), values = project(b, lane)
                weighted = (keys.astype(jnp.float32) * to_end).astype(jnp.bfloat16)
                key_state = dot(weighted, values, (0, 0))
                weighted = (queries.astype(jnp.float32) * from_start).astype(jnp.bfloat16)
                upstream = upper[pl.ds(b * BLOCK, BLOCK), lane]
                query_state = dot(weighted, upstream, (0, 0))
                states[0, h, b] = key_state
                states[1, h, b] = query_state
                decay = from_start[BLOCK - 1 :]
                forward = decay * forward + key_state
                query_states.append(query_state)
                decays.append(decay)
            backward = jnp.zeros((HEAD_DIM, HEAD_DIM), jnp.float32)
            for b in reversed(range(blocks)):
                backward = decays[b] * backward + query_states[b]
            sums_out[0, h] = forward.astype(jnp.bfloat16)
            sums_out[1, h] = backward.astype(jnp.bfloat16)

        for move in sums[pair]:
            move.start()

    def differentiate(pair):
        for move in sums[pair]:
            move.wait_recv()

        @pl.loop(0, 2)
        def _(i):
            h = 2 * pair + i
            lane = pl.ds(pl.multiple_of(h * HEAD_DIM, HEAD_DIM), HEAD_DIM)
            state = jnp.zeros((HEAD_DIM, HEAD_DIM), jnp.float32)
            reverse = jnp.zeros((HEAD_DIM, HEAD_DIM), jnp.float32)
            for flip in (1, 2, 3):
                owner = place ^ flip
                share = jnp.ones((1, HEAD_DIM), jnp.float32)
                for other in (1, 2, 3):
                    if other != flip:
                        at = place ^ other
                        between = ((at > owner) & (at < place)) | ((at < owner) & (at > place))
                        share = jnp.where(between, decays_in[other - 1, pl.ds(h, 1)] * share, share)
                came = share * sums_in[flip - 1, h].astype(jnp.float32)
                state = jnp.where(owner < place, state + came, state)
                reverse = jnp.where(owner > place, reverse + came, reverse)
            decays = [factors(b, lane)[2][BLOCK - 1 :] for b in range(blocks)]
            behind = [None] * blocks
            for b in reversed(range(blocks)):
                behind[b] = reverse.astype(jnp.bfloat16)
                reverse = decays[b] * reverse + states[1, h, b]
            for b in range(blocks):
                before = state.astype(jnp.bfloat16)
                state = decays[b] * state + states[0, h, b]
                span = pl.ds(b * BLOCK, BLOCK)
                decay, doc, from_start, to_end = factors(b, lane)
                gap = jnp.minimum(
                    jnp.concatenate([decay, decay], axis=1) - decay_rows[pl.ds(h, 1), span], 0.0
                )
                rows_at = lax.broadcasted_iota(jnp.int32, (BLOCK, BLOCK), 0)
                cols_at = lax.broadcasted_iota(jnp.int32, (BLOCK, BLOCK), 1)
                same = jnp.concatenate([doc, doc], axis=1) == documents(b, (1, BLOCK), 1)
                pair_weight = jnp.where(same & (rows_at >= cols_at), jnp.exp(gap), 0.0)
                (point_q, gate_q, queries), (point_k, gate_k, keys), values = project(b, lane)
                upstream = upper[span, lane]
                query_key = (dot(queries, keys, (1, 1)) * pair_weight).astype(jnp.bfloat16)
                value_score = (dot(upstream, values, (1, 1)) * pair_weight).astype(jnp.bfloat16)
                query_gradient = dot(value_score, keys, (1, 0)) + from_start * dot(
                    upstream, before, (1, 1)
                )
                key_gradient = dot(value_score, queries, (0, 0)) + to_end * dot(
                    values, behind[b], (1, 1)
                )
                value_gradient = dot(query_key, upstream, (0, 0)) + to_end * dot(
                    keys, behind[b], (1, 0)
                )
                slope_q = gate_q * (1.0 + point_q * (1.0 - gate_q)) * HEAD_DIM ** (-0.5)
                slope_k = gate_k * (1.0 + point_k * (1.0 - gate_k))
                grads[0, span, lane] = (query_gradient * slope_q).astype(jnp.bfloat16)
                grads[1, span, lane] = (key_gradient * slope_k).astype(jnp.bfloat16)
                grads[2, span, lane] = value_gradient.astype(jnp.bfloat16)

    def prepare():
        before = lax.broadcasted_iota(jnp.int32, (BLOCK, BLOCK), 0) <= lax.broadcasted_iota(
            jnp.int32, (BLOCK, BLOCK), 1
        )
        triangle = before.astype(jnp.float32)
        heads = log_ref.shape[0]
        for b in range(tokens // BLOCK):
            span = pl.ds(b * BLOCK, BLOCK)
            sums_of = lax.dot_general(
                log_ref[:, span], triangle, (((1,), (0,)), ((), ())),
                precision=lax.Precision.HIGHEST, preferred_element_type=jnp.float32,
            )
            decay_rows[pl.ds(0, heads), span] = sums_of
            for h in range(heads):
                wide = jnp.broadcast_to(sums_of[h : h + 1], (HEAD_DIM, BLOCK))
                decay_cols[span, pl.ds(h * HEAD_DIM, HEAD_DIM)] = wide.T
        decays_out[...] = jnp.ones_like(decays_out)
        for h in range(heads):
            product = jnp.ones((1, HEAD_DIM), jnp.float32)
            for b in range(tokens // BLOCK):
                from_start = factors(b, pl.ds(h * HEAD_DIM, HEAD_DIM))[2]
                product = product * from_start[BLOCK - 1 :]
            decays_out[pl.ds(h, 1)] = product

    prepare()
    for move in decays:
        move.start()
    arrived(0, 0)
    arrived(0, 1)
    arrived(1, 0)
    side[0].wait_recv()
    side[1].wait_recv()
    side[2].start()
    side[3].start()
    arrived(1, 1)
    own_w.wait()
    own_x.wait()
    own_up.wait()
    arrived(2, 0)
    arrived(2, 1)
    for pair in twin:
        for move in pair:
            move.wait_recv()
    for move in (*mix, *far[0], *far[1]):
        move.start()
    feats_copy = pltpu.make_async_copy(feats.at[place], feats_out, local.at[2])
    feats_copy.start()
    multiply(place, 0, True, 0, rows)
    multiply(place, 1, True, 0, rows)
    side[2].wait_recv()
    side[3].wait_recv()
    multiply(place ^ 1, 0, False, 0, rows)
    for move in mix:
        move.wait_recv()
    spread[0].start()
    spread_twin[0].start()
    multiply(place ^ 2, 0, False, 0, rows)
    multiply(place ^ 1, 1, False, 0, rows)
    multiply(place ^ 2, 1, False, 0, rows)
    near_copies = [
        pltpu.make_async_copy(wall.at[place ^ f], wall_out.at[place ^ f], local.at[3 + f])
        for f in range(3)
    ]
    for move in near_copies:
        move.start()
    for move in decays:
        move.wait_recv()
    for move in far[0]:
        move.wait_recv()
    multiply(place ^ 3, 0, False, 0, rows)
    summarize(0)
    for move in far[2]:
        move.start()
    spread[0].wait_recv()
    spread[1].start()
    spread_twin[1].start()
    for move in far[1]:
        move.wait_recv()
    multiply(place ^ 3, 1, False, 0, part)
    multiply(place ^ 3, 1, False, near, part)
    differentiate(0)
    spread[1].wait_recv()
    spread[2].start()
    spread_twin[2].start()
    for move in far[2]:
        move.wait_recv()
    multiply(place ^ 3, 1, False, part, part)
    multiply(place ^ 3, 1, False, near + part, part)
    summarize(1)
    for move in direct:
        move.start()
    far_copy = pltpu.make_async_copy(wall.at[place ^ 3], wall_out.at[place ^ 3], local.at[6])
    far_copy.start()
    differentiate(1)
    grads_copy = pltpu.make_async_copy(grads, grads_out, local.at[7])
    grads_copy.start()
    spread[2].wait_recv()
    for move in direct:
        move.wait_recv()
    spread_twin[3].start()
    for move in spread_twin:
        move.wait_recv()
    for move in (feats_copy, *near_copies, far_copy, grads_copy):
        move.wait()
    for moves in (*ring, *twin, side, *far, mix, spread, spread_twin, direct, decays, *sums):
        for move in moves:
            move.wait_send()


def gather_call(starts, log_decay, inputs, weights, cotangent):
    (tokens, cols), (_, rows, local_cols) = inputs.shape, weights.shape
    bf16, f32 = jnp.bfloat16, jnp.float32
    blocks = tokens // BLOCK
    shapes = [
        ((tokens, 2 * cols), bf16),
        ((4, 3, rows, local_cols), bf16),
        ((3, tokens, local_cols), bf16),
        ((3, tokens, 2 * cols), bf16),
    ]
    buffers = [
        ((4, tokens, 2 * cols), bf16),
        ((4, 3, rows, local_cols), bf16),
        ((3, tokens, local_cols), f32),
        ((3, tokens, local_cols), bf16),
        ((tokens, local_cols), bf16),
        ((8, tokens), f32),
        ((tokens, local_cols), f32),
        ((8, HEAD_DIM), f32),
        ((3, 8, HEAD_DIM), f32),
        ((2, 4, blocks, HEAD_DIM, HEAD_DIM), f32),
        ((2, 4, HEAD_DIM, HEAD_DIM), bf16),
        ((3, 4, HEAD_DIM, HEAD_DIM), bf16),
    ]
    anywhere = pl.BlockSpec(memory_space=pl.ANY)
    return pl.pallas_call(
        gather_kernel,
        in_specs=[pl.BlockSpec(memory_space=pltpu.SMEM), pl.BlockSpec(memory_space=pltpu.VMEM)]
        + [anywhere] * 3,
        out_specs=[anywhere] * 4,
        out_shape=[jax.ShapeDtypeStruct(*shape) for shape in shapes],
        scratch_shapes=[pltpu.VMEM(*shape) for shape in buffers]
        + [
            pltpu.SemaphoreType.DMA((46,)),
            pltpu.SemaphoreType.DMA((46,)),
            pltpu.SemaphoreType.DMA((9,)),
        ],
        compiler_params=pltpu.CompilerParams(
            collective_id=0, has_side_effects=True, vmem_limit_bytes=58 << 20
        ),
        name="gather",
    )(starts, log_decay, inputs, weights, cotangent)


def finish_kernel(
    grad_ref, feats_ref, wall_ref, swap_ref, input_out, weight_out,
    grads, tokens_buf, rows_buf, total, keep, twin_out, twin_in, ring_out, ring_in,
    send, recv, local,
):
    place, head = lax.axis_index("seq"), lax.axis_index("head")
    z, core = head // 2, head % 2
    _, tokens, local_cols = grad_ref.shape
    rows, cols = total.shape[1], keep.shape[1]
    half, chunk = tokens // 2, tokens // 8
    x_id, y_id = (place ^ 1, head), (place ^ 2, head)
    next_id, last_id = (place, (head + 2) % 8), (place, (head + 6) % 8)
    twin_id = (place, head ^ 1)
    remote = remote_maker(send, recv)
    low, high = pl.ds(0, half), pl.ds(half, half)

    def fetch_rows(turn, part):
        owner = (z + 7 - turn) % 4
        side = pl.multiple_of((core if part else 1 - core) * cols, cols)
        return pltpu.make_async_copy(
            wall_ref.at[owner, :, pl.ds(side, cols)], rows_buf.at[part], local.at[part]
        )

    def fetch_tokens(flip):
        source = feats_ref if flip == 0 else swap_ref.at[flip - 1]
        return pltpu.make_async_copy(source, tokens_buf.at[flip % 2], local.at[2 + flip])

    own = pltpu.make_async_copy(grad_ref, grads.at[0], local.at[6])
    own.start()
    fetched_rows = [fetch_rows(0, 0), fetch_rows(0, 1)]
    for move in fetched_rows:
        move.start()
    fetched = [fetch_tokens(0), fetch_tokens(1)]
    for move in fetched:
        move.start()
    side = [
        remote(i, grad_ref.at[:, part], grads.at[flip, :, part], device)
        for i, (part, flip, device) in enumerate(
            ((high, 1, x_id), (low, 2, y_id), (low, 1, x_id), (high, 2, y_id))
        )
    ]
    far = [
        remote(4, grads.at[2, :, low], grads.at[3, :, low], x_id),
        remote(5, grads.at[1, :, high], grads.at[3, :, high], y_id),
    ]
    twin = [remote(6 + k, twin_out.at[k % 2], twin_in.at[k], twin_id) for k in range(4)]
    ring = [
        [
            remote(10 + 2 * k + p, ring_out.at[k, part], ring_in.at[k, part], next_id)
            for p, part in enumerate((low, high))
        ]
        for k in range(3)
    ]
    greet((x_id, y_id, next_id, last_id, twin_id))
    for move in side:
        move.start()
    own.wait()

    def back(part, target):
        fetched_rows[part].wait()

        @pl.loop(0, 4)
        def _(i):
            span = pl.ds(pl.multiple_of(i * (tokens // 4), tokens // 4), tokens // 4)
            term = None
            for k in range(3):
                piece = dot(grads[0, k, span, :], rows_buf[part, k], (1, 1))
                term = piece if term is None else term + piece
            target[span, :] = term.astype(target.dtype)

    def input_block(turn):
        if turn >= 2:
            twin[turn - 2].wait_send()
        back(0, twin_out.at[turn % 2])
        twin[turn].start()
        if turn < 3:
            fetched_rows[0] = fetch_rows(turn + 1, 0)
            fetched_rows[0].start()
        back(1, keep)
        if turn < 3:
            fetched_rows[1] = fetch_rows(turn + 1, 1)
            fetched_rows[1].start()
        twin[turn].wait_recv()

    def pass_on(turn):
        for p, part in enumerate((low, high)):
            if turn > 0:
                ring[turn - 1][p].wait_recv()

            @pl.loop(0, 2)
            def _(i):
                quarter = tokens // 4
                span = pl.ds(pl.multiple_of(p * half + i * quarter, quarter), quarter)
                sum_ = keep[span, :] + twin_in[turn, span, :].astype(jnp.float32)
                if turn > 0:
                    sum_ = sum_ + ring_in[turn - 1, span, :].astype(jnp.float32)
                target = ring_out.at[turn] if turn < 3 else twin_out.at[0]
                target[span, :] = sum_.astype(jnp.bfloat16)

            if turn < 3:
                ring[turn][p].start()

    def weight_block(flip):
        slot = flip % 2
        fetched[slot].wait()

        @pl.loop(0, rows // BLOCK)
        def _(i):
            span = pl.ds(pl.multiple_of(i * BLOCK, BLOCK), BLOCK)
            turned = tokens_buf[slot, :, span].T
            for k in range(3):
                term = jnp.dot(turned, grads[flip, k], preferred_element_type=jnp.float32)
                total[k, span, :] = term if flip == 0 else total[k, span, :] + term

        if flip < 2:
            fetched[slot] = fetch_tokens(flip + 2)
            fetched[slot].start()

    input_block(0)
    pass_on(0)
    input_block(1)
    weight_block(0)
    side[0].wait_recv()
    far[1].start()
    side[1].wait_recv()
    far[0].start()
    pass_on(1)
    input_block(2)
    side[2].wait_recv()
    weight_block(1)
    pass_on(2)
    input_block(3)
    side[3].wait_recv()
    weight_block(2)
    for move in far:
        move.wait_recv()
    weight_block(3)
    stores = []
    for part in range(2):
        span = pl.ds(part * (rows // 2), rows // 2)
        for k in range(3):
            rows_buf[part, k] = total[k, span, :].astype(jnp.bfloat16)
        stores.append(
            pltpu.make_async_copy(rows_buf.at[part], weight_out.at[:, span], local.at[part])
        )
        stores[-1].start()
    twin[2].wait_send()
    twin[3].wait_send()
    pass_on(3)
    stores.append(pltpu.make_async_copy(twin_out.at[0], input_out, local.at[6]))
    stores[-1].start()
    for move in stores:
        move.wait()
    for move in (*side, *far, *ring[0], *ring[1], *ring[2]):
        move.wait_send()


def finish_call(gradient, feats, wall, swap):
    _, tokens, local_cols = gradient.shape
    rows = wall.shape[2]
    cols = rows // 2
    bf16, f32 = jnp.bfloat16, jnp.float32
    anywhere = pl.BlockSpec(memory_space=pl.ANY)
    return pl.pallas_call(
        finish_kernel,
        in_specs=[anywhere] * 4,
        out_specs=[anywhere] * 2,
        out_shape=[
            jax.ShapeDtypeStruct((tokens, cols), bf16),
            jax.ShapeDtypeStruct((3, rows, local_cols), bf16),
        ],
        scratch_shapes=[
            pltpu.VMEM((4, 3, tokens, local_cols), bf16),
            pltpu.VMEM((2, tokens, rows), bf16),
            pltpu.VMEM((2, 3, cols, local_cols), bf16),
            pltpu.VMEM((3, rows, local_cols), f32),
            pltpu.VMEM((tokens, cols), f32),
            pltpu.VMEM((2, tokens, cols), bf16),
            pltpu.VMEM((4, tokens, cols), bf16),
            pltpu.VMEM((3, tokens, cols), bf16),
            pltpu.VMEM((3, tokens, cols), bf16),
            pltpu.SemaphoreType.DMA((16,)),
            pltpu.SemaphoreType.DMA((16,)),
            pltpu.SemaphoreType.DMA((7,)),
        ],
        compiler_params=pltpu.CompilerParams(
            collective_id=1, has_side_effects=True, vmem_limit_bytes=60 << 20
        ),
        name="finish",
    )(gradient, feats, wall, swap)


def fast_body(inputs, projection, cotangent, log_decay, document_starts):
    feats, wall, gradient, swap = gather_call(
        document_starts, log_decay, inputs, projection.transpose(1, 0, 2), cotangent
    )
    input_gradient, weight_gradient = finish_call(gradient, feats, wall, swap)
    return (input_gradient, weight_gradient.transpose(1, 0, 2))


def solution(mesh):
    fast = (mesh.shape["seq"], mesh.shape["head"]) == (4, 8)
    placed = (P("seq", "head"), P("seq", None, "head"), P("seq", "head"), P("head", "seq"), P())
    return jax.shard_map(
        fast_body if fast else general_body,
        mesh=mesh,
        in_specs=placed,
        out_specs=(P("seq", "head"), P("seq", None, "head")),
        check_vma=False,
    )
```

```python
import jax
import jax.numpy as jnp
from jax import lax
from jax.experimental import pallas as pl
from jax.experimental.layout import Layout, with_layout_constraint
from jax.experimental.pallas import tpu as pltpu
from jax.sharding import PartitionSpec as P

HEAD_DIM = 128
BLOCK = 256


def hop(array, axis, flip):
    return lax.ppermute(array, axis, [(i, i ^ flip) for i in range(lax.axis_size(axis))])


def gather_states(packed, axis):
    length, place = (lax.axis_size(axis), lax.axis_index(axis))
    if length != 4:
        whole = lax.all_gather(packed, axis)
        return [whole[k] for k in range(length)], jnp.arange(length, dtype=jnp.int32)
    parts = [packed] + [hop(packed, axis, flip) for flip in range(1, length)]
    return parts, place ^ jnp.arange(length, dtype=jnp.int32)


def device_weights(device_decay, owners, axis):
    length, place = (lax.axis_size(axis), lax.axis_index(axis))
    if length == 4:
        slab = jnp.broadcast_to(device_decay[:, None], (device_decay.shape[0], HEAD_DIM))
        hops = [slab] + [hop(slab, axis, flip) for flip in range(1, length)]
        arrived = jnp.stack([part[:, 0] for part in hops])
        mine = owners[None, :] == jnp.arange(length, dtype=jnp.int32)[:, None]
        decays = jnp.sum(jnp.where(mine[:, :, None], arrived[None], 0.0), axis=1)
    else:
        decays = lax.all_gather(device_decay, axis)
    at, other = owners[:, None], jnp.arange(length, dtype=jnp.int32)[None]
    before = (other > at) & (other < place)
    after = (other < at) & (other > place)
    weights = []
    for between, counts in ((before, owners < place), (after, owners > place)):
        product = jnp.prod(jnp.where(between[:, :, None], decays[None], 1.0), axis=1)
        weights.append(jnp.where(counts[:, None], product, 0.0))
    return jnp.stack(weights)


def gather_rows(part, axis):
    length, place, rows = (lax.axis_size(axis), lax.axis_index(axis), part.shape[1])
    if length != 4:
        whole = lax.all_gather(part, axis, axis=1, tiled=True)
        return [(0, 0, whole)]
    half = rows // 2
    low, high = part[:, :half], part[:, half:]
    x_high = hop(high, axis, 1)
    y_low = hop(low, axis, 2)
    x_low = hop(low, axis, 1)
    y_high = hop(high, axis, 2)
    d_low = hop(y_low, axis, 1)
    d_high = hop(x_high, axis, 2)
    return [
        (place, 0, low),
        (place, half, high),
        (place ^ 1, half, x_high),
        (place ^ 2, 0, y_low),
        (place ^ 1, 0, x_low),
        (place ^ 2, half, y_high),
        (place ^ 3, 0, d_low),
        (place ^ 3, half, d_high),
    ]


def scatter_rows(partial, between, source, axis, rows):
    length, place = (lax.axis_size(axis), lax.axis_index(axis))
    if length != 4:
        whole = partial(source, 0, 0, rows * length)
        return [between(source, 0, 1)], lax.psum_scatter(whole, axis, scatter_dimension=1, tiled=True)
    half = rows // 2

    def add(*terms):
        return sum(term.astype(jnp.float32) for term in terms).astype(jnp.bfloat16)

    far_low, far_high = partial(source, place ^ 3, 0, half), partial(source, place ^ 3, half, half)
    source, far_low, far_high = lax.optimization_barrier((source, far_low, far_high))
    far_low, far_high = hop(far_low, axis, 1), hop(far_high, axis, 2)
    beside = between(source, 0, 1)
    source, beside = lax.optimization_barrier((source, beside))
    x_low, y_high = partial(source, place ^ 1, 0, half), partial(source, place ^ 2, half, half)
    source, x_low, y_high = lax.optimization_barrier((source, x_low, y_high))
    x_low, y_high = hop(x_low, axis, 1), hop(y_high, axis, 2)
    x_high = hop(add(partial(source, place ^ 1, half, half), far_high), axis, 1)
    y_low = hop(add(partial(source, place ^ 2, 0, half), far_low), axis, 2)
    own_low, own_high = partial(source, place, 0, half), partial(source, place, half, half)
    whole = jnp.concatenate([add(own_low, x_low, y_low), add(own_high, x_high, y_high)], axis=1)
    return [beside], whole


def running_sum(values):
    inside = jnp.arange(values.shape[-1], dtype=jnp.int32)
    triangle = (inside[:, None] <= inside[None, :]).astype(jnp.float32)
    return jnp.einsum("hbu,ut->hbt", values, triangle, precision=lax.Precision.HIGHEST)


def block_factors(decay_sum, doc_index, doc_begin):
    inside = jnp.arange(doc_index.shape[-1], dtype=jnp.int32)
    causal = inside[:, None] >= inside[None, :]
    same_doc = (doc_index[:, :, None] == doc_index[:, None, :]) & causal[None]
    spread = jnp.minimum(decay_sum[..., :, None] - decay_sum[..., None, :], 0.0)
    pair_weight = jnp.where(same_doc[None], jnp.exp(spread), 0.0)
    to_end = jnp.where(
        (doc_index == doc_index[:, -1:])[None], jnp.exp(decay_sum[..., -1:] - decay_sum), 0.0
    )
    began_flag = doc_index == doc_index[:, :1] - doc_begin[:, :1]
    from_start = jnp.where(began_flag[None], jnp.exp(decay_sum), 0.0)
    return (pair_weight, to_end, from_start, from_start[..., -1])


def dot(left, right, contract):
    return lax.dot_general(
        left, right, ((contract[:1], contract[1:]), ((), ())), preferred_element_type=jnp.float32
    )


def projections(proj_ref, span):
    point_q, point_k = proj_ref[0, span], proj_ref[1, span]
    gate_q, gate_k = jax.nn.sigmoid(point_q), jax.nn.sigmoid(point_k)
    queries = (point_q * gate_q * HEAD_DIM ** (-0.5)).astype(jnp.bfloat16)
    keys = (point_k * gate_k).astype(jnp.bfloat16)
    values = proj_ref[2, span].astype(jnp.bfloat16)
    return (point_q, gate_q, queries), (point_k, gate_k, keys), values


def state_kernel(proj_ref, up_ref, start_ref, end_ref, key_ref, query_ref, total_ref):
    blocks = key_ref.shape[1]
    forward = jnp.zeros((HEAD_DIM, HEAD_DIM), jnp.float32)
    query_states, decays = [], []
    for b in range(blocks):
        span = pl.ds(b * BLOCK, BLOCK)
        (_, _, queries), (_, _, keys), values = projections(proj_ref, span)
        keys_weighted = (keys.astype(jnp.float32) * end_ref[0, span]).astype(jnp.bfloat16)
        queries_weighted = (queries.astype(jnp.float32) * start_ref[0, span]).astype(jnp.bfloat16)
        key_state = dot(keys_weighted, values, (0, 0))
        query_state = dot(queries_weighted, up_ref[span], (0, 0))
        key_ref[0, b] = key_state
        query_ref[0, b] = query_state
        decay = start_ref[0, pl.ds(b * BLOCK + BLOCK - 1, 1)]
        forward = decay * forward + key_state
        query_states.append(query_state)
        decays.append(decay)
    backward = jnp.zeros((HEAD_DIM, HEAD_DIM), jnp.float32)
    for b in reversed(range(blocks)):
        backward = decays[b] * backward + query_states[b]
    total_ref[0, 0] = forward.astype(jnp.bfloat16)
    total_ref[1, 0] = backward.astype(jnp.bfloat16)


def gradient_kernel(
    weight_ref, proj_ref, up_ref, start_ref, end_ref, pair_ref, key_ref, query_ref, *rest
):
    totals, out_ref = rest[:-1], rest[-1]
    blocks = key_ref.shape[1]
    head = pl.program_id(0)
    state = jnp.zeros((HEAD_DIM, HEAD_DIM), jnp.float32)
    reverse = jnp.zeros((HEAD_DIM, HEAD_DIM), jnp.float32)
    for k, total in enumerate(totals):
        state = state + weight_ref[0, k, head] * total[0, 0].astype(jnp.float32)
        reverse = reverse + weight_ref[1, k, head] * total[1, 0].astype(jnp.float32)
    decays = [start_ref[0, pl.ds(b * BLOCK + BLOCK - 1, 1)] for b in range(blocks)]
    after = [None] * blocks
    for b in reversed(range(blocks)):
        after[b] = reverse.astype(jnp.bfloat16)
        reverse = decays[b] * reverse + query_ref[0, b]
    for b in range(blocks):
        before = state.astype(jnp.bfloat16)
        state = decays[b] * state + key_ref[0, b]
        span = pl.ds(b * BLOCK, BLOCK)
        (point_q, gate_q, queries), (point_k, gate_k, keys), values = projections(proj_ref, span)
        upstream = up_ref[span]
        from_start, to_end, pair = start_ref[0, span], end_ref[0, span], pair_ref[0, b]
        query_key = (dot(queries, keys, (1, 1)) * pair).astype(jnp.bfloat16)
        value_score = (dot(upstream, values, (1, 1)) * pair).astype(jnp.bfloat16)
        query_gradient = dot(value_score, keys, (1, 0)) + from_start * dot(
            upstream, before, (1, 1)
        )
        key_gradient = dot(value_score, queries, (0, 0)) + to_end * dot(values, after[b], (1, 1))
        value_gradient = dot(query_key, upstream, (0, 0)) + to_end * dot(keys, after[b], (1, 0))
        slope_q = gate_q * (1.0 + point_q * (1.0 - gate_q)) * HEAD_DIM ** (-0.5)
        slope_k = gate_k * (1.0 + point_k * (1.0 - gate_k))
        out_ref[0, span] = (query_gradient * slope_q).astype(jnp.bfloat16)
        out_ref[1, span] = (key_gradient * slope_k).astype(jnp.bfloat16)
        out_ref[2, span] = value_gradient.astype(jnp.bfloat16)


def input_kernel(gradient_ref, weight_ref, out_ref):
    for first in range(0, out_ref.shape[0], BLOCK):
        span = pl.ds(first, BLOCK)
        total = dot(gradient_ref[0, span], weight_ref[0], (1, 1))
        for k in (1, 2):
            total = total + dot(gradient_ref[k, span], weight_ref[k], (1, 1))
        out_ref[span] = total.astype(jnp.bfloat16)


def general_body(inputs, projection, cotangent, log_decay, document_starts):
    tokens = inputs.shape[0]
    heads_here = log_decay.shape[0]
    local_cols = cotangent.shape[1]
    blocks = tokens // BLOCK
    features = lax.all_gather(inputs, "head", axis=1, tiled=True)
    rows = projection.shape[0]
    blocks_w = gather_rows(projection.transpose(1, 0, 2), "seq")

    def feature_rows(owner, first, count):
        return lax.dynamic_slice_in_dim(features, owner * rows + first, count, axis=1)

    offset = lax.axis_index("seq") * tokens
    positions = offset + jnp.arange(tokens, dtype=jnp.int32)
    doc_index = (
        jnp.sum((document_starts[None, :] <= positions[:, None]).astype(jnp.int32), axis=1) - 1
    )
    doc_begin = jnp.any(document_starts[None, :] == positions[:, None], axis=1).astype(jnp.int32)
    decay_sum = running_sum(log_decay.reshape(heads_here, blocks, BLOCK))
    pair_weight, to_end, from_start, block_decay = block_factors(
        decay_sum, doc_index.reshape(blocks, BLOCK), doc_begin.reshape(blocks, BLOCK)
    )
    lanes = (heads_here, tokens, HEAD_DIM)
    to_end = jnp.broadcast_to(to_end.reshape(heads_here, tokens)[..., None], lanes)
    from_start = jnp.broadcast_to(from_start.reshape(heads_here, tokens)[..., None], lanes)
    device_decay = jnp.prod(block_decay, axis=1)

    zero = jnp.zeros((), jnp.bfloat16)
    if len(blocks_w) > 2:
        owner, first, block = blocks_w[2]
        zero, block = lax.optimization_barrier((zero, block))
        blocks_w[2] = (owner, first, block)
    weights_all = jnp.broadcast_to(zero, (3, features.shape[1], local_cols))

    def place_rows(whole, some):
        for owner, first, block in some:
            whole = lax.dynamic_update_slice_in_dim(whole, block, owner * rows + first, axis=1)
        return whole

    early, late = blocks_w[:6], blocks_w[6:]
    weights_all = place_rows(weights_all, early)
    features, weights_all, from_start, to_end, pair_weight = lax.optimization_barrier(
        (features, weights_all, from_start, to_end, pair_weight)
    )
    projected = None
    for k, (owner, first, block) in enumerate(blocks_w):
        piece = jnp.einsum(
            "td,kdc->ktc",
            feature_rows(owner, first, block.shape[1]),
            block,
            preferred_element_type=jnp.float32,
        )
        projected = piece if projected is None else lax.optimization_barrier(projected) + piece
        if k == min(5, len(blocks_w) - 1):
            projected, device_decay = lax.optimization_barrier((projected, device_decay))
    weights_all = place_rows(weights_all, late)

    proj_spec = pl.BlockSpec((3, tokens, HEAD_DIM), lambda h: (0, 0, h))
    up_spec = pl.BlockSpec((tokens, HEAD_DIM), lambda h: (0, h))
    lane_spec = pl.BlockSpec((1, tokens, HEAD_DIM), lambda h: (h, 0, 0))
    state_spec = pl.BlockSpec((1, blocks, HEAD_DIM, HEAD_DIM), lambda h: (h, 0, 0, 0))
    total_spec = pl.BlockSpec((2, 1, HEAD_DIM, HEAD_DIM), lambda h: (0, h, 0, 0))
    pair_spec = pl.BlockSpec((1, blocks, BLOCK, BLOCK), lambda h: (h, 0, 0, 0))
    states = jax.ShapeDtypeStruct((heads_here, blocks, HEAD_DIM, HEAD_DIM), jnp.float32)
    key_state, query_state, totals = pl.pallas_call(
        state_kernel,
        grid=(heads_here,),
        in_specs=[proj_spec, up_spec, lane_spec, lane_spec],
        out_specs=[state_spec, state_spec, total_spec],
        out_shape=[
            states,
            states,
            jax.ShapeDtypeStruct((2, heads_here, HEAD_DIM, HEAD_DIM), jnp.bfloat16),
        ],
    )(projected, cotangent, from_start, to_end)
    parts, owners = gather_states(totals, "seq")
    weights = device_weights(device_decay, owners, "seq")
    project_gradient = pl.pallas_call(
        gradient_kernel,
        grid=(heads_here,),
        in_specs=[pl.BlockSpec(memory_space=pltpu.SMEM)]
        + [proj_spec, up_spec, lane_spec, lane_spec, pair_spec, state_spec, state_spec]
        + [total_spec] * len(parts),
        out_specs=proj_spec,
        out_shape=jax.ShapeDtypeStruct(projected.shape, jnp.bfloat16),
    )(weights, projected, cotangent, from_start, to_end, pair_weight, key_state, query_state, *parts)

    def weight_partial(gradient, owner, first, count):
        term = jnp.einsum(
            "td,ktc->kdc",
            feature_rows(owner, first, count),
            gradient,
            preferred_element_type=jnp.float32,
        ).astype(jnp.bfloat16)
        return with_layout_constraint(term, Layout(major_to_minor=(0, 1, 2)))

    def input_partial(gradient, part, of):
        columns = features.shape[1]
        tile, count = columns // 8, tokens // of
        return pl.pallas_call(
            input_kernel,
            grid=(columns // tile,),
            in_specs=[
                pl.BlockSpec((3, count, local_cols), lambda i: (0, part, 0)),
                pl.BlockSpec((3, tile, local_cols), lambda i: (0, i, 0)),
            ],
            out_specs=pl.BlockSpec((count, tile), lambda i: (0, i)),
            out_shape=jax.ShapeDtypeStruct((count, columns), jnp.bfloat16),
            cost_estimate=pl.CostEstimate(flops=1, bytes_accessed=1, transcendentals=0),
            compiler_params=pltpu.CompilerParams(vmem_limit_bytes=40 << 20),
        )(gradient, weights_all)

    input_partials, weight_gradient = scatter_rows(
        weight_partial, input_partial, project_gradient, "seq", rows
    )
    input_gradient = lax.psum_scatter(
        input_partials[0], "head", scatter_dimension=1, tiled=True
    )
    weight_gradient = weight_gradient.transpose(1, 0, 2)
    return (input_gradient, weight_gradient)


MESH = pl.DeviceIdType.MESH
PAIR = 2 * HEAD_DIM


def remote_maker(send, recv):
    def remote(index, source, target, device):
        return pltpu.make_async_remote_copy(
            src_ref=source,
            dst_ref=target,
            send_sem=send.at[index],
            recv_sem=recv.at[index],
            device_id=device,
            device_id_type=MESH,
        )

    return remote


def greet(others):
    barrier = pltpu.get_barrier_semaphore()
    for other in others:
        pl.semaphore_signal(barrier, inc=1, device_id=other, device_id_type=MESH)
    pl.semaphore_wait(barrier, len(others))


def gather_kernel(
    starts_ref, log_ref, x_ref, w_ref, up_ref, feats_out, wall_out, grads_out, swap,
    feats, wall, total, grads, upper, decay_rows, decay_cols, decays_out, decays_in, states,
    sums_out, sums_in, send, recv, local,
):
    place, head = lax.axis_index("seq"), lax.axis_index("head")
    z, core = head // 2, head % 2
    tokens, cols = x_ref.shape
    rows = w_ref.shape[1]
    half, near, chunk = tokens // 2, rows // 2, tokens // 8
    blocks = tokens // BLOCK
    x_id, y_id, far_id = (place ^ 1, head), (place ^ 2, head), (place ^ 3, head)
    next_id, last_id = (place, (head + 2) % 8), (place, (head + 6) % 8)
    twin_id = (place, head ^ 1)
    mine = pl.ds(pl.multiple_of(core * cols, cols), cols)
    remote = remote_maker(send, recv)

    own_w = pltpu.make_async_copy(w_ref, wall.at[place], local.at[0])
    own_x = pltpu.make_async_copy(x_ref, feats.at[z, :, mine], local.at[1])
    own_up = pltpu.make_async_copy(up_ref, upper, local.at[8])
    own_w.start()
    own_x.start()
    own_up.start()

    def block(step, part):
        return feats.at[(z + 4 - step) % 4, pl.ds(part * half, half), mine]

    def x_part(step, part):
        return x_ref.at[pl.ds(part * half, half)] if step == 0 else block(step, part)

    ring = [
        [remote(2 * k + p, x_part(k, p), block(k, p), next_id) for p in range(2)] for k in range(3)
    ]
    twin = [
        [remote(6 + 2 * k + p, x_part(k, p), block(k, p), twin_id) for p in range(2)]
        for k in range(4)
    ]
    low, high = pl.ds(0, near), pl.ds(near, near)
    side = [
        remote(14 + i, w_ref.at[:, part], wall.at[place, :, part], device)
        for i, (part, device) in enumerate(((high, x_id), (low, y_id), (low, x_id), (high, y_id)))
    ]

    def patch(owner, top, count, pair):
        return wall.at[owner, :, pl.ds(top, count), pl.ds(pair * PAIR, PAIR)]

    def forward(index, top, count, pair):
        first, second = patch(place ^ 2, top, count, pair), patch(place ^ 1, near + top, count, pair)
        return [remote(index, first, first, x_id), remote(index + 1, second, second, y_id)]

    part = near // 2
    filler = near // 3
    far = [
        forward(18, 0, filler, 0),
        forward(20, filler, near - filler, 0),
        forward(22, 0, part, 1),
        forward(24, part, part, 1),
    ]

    def share(who):
        return pl.ds(pl.multiple_of(who * chunk, chunk), chunk)

    others = ((1, x_id), (2, y_id), (3, far_id))
    mix = [
        remote(25 + flip, feats.at[place ^ flip, share(head)], swap.at[flip - 1, share(head)], device)
        for flip, device in others
    ]

    def shared(step):
        return swap.at[:, share((head + 8 - 2 * step) % 8)]

    ringed = chunk // 4

    def ring_rows(step):
        top = pl.multiple_of((head + 8 - 2 * step) % 8 * chunk, chunk)
        return pl.ds(top, chunk if step < 2 else ringed)

    spread = [
        [
            remote(
                29 + 3 * k + flip, swap.at[flip, ring_rows(k)], swap.at[flip, ring_rows(k)], next_id
            )
            for flip in range(3)
        ]
        for k in range(3)
    ]
    spread_twin = [remote(38 + k, shared(k), shared(k), twin_id) for k in range(4)]
    direct_rows = pl.ds(
        pl.multiple_of((head + 2) % 8 * chunk + ringed, chunk // 8), chunk - ringed
    )
    direct = [
        remote(41 + flip, feats.at[place ^ flip, direct_rows], swap.at[flip - 1, direct_rows], device)
        for flip, device in others
    ]
    decays = [
        remote(44 + flip, decays_out, decays_in.at[flip - 1], device) for flip, device in others
    ]
    way = (place % 2, place // 2, place // 2)
    sums = [
        [
            remote(
                47 + 3 * pair + flip, sums_out.at[way[flip - 1], pl.ds(2 * pair, 2)],
                sums_in.at[flip - 1, pl.ds(2 * pair, 2)], device,
            )
            for flip, device in others
        ]
        for pair in range(2)
    ]

    greet((x_id, y_id, far_id, next_id, last_id, twin_id))
    ring[0][0].start()
    side[0].start()
    side[1].start()
    ring[0][1].start()
    twin[0][0].start()
    twin[0][1].start()

    def arrived(step, part):
        ring[step][part].wait_recv()
        if step < 2:
            ring[step + 1][part].start()
        twin[step + 1][part].start()

    def multiply(owner, pair, begin, top, count):
        columns = pl.ds(pair * PAIR, PAIR)

        @pl.loop(0, 6)
        def _(i):
            k, span = i // 2, pl.ds(pl.multiple_of(i % 2 * half, half), half)
            term = jnp.dot(
                feats[owner, span, pl.ds(top, count)],
                wall[owner, k, pl.ds(top, count), columns],
                preferred_element_type=jnp.float32,
            )
            total[k, span, columns] = term if begin else total[k, span, columns] + term

    def documents(b, shape, axis):
        at = lax.broadcasted_iota(jnp.int32, shape, axis) + (place * tokens + b * BLOCK)
        return sum((starts_ref[i] <= at).astype(jnp.int32) for i in range(starts_ref.shape[0]))

    def factors(b, lane):
        span = pl.ds(b * BLOCK, BLOCK)
        decay, doc = decay_cols[span, lane], documents(b, (BLOCK, HEAD_DIM), 0)
        last = decay_cols[pl.ds(b * BLOCK + BLOCK - 1, 1), lane]
        first, final = 0, 0
        top = place * tokens + b * BLOCK
        for i in range(starts_ref.shape[0]):
            first = first + (starts_ref[i] < top).astype(jnp.int32)
            final = final + (starts_ref[i] <= top + (BLOCK - 1)).astype(jnp.int32)
        from_start = jnp.where(doc == first, jnp.exp(decay), 0.0)
        to_end = jnp.where(doc == final, jnp.exp(last - decay), 0.0)
        return decay, doc, from_start, to_end

    def project(b, lane):
        span = pl.ds(b * BLOCK, BLOCK)
        point_q, point_k = total[0, span, lane], total[1, span, lane]
        gate_q, gate_k = jax.nn.sigmoid(point_q), jax.nn.sigmoid(point_k)
        queries = (point_q * gate_q * HEAD_DIM ** (-0.5)).astype(jnp.bfloat16)
        keys = (point_k * gate_k).astype(jnp.bfloat16)
        values = total[2, span, lane].astype(jnp.bfloat16)
        return (point_q, gate_q, queries), (point_k, gate_k, keys), values

    def summarize(pair):
        @pl.loop(0, 2)
        def _(i):
            h = 2 * pair + i
            lane = pl.ds(pl.multiple_of(h * HEAD_DIM, HEAD_DIM), HEAD_DIM)
            forward = jnp.zeros((HEAD_DIM, HEAD_DIM), jnp.float32)
            query_states, decays = [], []
            for b in range(blocks):
                _, _, from_start, to_end = factors(b, lane)
                (_, _, queries), (_, _, keys), values = project(b, lane)
                weighted = (keys.astype(jnp.float32) * to_end).astype(jnp.bfloat16)
                key_state = dot(weighted, values, (0, 0))
                weighted = (queries.astype(jnp.float32) * from_start).astype(jnp.bfloat16)
                upstream = upper[pl.ds(b * BLOCK, BLOCK), lane]
                query_state = dot(weighted, upstream, (0, 0))
                states[0, h, b] = key_state
                states[1, h, b] = query_state
                decay = from_start[BLOCK - 1 :]
                forward = decay * forward + key_state
                query_states.append(query_state)
                decays.append(decay)
            backward = jnp.zeros((HEAD_DIM, HEAD_DIM), jnp.float32)
            for b in reversed(range(blocks)):
                backward = decays[b] * backward + query_states[b]
            sums_out[0, h] = forward.astype(jnp.bfloat16)
            sums_out[1, h] = backward.astype(jnp.bfloat16)

        for move in sums[pair]:
            move.start()

    def differentiate(pair):
        for move in sums[pair]:
            move.wait_recv()

        @pl.loop(0, 2)
        def _(i):
            h = 2 * pair + i
            lane = pl.ds(pl.multiple_of(h * HEAD_DIM, HEAD_DIM), HEAD_DIM)
            state = jnp.zeros((HEAD_DIM, HEAD_DIM), jnp.float32)
            reverse = jnp.zeros((HEAD_DIM, HEAD_DIM), jnp.float32)
            for flip in (1, 2, 3):
                owner = place ^ flip
                share = jnp.ones((1, HEAD_DIM), jnp.float32)
                for other in (1, 2, 3):
                    if other != flip:
                        at = place ^ other
                        between = ((at > owner) & (at < place)) | ((at < owner) & (at > place))
                        share = jnp.where(between, decays_in[other - 1, pl.ds(h, 1)] * share, share)
                came = share * sums_in[flip - 1, h].astype(jnp.float32)
                state = jnp.where(owner < place, state + came, state)
                reverse = jnp.where(owner > place, reverse + came, reverse)
            decays = [factors(b, lane)[2][BLOCK - 1 :] for b in range(blocks)]
            behind = [None] * blocks
            for b in reversed(range(blocks)):
                behind[b] = reverse.astype(jnp.bfloat16)
                reverse = decays[b] * reverse + states[1, h, b]
            for b in range(blocks):
                before = state.astype(jnp.bfloat16)
                state = decays[b] * state + states[0, h, b]
                span = pl.ds(b * BLOCK, BLOCK)
                decay, doc, from_start, to_end = factors(b, lane)
                gap = jnp.minimum(
                    jnp.concatenate([decay, decay], axis=1) - decay_rows[pl.ds(h, 1), span], 0.0
                )
                rows_at = lax.broadcasted_iota(jnp.int32, (BLOCK, BLOCK), 0)
                cols_at = lax.broadcasted_iota(jnp.int32, (BLOCK, BLOCK), 1)
                same = jnp.concatenate([doc, doc], axis=1) == documents(b, (1, BLOCK), 1)
                pair_weight = jnp.where(same & (rows_at >= cols_at), jnp.exp(gap), 0.0)
                (point_q, gate_q, queries), (point_k, gate_k, keys), values = project(b, lane)
                upstream = upper[span, lane]
                query_key = (dot(queries, keys, (1, 1)) * pair_weight).astype(jnp.bfloat16)
                value_score = (dot(upstream, values, (1, 1)) * pair_weight).astype(jnp.bfloat16)
                query_gradient = dot(value_score, keys, (1, 0)) + from_start * dot(
                    upstream, before, (1, 1)
                )
                key_gradient = dot(value_score, queries, (0, 0)) + to_end * dot(
                    values, behind[b], (1, 1)
                )
                value_gradient = dot(query_key, upstream, (0, 0)) + to_end * dot(
                    keys, behind[b], (1, 0)
                )
                slope_q = gate_q * (1.0 + point_q * (1.0 - gate_q)) * HEAD_DIM ** (-0.5)
                slope_k = gate_k * (1.0 + point_k * (1.0 - gate_k))
                grads[0, span, lane] = (query_gradient * slope_q).astype(jnp.bfloat16)
                grads[1, span, lane] = (key_gradient * slope_k).astype(jnp.bfloat16)
                grads[2, span, lane] = value_gradient.astype(jnp.bfloat16)

    def prepare():
        before = lax.broadcasted_iota(jnp.int32, (BLOCK, BLOCK), 0) <= lax.broadcasted_iota(
            jnp.int32, (BLOCK, BLOCK), 1
        )
        triangle = before.astype(jnp.float32)
        heads = log_ref.shape[0]
        for b in range(tokens // BLOCK):
            span = pl.ds(b * BLOCK, BLOCK)
            sums_of = lax.dot_general(
                log_ref[:, span], triangle, (((1,), (0,)), ((), ())),
                precision=lax.Precision.HIGHEST, preferred_element_type=jnp.float32,
            )
            decay_rows[pl.ds(0, heads), span] = sums_of
            for h in range(heads):
                wide = jnp.broadcast_to(sums_of[h : h + 1], (HEAD_DIM, BLOCK))
                decay_cols[span, pl.ds(h * HEAD_DIM, HEAD_DIM)] = wide.T
        decays_out[...] = jnp.ones_like(decays_out)
        for h in range(heads):
            product = jnp.ones((1, HEAD_DIM), jnp.float32)
            for b in range(tokens // BLOCK):
                from_start = factors(b, pl.ds(h * HEAD_DIM, HEAD_DIM))[2]
                product = product * from_start[BLOCK - 1 :]
            decays_out[pl.ds(h, 1)] = product

    prepare()
    for move in decays:
        move.start()
    arrived(0, 0)
    arrived(0, 1)
    arrived(1, 0)
    side[0].wait_recv()
    side[1].wait_recv()
    for move in (side[2], side[3], *far[0]):
        move.start()
    arrived(1, 1)
    own_w.wait()
    own_x.wait()
    own_up.wait()
    arrived(2, 0)
    arrived(2, 1)
    for pair in twin:
        for move in pair:
            move.wait_recv()
    for move in (*mix, *far[1], *far[2]):
        move.start()
    feats_copy = pltpu.make_async_copy(feats.at[place], feats_out, local.at[2])
    feats_copy.start()
    multiply(place, 0, True, 0, rows)
    multiply(place, 1, True, 0, rows)
    for flip in range(2):
        mix[flip].wait_recv()
        spread[0][flip].start()
    side[2].wait_recv()
    side[3].wait_recv()
    multiply(place ^ 1, 0, False, 0, rows)
    multiply(place ^ 2, 0, False, 0, rows)
    mix[2].wait_recv()
    spread[0][2].start()
    spread_twin[0].start()
    multiply(place ^ 1, 1, False, 0, rows)
    multiply(place ^ 2, 1, False, 0, rows)
    near_copies = [
        pltpu.make_async_copy(wall.at[place ^ f], wall_out.at[place ^ f], local.at[3 + f])
        for f in range(3)
    ]
    for move in near_copies:
        move.start()
    for move in decays:
        move.wait_recv()
    def spread_on(step):
        for flip in range(3):
            spread[step][flip].wait_recv()
            spread[step + 1][flip].start()
        spread_twin[step + 1].start()

    for move in (*far[0], *far[1]):
        move.wait_recv()
    multiply(place ^ 3, 0, False, 0, rows)
    spread_on(0)
    summarize(0)
    for move in far[3]:
        move.start()
    for move in far[2]:
        move.wait_recv()
    multiply(place ^ 3, 1, False, 0, part)
    multiply(place ^ 3, 1, False, near, part)
    differentiate(0)
    for move in far[3]:
        move.wait_recv()
    for move in direct:
        move.start()
    multiply(place ^ 3, 1, False, part, part)
    multiply(place ^ 3, 1, False, near + part, part)
    summarize(1)
    spread_on(1)
    far_copy = pltpu.make_async_copy(wall.at[place ^ 3], wall_out.at[place ^ 3], local.at[6])
    far_copy.start()
    differentiate(1)
    grads_copy = pltpu.make_async_copy(grads, grads_out, local.at[7])
    grads_copy.start()
    for move in (*spread[2], *direct):
        move.wait_recv()
    spread_twin[3].start()
    for move in spread_twin:
        move.wait_recv()
    for move in (feats_copy, *near_copies, far_copy, grads_copy):
        move.wait()
    for moves in (*ring, *twin, side, *far, mix, *spread, spread_twin, direct, decays, *sums):
        for move in moves:
            move.wait_send()


def gather_call(starts, log_decay, inputs, weights, cotangent):
    (tokens, cols), (_, rows, local_cols) = inputs.shape, weights.shape
    bf16, f32 = jnp.bfloat16, jnp.float32
    blocks = tokens // BLOCK
    shapes = [
        ((tokens, 2 * cols), bf16),
        ((4, 3, rows, local_cols), bf16),
        ((3, tokens, local_cols), bf16),
        ((3, tokens, 2 * cols), bf16),
    ]
    buffers = [
        ((4, tokens, 2 * cols), bf16),
        ((4, 3, rows, local_cols), bf16),
        ((3, tokens, local_cols), f32),
        ((3, tokens, local_cols), bf16),
        ((tokens, local_cols), bf16),
        ((8, tokens), f32),
        ((tokens, local_cols), f32),
        ((8, HEAD_DIM), f32),
        ((3, 8, HEAD_DIM), f32),
        ((2, 4, blocks, HEAD_DIM, HEAD_DIM), f32),
        ((2, 4, HEAD_DIM, HEAD_DIM), bf16),
        ((3, 4, HEAD_DIM, HEAD_DIM), bf16),
    ]
    anywhere = pl.BlockSpec(memory_space=pl.ANY)
    return pl.pallas_call(
        gather_kernel,
        in_specs=[pl.BlockSpec(memory_space=pltpu.SMEM), pl.BlockSpec(memory_space=pltpu.VMEM)]
        + [anywhere] * 3,
        out_specs=[anywhere] * 4,
        out_shape=[jax.ShapeDtypeStruct(*shape) for shape in shapes],
        scratch_shapes=[pltpu.VMEM(*shape) for shape in buffers]
        + [
            pltpu.SemaphoreType.DMA((54,)),
            pltpu.SemaphoreType.DMA((54,)),
            pltpu.SemaphoreType.DMA((9,)),
        ],
        compiler_params=pltpu.CompilerParams(
            collective_id=0, has_side_effects=True, vmem_limit_bytes=58 << 20
        ),
        name="gather",
    )(starts, log_decay, inputs, weights, cotangent)


def finish_kernel(
    grad_ref, feats_ref, wall_ref, swap_ref, keep_out, last_out, weight_out,
    grads, tokens_buf, rows_buf, total, keep, twin_out, twin_in, ring_out, ring_in,
    send, recv, local,
):
    place, head = lax.axis_index("seq"), lax.axis_index("head")
    z, core = head // 2, head % 2
    _, tokens, local_cols = grad_ref.shape
    rows, cols = total.shape[1], keep.shape[1]
    half, chunk = tokens // 2, tokens // 8
    x_id, y_id = (place ^ 1, head), (place ^ 2, head)
    next_id, last_id = (place, (head + 2) % 8), (place, (head + 6) % 8)
    twin_id = (place, head ^ 1)
    remote = remote_maker(send, recv)
    low, high = pl.ds(0, half), pl.ds(half, half)

    def fetch_rows(turn, part):
        owner = (z + 7 - turn) % 4
        side = pl.multiple_of((core if part else 1 - core) * cols, cols)
        return pltpu.make_async_copy(
            wall_ref.at[owner, :, pl.ds(side, cols)], rows_buf.at[part], local.at[part]
        )

    def fetch_tokens(flip):
        source = feats_ref if flip == 0 else swap_ref.at[flip - 1]
        return pltpu.make_async_copy(source, tokens_buf.at[flip % 2], local.at[2 + flip])

    own = pltpu.make_async_copy(grad_ref, grads.at[0], local.at[6])
    own.start()
    fetched_rows = [fetch_rows(0, 0), fetch_rows(0, 1)]
    for move in fetched_rows:
        move.start()
    fetched = [fetch_tokens(0), fetch_tokens(1)]
    for move in fetched:
        move.start()
    side = [
        remote(i, grad_ref.at[:, part], grads.at[flip, :, part], device)
        for i, (part, flip, device) in enumerate(
            ((high, 1, x_id), (low, 2, y_id), (low, 1, x_id), (high, 2, y_id))
        )
    ]
    part_rows = half // 2
    far = [
        [
            remote(
                4 + 2 * i + j, grads.at[flip, :, pl.ds(top + i * part_rows, part_rows)],
                grads.at[3, :, pl.ds(top + i * part_rows, part_rows)], device,
            )
            for j, (flip, top, device) in enumerate(((2, 0, x_id), (1, half, y_id)))
        ]
        for i in range(2)
    ]
    twin = [
        [
            remote(8 + 2 * k + p, twin_out.at[k % 2, part], twin_in.at[k, part], twin_id)
            for p, part in enumerate((low, high))
        ]
        for k in range(4)
    ]
    ring = [
        [
            remote(
                16 + 2 * k + p, ring_out.at[k, part],
                ring_in.at[k, part] if k < 2 else last_out.at[part], next_id,
            )
            for p, part in enumerate((low, high))
        ]
        for k in range(3)
    ]
    greet((x_id, y_id, next_id, last_id, twin_id))
    for move in side:
        move.start()
    own.wait()

    def back(part, p, target):
        @pl.loop(0, 2)
        def _(i):
            quarter = tokens // 4
            span = pl.ds(pl.multiple_of(p * half + i * quarter, quarter), quarter)
            term = None
            for k in range(3):
                piece = dot(grads[0, k, span, :], rows_buf[part, k], (1, 1))
                term = piece if term is None else term + piece
            target[span, :] = term.astype(target.dtype)

    def input_half(turn, p):
        if p == 0:
            for move in fetched_rows:
                move.wait()
        if turn >= 2:
            twin[turn - 2][p].wait_send()
        back(0, p, twin_out.at[turn % 2])
        twin[turn][p].start()
        back(1, p, keep)
        if p == 1 and turn < 3:
            for part in range(2):
                fetched_rows[part] = fetch_rows(turn + 1, part)
                fetched_rows[part].start()

    def pass_half(turn, p):
        twin[turn][p].wait_recv()
        if turn in (1, 2):
            ring[turn - 1][p].wait_recv()

        @pl.loop(0, 2)
        def _(i):
            quarter = tokens // 4
            span = pl.ds(pl.multiple_of(p * half + i * quarter, quarter), quarter)
            sum_ = keep[span, :] + twin_in[turn, span, :].astype(jnp.float32)
            if turn in (1, 2):
                sum_ = sum_ + ring_in[turn - 1, span, :].astype(jnp.float32)
            if turn < 3:
                ring_out[turn, span, :] = sum_.astype(jnp.bfloat16)
            else:
                keep[span, :] = sum_

        if turn < 3:
            ring[turn][p].start()

    def weight_block(flip):
        slot = flip % 2
        fetched[slot].wait()

        @pl.loop(0, rows // BLOCK)
        def _(i):
            span = pl.ds(pl.multiple_of(i * BLOCK, BLOCK), BLOCK)
            turned = tokens_buf[slot, :, span].T
            for k in range(3):
                term = jnp.dot(turned, grads[flip, k], preferred_element_type=jnp.float32)
                total[k, span, :] = term if flip == 0 else total[k, span, :] + term

        if flip < 2:
            fetched[slot] = fetch_tokens(flip + 2)
            fetched[slot].start()

    def weight_rest(i, part):
        slot = 3 % 2
        if i == 0 and part == 0:
            fetched[slot].wait()
        tops = [top + i * part_rows for top in (0, half)]

        @pl.loop(0, cols // BLOCK)
        def _(j):
            top = pl.multiple_of(j * BLOCK, BLOCK)
            span = pl.ds(pl.multiple_of(part * cols + top, BLOCK), BLOCK)
            turned = [tokens_buf[slot, pl.ds(t, part_rows), span].T for t in tops]
            for k in range(3):
                term = total[k, span, :]
                for t, rows_of in zip(tops, turned):
                    term = term + jnp.dot(
                        rows_of, grads[3, k, pl.ds(t, part_rows)], preferred_element_type=jnp.float32
                    )
                if i == 0:
                    total[k, span, :] = term
                else:
                    rows_buf[part, k, pl.ds(top, BLOCK), :] = term.astype(jnp.bfloat16)

    for p in range(2):
        input_half(0, p)
        pass_half(0, p)
    for p in range(2):
        input_half(1, p)
    weight_block(0)
    side[0].wait_recv()
    side[1].wait_recv()
    for moves in far:
        for move in moves:
            move.start()
    for p in range(2):
        pass_half(1, p)
    for p in range(2):
        input_half(2, p)
    side[2].wait_recv()
    weight_block(1)
    for p in range(2):
        pass_half(2, p)
    for p in range(2):
        input_half(3, p)
        pass_half(3, p)
    keep_copy = pltpu.make_async_copy(keep, keep_out, local.at[6])
    keep_copy.start()
    side[3].wait_recv()
    weight_block(2)
    stores = [
        pltpu.make_async_copy(
            rows_buf.at[part], weight_out.at[:, pl.ds(part * cols, cols)], local.at[part]
        )
        for part in range(2)
    ]
    for i in range(2):
        for move in far[i]:
            move.wait_recv()
        for part in range(2):
            weight_rest(i, part)
            if i == 1:
                stores[part].start()
    for move in ring[2]:
        move.wait_recv()
    for move in (keep_copy, *stores):
        move.wait()
    for moves in (side, *far, *ring, twin[2], twin[3]):
        for move in moves:
            move.wait_send()


def close_kernel(keep_ref, last_ref, rows_ref, input_ref, weight_ref):
    input_ref[...] = (keep_ref[...] + last_ref[...].astype(jnp.float32)).astype(jnp.bfloat16)
    weight_ref[...] = rows_ref[...]


def close_call(keep, last, weight):
    (tokens, cols), (_, rows, local_cols) = keep.shape, weight.shape
    steps = 4
    input_spec = pl.BlockSpec((tokens // steps, cols), lambda i: (i, 0))
    weight_spec = pl.BlockSpec((3, rows // steps, local_cols), lambda i: (0, i, 0))
    return pl.pallas_call(
        close_kernel,
        grid=(steps,),
        in_specs=[input_spec, input_spec, weight_spec],
        out_specs=[input_spec, weight_spec],
        out_shape=[
            jax.ShapeDtypeStruct(keep.shape, jnp.bfloat16),
            jax.ShapeDtypeStruct(weight.shape, weight.dtype),
        ],
        compiler_params=pltpu.CompilerParams(vmem_limit_bytes=62 << 20),
        name="close",
    )(keep, last, weight)


def finish_call(gradient, feats, wall, swap):
    _, tokens, local_cols = gradient.shape
    rows = wall.shape[2]
    cols = rows // 2
    bf16, f32 = jnp.bfloat16, jnp.float32
    anywhere = pl.BlockSpec(memory_space=pl.ANY)
    return pl.pallas_call(
        finish_kernel,
        in_specs=[anywhere] * 4,
        out_specs=[anywhere] * 3,
        out_shape=[
            jax.ShapeDtypeStruct((tokens, cols), f32),
            jax.ShapeDtypeStruct((tokens, cols), bf16),
            jax.ShapeDtypeStruct((3, rows, local_cols), bf16),
        ],
        scratch_shapes=[
            pltpu.VMEM((4, 3, tokens, local_cols), bf16),
            pltpu.VMEM((2, tokens, rows), bf16),
            pltpu.VMEM((2, 3, cols, local_cols), bf16),
            pltpu.VMEM((3, rows, local_cols), f32),
            pltpu.VMEM((tokens, cols), f32),
            pltpu.VMEM((2, tokens, cols), bf16),
            pltpu.VMEM((4, tokens, cols), bf16),
            pltpu.VMEM((3, tokens, cols), bf16),
            pltpu.VMEM((2, tokens, cols), bf16),
            pltpu.SemaphoreType.DMA((22,)),
            pltpu.SemaphoreType.DMA((22,)),
            pltpu.SemaphoreType.DMA((7,)),
        ],
        compiler_params=pltpu.CompilerParams(
            collective_id=1, has_side_effects=True, vmem_limit_bytes=60 << 20
        ),
        name="finish",
    )(gradient, feats, wall, swap)


def fast_body(inputs, projection, cotangent, log_decay, document_starts):
    feats, wall, gradient, swap = gather_call(
        document_starts, log_decay, inputs, projection.transpose(1, 0, 2), cotangent
    )
    input_gradient, weight_gradient = close_call(*finish_call(gradient, feats, wall, swap))
    return (input_gradient, weight_gradient.transpose(1, 0, 2))


def solution(mesh):
    fast = (mesh.shape["seq"], mesh.shape["head"]) == (4, 8)
    placed = (P("seq", "head"), P("seq", None, "head"), P("seq", "head"), P("head", "seq"), P())
    return jax.shard_map(
        fast_body if fast else general_body,
        mesh=mesh,
        in_specs=placed,
        out_specs=(P("seq", "head"), P("seq", None, "head")),
        check_vma=False,
    )
```

```python
import jax
import jax.numpy as jnp
from jax import lax
from jax.experimental import pallas as pl
from jax.experimental.layout import Layout, with_layout_constraint
from jax.experimental.pallas import tpu as pltpu
from jax.sharding import PartitionSpec as P

HEAD_DIM = 128
BLOCK = 256


def hop(array, axis, flip):
    return lax.ppermute(array, axis, [(i, i ^ flip) for i in range(lax.axis_size(axis))])


def gather_states(packed, axis):
    length, place = (lax.axis_size(axis), lax.axis_index(axis))
    if length != 4:
        whole = lax.all_gather(packed, axis)
        return [whole[k] for k in range(length)], jnp.arange(length, dtype=jnp.int32)
    parts = [packed] + [hop(packed, axis, flip) for flip in range(1, length)]
    return parts, place ^ jnp.arange(length, dtype=jnp.int32)


def device_weights(device_decay, owners, axis):
    length, place = (lax.axis_size(axis), lax.axis_index(axis))
    if length == 4:
        slab = jnp.broadcast_to(device_decay[:, None], (device_decay.shape[0], HEAD_DIM))
        hops = [slab] + [hop(slab, axis, flip) for flip in range(1, length)]
        arrived = jnp.stack([part[:, 0] for part in hops])
        mine = owners[None, :] == jnp.arange(length, dtype=jnp.int32)[:, None]
        decays = jnp.sum(jnp.where(mine[:, :, None], arrived[None], 0.0), axis=1)
    else:
        decays = lax.all_gather(device_decay, axis)
    at, other = owners[:, None], jnp.arange(length, dtype=jnp.int32)[None]
    before = (other > at) & (other < place)
    after = (other < at) & (other > place)
    weights = []
    for between, counts in ((before, owners < place), (after, owners > place)):
        product = jnp.prod(jnp.where(between[:, :, None], decays[None], 1.0), axis=1)
        weights.append(jnp.where(counts[:, None], product, 0.0))
    return jnp.stack(weights)


def gather_rows(part, axis):
    length, place, rows = (lax.axis_size(axis), lax.axis_index(axis), part.shape[1])
    if length != 4:
        whole = lax.all_gather(part, axis, axis=1, tiled=True)
        return [(0, 0, whole)]
    half = rows // 2
    low, high = part[:, :half], part[:, half:]
    x_high = hop(high, axis, 1)
    y_low = hop(low, axis, 2)
    x_low = hop(low, axis, 1)
    y_high = hop(high, axis, 2)
    d_low = hop(y_low, axis, 1)
    d_high = hop(x_high, axis, 2)
    return [
        (place, 0, low),
        (place, half, high),
        (place ^ 1, half, x_high),
        (place ^ 2, 0, y_low),
        (place ^ 1, 0, x_low),
        (place ^ 2, half, y_high),
        (place ^ 3, 0, d_low),
        (place ^ 3, half, d_high),
    ]


def scatter_rows(partial, between, source, axis, rows):
    length, place = (lax.axis_size(axis), lax.axis_index(axis))
    if length != 4:
        whole = partial(source, 0, 0, rows * length)
        return [between(source, 0, 1)], lax.psum_scatter(whole, axis, scatter_dimension=1, tiled=True)
    half = rows // 2

    def add(*terms):
        return sum(term.astype(jnp.float32) for term in terms).astype(jnp.bfloat16)

    far_low, far_high = partial(source, place ^ 3, 0, half), partial(source, place ^ 3, half, half)
    source, far_low, far_high = lax.optimization_barrier((source, far_low, far_high))
    far_low, far_high = hop(far_low, axis, 1), hop(far_high, axis, 2)
    beside = between(source, 0, 1)
    source, beside = lax.optimization_barrier((source, beside))
    x_low, y_high = partial(source, place ^ 1, 0, half), partial(source, place ^ 2, half, half)
    source, x_low, y_high = lax.optimization_barrier((source, x_low, y_high))
    x_low, y_high = hop(x_low, axis, 1), hop(y_high, axis, 2)
    x_high = hop(add(partial(source, place ^ 1, half, half), far_high), axis, 1)
    y_low = hop(add(partial(source, place ^ 2, 0, half), far_low), axis, 2)
    own_low, own_high = partial(source, place, 0, half), partial(source, place, half, half)
    whole = jnp.concatenate([add(own_low, x_low, y_low), add(own_high, x_high, y_high)], axis=1)
    return [beside], whole


def running_sum(values):
    inside = jnp.arange(values.shape[-1], dtype=jnp.int32)
    triangle = (inside[:, None] <= inside[None, :]).astype(jnp.float32)
    return jnp.einsum("hbu,ut->hbt", values, triangle, precision=lax.Precision.HIGHEST)


def block_factors(decay_sum, doc_index, doc_begin):
    inside = jnp.arange(doc_index.shape[-1], dtype=jnp.int32)
    causal = inside[:, None] >= inside[None, :]
    same_doc = (doc_index[:, :, None] == doc_index[:, None, :]) & causal[None]
    spread = jnp.minimum(decay_sum[..., :, None] - decay_sum[..., None, :], 0.0)
    pair_weight = jnp.where(same_doc[None], jnp.exp(spread), 0.0)
    to_end = jnp.where(
        (doc_index == doc_index[:, -1:])[None], jnp.exp(decay_sum[..., -1:] - decay_sum), 0.0
    )
    began_flag = doc_index == doc_index[:, :1] - doc_begin[:, :1]
    from_start = jnp.where(began_flag[None], jnp.exp(decay_sum), 0.0)
    return (pair_weight, to_end, from_start, from_start[..., -1])


def dot(left, right, contract):
    return lax.dot_general(
        left, right, ((contract[:1], contract[1:]), ((), ())), preferred_element_type=jnp.float32
    )


def projections(proj_ref, span):
    point_q, point_k = proj_ref[0, span], proj_ref[1, span]
    gate_q, gate_k = jax.nn.sigmoid(point_q), jax.nn.sigmoid(point_k)
    queries = (point_q * gate_q * HEAD_DIM ** (-0.5)).astype(jnp.bfloat16)
    keys = (point_k * gate_k).astype(jnp.bfloat16)
    values = proj_ref[2, span].astype(jnp.bfloat16)
    return (point_q, gate_q, queries), (point_k, gate_k, keys), values


def state_kernel(proj_ref, up_ref, start_ref, end_ref, key_ref, query_ref, total_ref):
    blocks = key_ref.shape[1]
    forward = jnp.zeros((HEAD_DIM, HEAD_DIM), jnp.float32)
    query_states, decays = [], []
    for b in range(blocks):
        span = pl.ds(b * BLOCK, BLOCK)
        (_, _, queries), (_, _, keys), values = projections(proj_ref, span)
        keys_weighted = (keys.astype(jnp.float32) * end_ref[0, span]).astype(jnp.bfloat16)
        queries_weighted = (queries.astype(jnp.float32) * start_ref[0, span]).astype(jnp.bfloat16)
        key_state = dot(keys_weighted, values, (0, 0))
        query_state = dot(queries_weighted, up_ref[span], (0, 0))
        key_ref[0, b] = key_state
        query_ref[0, b] = query_state
        decay = start_ref[0, pl.ds(b * BLOCK + BLOCK - 1, 1)]
        forward = decay * forward + key_state
        query_states.append(query_state)
        decays.append(decay)
    backward = jnp.zeros((HEAD_DIM, HEAD_DIM), jnp.float32)
    for b in reversed(range(blocks)):
        backward = decays[b] * backward + query_states[b]
    total_ref[0, 0] = forward.astype(jnp.bfloat16)
    total_ref[1, 0] = backward.astype(jnp.bfloat16)


def gradient_kernel(
    weight_ref, proj_ref, up_ref, start_ref, end_ref, pair_ref, key_ref, query_ref, *rest
):
    totals, out_ref = rest[:-1], rest[-1]
    blocks = key_ref.shape[1]
    head = pl.program_id(0)
    state = jnp.zeros((HEAD_DIM, HEAD_DIM), jnp.float32)
    reverse = jnp.zeros((HEAD_DIM, HEAD_DIM), jnp.float32)
    for k, total in enumerate(totals):
        state = state + weight_ref[0, k, head] * total[0, 0].astype(jnp.float32)
        reverse = reverse + weight_ref[1, k, head] * total[1, 0].astype(jnp.float32)
    decays = [start_ref[0, pl.ds(b * BLOCK + BLOCK - 1, 1)] for b in range(blocks)]
    after = [None] * blocks
    for b in reversed(range(blocks)):
        after[b] = reverse.astype(jnp.bfloat16)
        reverse = decays[b] * reverse + query_ref[0, b]
    for b in range(blocks):
        before = state.astype(jnp.bfloat16)
        state = decays[b] * state + key_ref[0, b]
        span = pl.ds(b * BLOCK, BLOCK)
        (point_q, gate_q, queries), (point_k, gate_k, keys), values = projections(proj_ref, span)
        upstream = up_ref[span]
        from_start, to_end, pair = start_ref[0, span], end_ref[0, span], pair_ref[0, b]
        query_key = (dot(queries, keys, (1, 1)) * pair).astype(jnp.bfloat16)
        value_score = (dot(upstream, values, (1, 1)) * pair).astype(jnp.bfloat16)
        query_gradient = dot(value_score, keys, (1, 0)) + from_start * dot(
            upstream, before, (1, 1)
        )
        key_gradient = dot(value_score, queries, (0, 0)) + to_end * dot(values, after[b], (1, 1))
        value_gradient = dot(query_key, upstream, (0, 0)) + to_end * dot(keys, after[b], (1, 0))
        slope_q = gate_q * (1.0 + point_q * (1.0 - gate_q)) * HEAD_DIM ** (-0.5)
        slope_k = gate_k * (1.0 + point_k * (1.0 - gate_k))
        out_ref[0, span] = (query_gradient * slope_q).astype(jnp.bfloat16)
        out_ref[1, span] = (key_gradient * slope_k).astype(jnp.bfloat16)
        out_ref[2, span] = value_gradient.astype(jnp.bfloat16)


def input_kernel(gradient_ref, weight_ref, out_ref):
    for first in range(0, out_ref.shape[0], BLOCK):
        span = pl.ds(first, BLOCK)
        total = dot(gradient_ref[0, span], weight_ref[0], (1, 1))
        for k in (1, 2):
            total = total + dot(gradient_ref[k, span], weight_ref[k], (1, 1))
        out_ref[span] = total.astype(jnp.bfloat16)


def general_body(inputs, projection, cotangent, log_decay, document_starts):
    tokens = inputs.shape[0]
    heads_here = log_decay.shape[0]
    local_cols = cotangent.shape[1]
    blocks = tokens // BLOCK
    features = lax.all_gather(inputs, "head", axis=1, tiled=True)
    rows = projection.shape[0]
    blocks_w = gather_rows(projection.transpose(1, 0, 2), "seq")

    def feature_rows(owner, first, count):
        return lax.dynamic_slice_in_dim(features, owner * rows + first, count, axis=1)

    offset = lax.axis_index("seq") * tokens
    positions = offset + jnp.arange(tokens, dtype=jnp.int32)
    doc_index = (
        jnp.sum((document_starts[None, :] <= positions[:, None]).astype(jnp.int32), axis=1) - 1
    )
    doc_begin = jnp.any(document_starts[None, :] == positions[:, None], axis=1).astype(jnp.int32)
    decay_sum = running_sum(log_decay.reshape(heads_here, blocks, BLOCK))
    pair_weight, to_end, from_start, block_decay = block_factors(
        decay_sum, doc_index.reshape(blocks, BLOCK), doc_begin.reshape(blocks, BLOCK)
    )
    lanes = (heads_here, tokens, HEAD_DIM)
    to_end = jnp.broadcast_to(to_end.reshape(heads_here, tokens)[..., None], lanes)
    from_start = jnp.broadcast_to(from_start.reshape(heads_here, tokens)[..., None], lanes)
    device_decay = jnp.prod(block_decay, axis=1)

    zero = jnp.zeros((), jnp.bfloat16)
    if len(blocks_w) > 2:
        owner, first, block = blocks_w[2]
        zero, block = lax.optimization_barrier((zero, block))
        blocks_w[2] = (owner, first, block)
    weights_all = jnp.broadcast_to(zero, (3, features.shape[1], local_cols))

    def place_rows(whole, some):
        for owner, first, block in some:
            whole = lax.dynamic_update_slice_in_dim(whole, block, owner * rows + first, axis=1)
        return whole

    early, late = blocks_w[:6], blocks_w[6:]
    weights_all = place_rows(weights_all, early)
    features, weights_all, from_start, to_end, pair_weight = lax.optimization_barrier(
        (features, weights_all, from_start, to_end, pair_weight)
    )
    projected = None
    for k, (owner, first, block) in enumerate(blocks_w):
        piece = jnp.einsum(
            "td,kdc->ktc",
            feature_rows(owner, first, block.shape[1]),
            block,
            preferred_element_type=jnp.float32,
        )
        projected = piece if projected is None else lax.optimization_barrier(projected) + piece
        if k == min(5, len(blocks_w) - 1):
            projected, device_decay = lax.optimization_barrier((projected, device_decay))
    weights_all = place_rows(weights_all, late)

    proj_spec = pl.BlockSpec((3, tokens, HEAD_DIM), lambda h: (0, 0, h))
    up_spec = pl.BlockSpec((tokens, HEAD_DIM), lambda h: (0, h))
    lane_spec = pl.BlockSpec((1, tokens, HEAD_DIM), lambda h: (h, 0, 0))
    state_spec = pl.BlockSpec((1, blocks, HEAD_DIM, HEAD_DIM), lambda h: (h, 0, 0, 0))
    total_spec = pl.BlockSpec((2, 1, HEAD_DIM, HEAD_DIM), lambda h: (0, h, 0, 0))
    pair_spec = pl.BlockSpec((1, blocks, BLOCK, BLOCK), lambda h: (h, 0, 0, 0))
    states = jax.ShapeDtypeStruct((heads_here, blocks, HEAD_DIM, HEAD_DIM), jnp.float32)
    key_state, query_state, totals = pl.pallas_call(
        state_kernel,
        grid=(heads_here,),
        in_specs=[proj_spec, up_spec, lane_spec, lane_spec],
        out_specs=[state_spec, state_spec, total_spec],
        out_shape=[
            states,
            states,
            jax.ShapeDtypeStruct((2, heads_here, HEAD_DIM, HEAD_DIM), jnp.bfloat16),
        ],
    )(projected, cotangent, from_start, to_end)
    parts, owners = gather_states(totals, "seq")
    weights = device_weights(device_decay, owners, "seq")
    project_gradient = pl.pallas_call(
        gradient_kernel,
        grid=(heads_here,),
        in_specs=[pl.BlockSpec(memory_space=pltpu.SMEM)]
        + [proj_spec, up_spec, lane_spec, lane_spec, pair_spec, state_spec, state_spec]
        + [total_spec] * len(parts),
        out_specs=proj_spec,
        out_shape=jax.ShapeDtypeStruct(projected.shape, jnp.bfloat16),
    )(weights, projected, cotangent, from_start, to_end, pair_weight, key_state, query_state, *parts)

    def weight_partial(gradient, owner, first, count):
        term = jnp.einsum(
            "td,ktc->kdc",
            feature_rows(owner, first, count),
            gradient,
            preferred_element_type=jnp.float32,
        ).astype(jnp.bfloat16)
        return with_layout_constraint(term, Layout(major_to_minor=(0, 1, 2)))

    def input_partial(gradient, part, of):
        columns = features.shape[1]
        tile, count = columns // 8, tokens // of
        return pl.pallas_call(
            input_kernel,
            grid=(columns // tile,),
            in_specs=[
                pl.BlockSpec((3, count, local_cols), lambda i: (0, part, 0)),
                pl.BlockSpec((3, tile, local_cols), lambda i: (0, i, 0)),
            ],
            out_specs=pl.BlockSpec((count, tile), lambda i: (0, i)),
            out_shape=jax.ShapeDtypeStruct((count, columns), jnp.bfloat16),
            cost_estimate=pl.CostEstimate(flops=1, bytes_accessed=1, transcendentals=0),
            compiler_params=pltpu.CompilerParams(vmem_limit_bytes=40 << 20),
        )(gradient, weights_all)

    input_partials, weight_gradient = scatter_rows(
        weight_partial, input_partial, project_gradient, "seq", rows
    )
    input_gradient = lax.psum_scatter(
        input_partials[0], "head", scatter_dimension=1, tiled=True
    )
    weight_gradient = weight_gradient.transpose(1, 0, 2)
    return (input_gradient, weight_gradient)


MESH = pl.DeviceIdType.MESH
PAIR = 2 * HEAD_DIM


def remote_maker(send, recv):
    def remote(index, source, target, device):
        return pltpu.make_async_remote_copy(
            src_ref=source,
            dst_ref=target,
            send_sem=send.at[index],
            recv_sem=recv.at[index],
            device_id=device,
            device_id_type=MESH,
        )

    return remote


def greet(others):
    barrier = pltpu.get_barrier_semaphore()
    for other in others:
        pl.semaphore_signal(barrier, inc=1, device_id=other, device_id_type=MESH)
    pl.semaphore_wait(barrier, len(others))


def gather_kernel(
    starts_ref, log_ref, x_ref, w_ref, up_ref, feats_out, wall_out, grads_out, swap,
    feats, wall, total, grads, upper, decay_rows, decay_cols, decays_out, decays_in, states,
    sums_out, sums_in, send, recv, local,
):
    place, head = lax.axis_index("seq"), lax.axis_index("head")
    z, core = head // 2, head % 2
    tokens, cols = x_ref.shape
    rows = w_ref.shape[1]
    half, near, chunk = tokens // 2, rows // 2, tokens // 8
    blocks = tokens // BLOCK
    x_id, y_id, far_id = (place ^ 1, head), (place ^ 2, head), (place ^ 3, head)
    next_id, last_id = (place, (head + 2) % 8), (place, (head + 6) % 8)
    twin_id = (place, head ^ 1)
    mine = pl.ds(pl.multiple_of(core * cols, cols), cols)
    remote = remote_maker(send, recv)

    own_w = pltpu.make_async_copy(w_ref, wall.at[place], local.at[0])
    own_x = pltpu.make_async_copy(x_ref, feats.at[z, :, mine], local.at[1])
    own_up = pltpu.make_async_copy(up_ref, upper, local.at[8])
    own_w.start()
    own_x.start()
    own_up.start()

    def block(step, part):
        return feats.at[(z + 4 - step) % 4, pl.ds(part * half, half), mine]

    def x_part(step, part):
        return x_ref.at[pl.ds(part * half, half)] if step == 0 else block(step, part)

    ring = [
        [remote(2 * k + p, x_part(k, p), block(k, p), next_id) for p in range(2)] for k in range(3)
    ]
    twin = [
        [remote(6 + 2 * k + p, x_part(k, p), block(k, p), twin_id) for p in range(2)]
        for k in range(4)
    ]
    low, high = pl.ds(0, near), pl.ds(near, near)
    side = [
        remote(14 + i, w_ref.at[:, part], wall.at[place, :, part], device)
        for i, (part, device) in enumerate(((high, x_id), (low, y_id), (low, x_id), (high, y_id)))
    ]

    def patch(owner, top, count, pair):
        return wall.at[owner, :, pl.ds(top, count), pl.ds(pair * PAIR, PAIR)]

    def forward(index, top, count, pair):
        first, second = patch(place ^ 2, top, count, pair), patch(place ^ 1, near + top, count, pair)
        return [remote(index, first, first, x_id), remote(index + 1, second, second, y_id)]

    part = near // 2
    filler = near // 3
    far = [
        forward(18, 0, filler, 0),
        forward(20, filler, near - filler, 0),
        forward(22, 0, part, 1),
        forward(24, part, part, 1),
    ]

    def share(who):
        return pl.ds(pl.multiple_of(who * chunk, chunk), chunk)

    others = ((1, x_id), (2, y_id), (3, far_id))
    mix = [
        remote(25 + flip, feats.at[place ^ flip, share(head)], swap.at[flip - 1, share(head)], device)
        for flip, device in others
    ]

    def shared(step):
        return swap.at[:, share((head + 8 - 2 * step) % 8)]

    ringed = chunk * 5 // 8

    def ring_rows(step):
        top = pl.multiple_of((head + 8 - 2 * step) % 8 * chunk, chunk)
        return pl.ds(top, chunk if step < 2 else ringed)

    spread = [
        [
            remote(
                29 + 3 * k + flip, swap.at[flip, ring_rows(k)], swap.at[flip, ring_rows(k)], next_id
            )
            for flip in range(3)
        ]
        for k in range(3)
    ]
    spread_twin = [remote(38 + k, shared(k), shared(k), twin_id) for k in range(4)]
    direct_rows = pl.ds(
        pl.multiple_of((head + 2) % 8 * chunk + ringed, chunk // 8), chunk - ringed
    )
    direct = [
        remote(41 + flip, feats.at[place ^ flip, direct_rows], swap.at[flip - 1, direct_rows], device)
        for flip, device in others
    ]
    decays = [
        remote(44 + flip, decays_out, decays_in.at[flip - 1], device) for flip, device in others
    ]
    way = (place % 2, place // 2, place // 2)
    sums = [
        [
            remote(
                47 + 3 * pair + flip, sums_out.at[way[flip - 1], pl.ds(2 * pair, 2)],
                sums_in.at[flip - 1, pl.ds(2 * pair, 2)], device,
            )
            for flip, device in others
        ]
        for pair in range(2)
    ]

    greet((x_id, y_id, far_id, next_id, last_id, twin_id))
    ring[0][0].start()
    side[0].start()
    side[1].start()
    ring[0][1].start()
    twin[0][0].start()
    twin[0][1].start()

    def arrived(step, part):
        ring[step][part].wait_recv()
        if step < 2:
            ring[step + 1][part].start()
        twin[step + 1][part].start()

    def multiply(owner, pair, begin, top, count):
        columns = pl.ds(pair * PAIR, PAIR)

        @pl.loop(0, 6)
        def _(i):
            k, span = i // 2, pl.ds(pl.multiple_of(i % 2 * half, half), half)
            term = jnp.dot(
                feats[owner, span, pl.ds(top, count)],
                wall[owner, k, pl.ds(top, count), columns],
                preferred_element_type=jnp.float32,
            )
            total[k, span, columns] = term if begin else total[k, span, columns] + term

    def documents(b, shape, axis):
        at = lax.broadcasted_iota(jnp.int32, shape, axis) + (place * tokens + b * BLOCK)
        return sum((starts_ref[i] <= at).astype(jnp.int32) for i in range(starts_ref.shape[0]))

    def factors(b, lane):
        span = pl.ds(b * BLOCK, BLOCK)
        decay, doc = decay_cols[span, lane], documents(b, (BLOCK, HEAD_DIM), 0)
        last = decay_cols[pl.ds(b * BLOCK + BLOCK - 1, 1), lane]
        first, final = 0, 0
        top = place * tokens + b * BLOCK
        for i in range(starts_ref.shape[0]):
            first = first + (starts_ref[i] < top).astype(jnp.int32)
            final = final + (starts_ref[i] <= top + (BLOCK - 1)).astype(jnp.int32)
        from_start = jnp.where(doc == first, jnp.exp(decay), 0.0)
        to_end = jnp.where(doc == final, jnp.exp(last - decay), 0.0)
        return decay, doc, from_start, to_end

    def project(b, lane):
        span = pl.ds(b * BLOCK, BLOCK)
        point_q, point_k = total[0, span, lane], total[1, span, lane]
        gate_q, gate_k = jax.nn.sigmoid(point_q), jax.nn.sigmoid(point_k)
        queries = (point_q * gate_q * HEAD_DIM ** (-0.5)).astype(jnp.bfloat16)
        keys = (point_k * gate_k).astype(jnp.bfloat16)
        values = total[2, span, lane].astype(jnp.bfloat16)
        return (point_q, gate_q, queries), (point_k, gate_k, keys), values

    def summarize(pair):
        @pl.loop(0, 2)
        def _(i):
            h = 2 * pair + i
            lane = pl.ds(pl.multiple_of(h * HEAD_DIM, HEAD_DIM), HEAD_DIM)
            forward = jnp.zeros((HEAD_DIM, HEAD_DIM), jnp.float32)
            query_states, decays = [], []
            for b in range(blocks):
                _, _, from_start, to_end = factors(b, lane)
                (_, _, queries), (_, _, keys), values = project(b, lane)
                weighted = (keys.astype(jnp.float32) * to_end).astype(jnp.bfloat16)
                key_state = dot(weighted, values, (0, 0))
                weighted = (queries.astype(jnp.float32) * from_start).astype(jnp.bfloat16)
                upstream = upper[pl.ds(b * BLOCK, BLOCK), lane]
                query_state = dot(weighted, upstream, (0, 0))
                states[0, h, b] = key_state
                states[1, h, b] = query_state
                decay = from_start[BLOCK - 1 :]
                forward = decay * forward + key_state
                query_states.append(query_state)
                decays.append(decay)
            backward = jnp.zeros((HEAD_DIM, HEAD_DIM), jnp.float32)
            for b in reversed(range(blocks)):
                backward = decays[b] * backward + query_states[b]
            sums_out[0, h] = forward.astype(jnp.bfloat16)
            sums_out[1, h] = backward.astype(jnp.bfloat16)

        for move in sums[pair]:
            move.start()

    def differentiate(pair):
        for move in sums[pair]:
            move.wait_recv()

        @pl.loop(0, 2)
        def _(i):
            h = 2 * pair + i
            lane = pl.ds(pl.multiple_of(h * HEAD_DIM, HEAD_DIM), HEAD_DIM)
            state = jnp.zeros((HEAD_DIM, HEAD_DIM), jnp.float32)
            reverse = jnp.zeros((HEAD_DIM, HEAD_DIM), jnp.float32)
            for flip in (1, 2, 3):
                owner = place ^ flip
                share = jnp.ones((1, HEAD_DIM), jnp.float32)
                for other in (1, 2, 3):
                    if other != flip:
                        at = place ^ other
                        between = ((at > owner) & (at < place)) | ((at < owner) & (at > place))
                        share = jnp.where(between, decays_in[other - 1, pl.ds(h, 1)] * share, share)
                came = share * sums_in[flip - 1, h].astype(jnp.float32)
                state = jnp.where(owner < place, state + came, state)
                reverse = jnp.where(owner > place, reverse + came, reverse)
            decays = [factors(b, lane)[2][BLOCK - 1 :] for b in range(blocks)]
            behind = [None] * blocks
            for b in reversed(range(blocks)):
                behind[b] = reverse.astype(jnp.bfloat16)
                reverse = decays[b] * reverse + states[1, h, b]
            for b in range(blocks):
                before = state.astype(jnp.bfloat16)
                state = decays[b] * state + states[0, h, b]
                span = pl.ds(b * BLOCK, BLOCK)
                decay, doc, from_start, to_end = factors(b, lane)
                gap = jnp.minimum(
                    jnp.concatenate([decay, decay], axis=1) - decay_rows[pl.ds(h, 1), span], 0.0
                )
                rows_at = lax.broadcasted_iota(jnp.int32, (BLOCK, BLOCK), 0)
                cols_at = lax.broadcasted_iota(jnp.int32, (BLOCK, BLOCK), 1)
                same = jnp.concatenate([doc, doc], axis=1) == documents(b, (1, BLOCK), 1)
                pair_weight = jnp.where(same & (rows_at >= cols_at), jnp.exp(gap), 0.0)
                (point_q, gate_q, queries), (point_k, gate_k, keys), values = project(b, lane)
                upstream = upper[span, lane]
                query_key = (dot(queries, keys, (1, 1)) * pair_weight).astype(jnp.bfloat16)
                value_score = (dot(upstream, values, (1, 1)) * pair_weight).astype(jnp.bfloat16)
                query_gradient = dot(value_score, keys, (1, 0)) + from_start * dot(
                    upstream, before, (1, 1)
                )
                key_gradient = dot(value_score, queries, (0, 0)) + to_end * dot(
                    values, behind[b], (1, 1)
                )
                value_gradient = dot(query_key, upstream, (0, 0)) + to_end * dot(
                    keys, behind[b], (1, 0)
                )
                slope_q = gate_q * (1.0 + point_q * (1.0 - gate_q)) * HEAD_DIM ** (-0.5)
                slope_k = gate_k * (1.0 + point_k * (1.0 - gate_k))
                grads[0, span, lane] = (query_gradient * slope_q).astype(jnp.bfloat16)
                grads[1, span, lane] = (key_gradient * slope_k).astype(jnp.bfloat16)
                grads[2, span, lane] = value_gradient.astype(jnp.bfloat16)

    def prepare():
        before = lax.broadcasted_iota(jnp.int32, (BLOCK, BLOCK), 0) <= lax.broadcasted_iota(
            jnp.int32, (BLOCK, BLOCK), 1
        )
        triangle = before.astype(jnp.float32)
        heads = log_ref.shape[0]
        for b in range(tokens // BLOCK):
            span = pl.ds(b * BLOCK, BLOCK)
            sums_of = lax.dot_general(
                log_ref[:, span], triangle, (((1,), (0,)), ((), ())),
                precision=lax.Precision.HIGHEST, preferred_element_type=jnp.float32,
            )
            decay_rows[pl.ds(0, heads), span] = sums_of
            for h in range(heads):
                wide = jnp.broadcast_to(sums_of[h : h + 1], (HEAD_DIM, BLOCK))
                decay_cols[span, pl.ds(h * HEAD_DIM, HEAD_DIM)] = wide.T
        decays_out[...] = jnp.ones_like(decays_out)
        for h in range(heads):
            product = jnp.ones((1, HEAD_DIM), jnp.float32)
            for b in range(tokens // BLOCK):
                from_start = factors(b, pl.ds(h * HEAD_DIM, HEAD_DIM))[2]
                product = product * from_start[BLOCK - 1 :]
            decays_out[pl.ds(h, 1)] = product

    prepare()
    for move in decays:
        move.start()
    arrived(0, 0)
    arrived(0, 1)
    arrived(1, 0)
    side[0].wait_recv()
    side[1].wait_recv()
    for move in (side[2], side[3], *far[0]):
        move.start()
    arrived(1, 1)
    own_w.wait()
    own_x.wait()
    own_up.wait()
    arrived(2, 0)
    arrived(2, 1)
    for pair in twin:
        for move in pair:
            move.wait_recv()
    for move in (*mix, *far[1], *far[2]):
        move.start()
    feats_copy = pltpu.make_async_copy(feats.at[place], feats_out, local.at[2])
    feats_copy.start()
    multiply(place, 0, True, 0, rows)
    multiply(place, 1, True, 0, rows)
    for flip in range(2):
        mix[flip].wait_recv()
        spread[0][flip].start()
    side[2].wait_recv()
    side[3].wait_recv()
    multiply(place ^ 1, 0, False, 0, rows)
    multiply(place ^ 2, 0, False, 0, rows)
    mix[2].wait_recv()
    spread[0][2].start()
    spread_twin[0].start()
    multiply(place ^ 1, 1, False, 0, rows)
    multiply(place ^ 2, 1, False, 0, rows)
    near_copies = [
        pltpu.make_async_copy(wall.at[place ^ f], wall_out.at[place ^ f], local.at[3 + f])
        for f in range(3)
    ]
    for move in near_copies:
        move.start()
    for move in decays:
        move.wait_recv()
    def spread_on(step):
        for flip in range(3):
            spread[step][flip].wait_recv()
            spread[step + 1][flip].start()
        spread_twin[step + 1].start()

    for move in (*far[0], *far[1]):
        move.wait_recv()
    multiply(place ^ 3, 0, False, 0, rows)
    spread_on(0)
    summarize(0)
    for move in far[3]:
        move.start()
    for move in far[2]:
        move.wait_recv()
    multiply(place ^ 3, 1, False, 0, part)
    multiply(place ^ 3, 1, False, near, part)
    differentiate(0)
    spread_on(1)
    for move in far[3]:
        move.wait_recv()
    multiply(place ^ 3, 1, False, part, part)
    multiply(place ^ 3, 1, False, near + part, part)
    summarize(1)
    for move in direct:
        move.start()
    far_copy = pltpu.make_async_copy(wall.at[place ^ 3], wall_out.at[place ^ 3], local.at[6])
    far_copy.start()
    differentiate(1)
    grads_copy = pltpu.make_async_copy(grads, grads_out, local.at[7])
    grads_copy.start()
    for move in (*spread[2], *direct):
        move.wait_recv()
    spread_twin[3].start()
    for move in spread_twin:
        move.wait_recv()
    for move in (feats_copy, *near_copies, far_copy, grads_copy):
        move.wait()
    for moves in (*ring, *twin, side, *far, mix, *spread, spread_twin, direct, decays, *sums):
        for move in moves:
            move.wait_send()


def gather_call(starts, log_decay, inputs, weights, cotangent):
    (tokens, cols), (_, rows, local_cols) = inputs.shape, weights.shape
    bf16, f32 = jnp.bfloat16, jnp.float32
    blocks = tokens // BLOCK
    shapes = [
        ((tokens, 2 * cols), bf16),
        ((4, 3, rows, local_cols), bf16),
        ((3, tokens, local_cols), bf16),
        ((3, tokens, 2 * cols), bf16),
    ]
    buffers = [
        ((4, tokens, 2 * cols), bf16),
        ((4, 3, rows, local_cols), bf16),
        ((3, tokens, local_cols), f32),
        ((3, tokens, local_cols), bf16),
        ((tokens, local_cols), bf16),
        ((8, tokens), f32),
        ((tokens, local_cols), f32),
        ((8, HEAD_DIM), f32),
        ((3, 8, HEAD_DIM), f32),
        ((2, 4, blocks, HEAD_DIM, HEAD_DIM), f32),
        ((2, 4, HEAD_DIM, HEAD_DIM), bf16),
        ((3, 4, HEAD_DIM, HEAD_DIM), bf16),
    ]
    anywhere = pl.BlockSpec(memory_space=pl.ANY)
    return pl.pallas_call(
        gather_kernel,
        in_specs=[pl.BlockSpec(memory_space=pltpu.SMEM), pl.BlockSpec(memory_space=pltpu.VMEM)]
        + [anywhere] * 3,
        out_specs=[anywhere] * 4,
        out_shape=[jax.ShapeDtypeStruct(*shape) for shape in shapes],
        scratch_shapes=[pltpu.VMEM(*shape) for shape in buffers]
        + [
            pltpu.SemaphoreType.DMA((54,)),
            pltpu.SemaphoreType.DMA((54,)),
            pltpu.SemaphoreType.DMA((9,)),
        ],
        compiler_params=pltpu.CompilerParams(
            collective_id=0, has_side_effects=True, vmem_limit_bytes=58 << 20
        ),
        name="gather",
    )(starts, log_decay, inputs, weights, cotangent)


def finish_kernel(
    grad_ref, feats_ref, wall_ref, swap_ref, keep_out, last_out, weight_out,
    grads, tokens_buf, rows_buf, total, keep, twin_out, twin_in, ring_out, ring_in,
    send, recv, local,
):
    place, head = lax.axis_index("seq"), lax.axis_index("head")
    z, core = head // 2, head % 2
    _, tokens, local_cols = grad_ref.shape
    rows, cols = total.shape[1], keep.shape[1]
    half, chunk = tokens // 2, tokens // 8
    x_id, y_id = (place ^ 1, head), (place ^ 2, head)
    next_id, last_id = (place, (head + 2) % 8), (place, (head + 6) % 8)
    twin_id = (place, head ^ 1)
    remote = remote_maker(send, recv)
    low, high = pl.ds(0, half), pl.ds(half, half)

    def fetch_rows(turn, part):
        owner = (z + 7 - turn) % 4
        side = pl.multiple_of((core if part else 1 - core) * cols, cols)
        return pltpu.make_async_copy(
            wall_ref.at[owner, :, pl.ds(side, cols)], rows_buf.at[part], local.at[part]
        )

    def fetch_tokens(flip):
        source = feats_ref if flip == 0 else swap_ref.at[flip - 1]
        return pltpu.make_async_copy(source, tokens_buf.at[flip % 2], local.at[2 + flip])

    own = pltpu.make_async_copy(grad_ref, grads.at[0], local.at[6])
    own.start()
    fetched_rows = [fetch_rows(0, 0), fetch_rows(0, 1)]
    for move in fetched_rows:
        move.start()
    fetched = [fetch_tokens(0), fetch_tokens(1)]
    for move in fetched:
        move.start()
    side = [
        remote(i, grad_ref.at[:, part], grads.at[flip, :, part], device)
        for i, (part, flip, device) in enumerate(
            ((high, 1, x_id), (low, 2, y_id), (low, 1, x_id), (high, 2, y_id))
        )
    ]
    part_rows = half // 2
    far = [
        [
            remote(
                4 + 2 * i + j, grads.at[flip, :, pl.ds(top + i * part_rows, part_rows)],
                grads.at[3, :, pl.ds(top + i * part_rows, part_rows)], device,
            )
            for j, (flip, top, device) in enumerate(((2, 0, x_id), (1, half, y_id)))
        ]
        for i in range(2)
    ]
    twin = [
        [
            remote(8 + 2 * k + p, twin_out.at[k % 2, part], twin_in.at[k, part], twin_id)
            for p, part in enumerate((low, high))
        ]
        for k in range(4)
    ]
    ring = [
        [
            remote(
                16 + 2 * k + p, ring_out.at[k, part],
                ring_in.at[k, part] if k < 2 else last_out.at[part], next_id,
            )
            for p, part in enumerate((low, high))
        ]
        for k in range(3)
    ]
    greet((x_id, y_id, next_id, last_id, twin_id))
    for move in side:
        move.start()
    own.wait()

    def back(part, p, target):
        @pl.loop(0, 2)
        def _(i):
            quarter = tokens // 4
            span = pl.ds(pl.multiple_of(p * half + i * quarter, quarter), quarter)
            term = None
            for k in range(3):
                piece = dot(grads[0, k, span, :], rows_buf[part, k], (1, 1))
                term = piece if term is None else term + piece
            target[span, :] = term.astype(target.dtype)

    def input_half(turn, p):
        if p == 0:
            for move in fetched_rows:
                move.wait()
        if turn >= 2:
            twin[turn - 2][p].wait_send()
        back(0, p, twin_out.at[turn % 2])
        twin[turn][p].start()
        back(1, p, keep)
        if p == 1 and turn < 3:
            for part in range(2):
                fetched_rows[part] = fetch_rows(turn + 1, part)
                fetched_rows[part].start()

    def pass_half(turn, p):
        twin[turn][p].wait_recv()
        if turn in (1, 2):
            ring[turn - 1][p].wait_recv()

        @pl.loop(0, 2)
        def _(i):
            quarter = tokens // 4
            span = pl.ds(pl.multiple_of(p * half + i * quarter, quarter), quarter)
            sum_ = keep[span, :] + twin_in[turn, span, :].astype(jnp.float32)
            if turn in (1, 2):
                sum_ = sum_ + ring_in[turn - 1, span, :].astype(jnp.float32)
            if turn < 3:
                ring_out[turn, span, :] = sum_.astype(jnp.bfloat16)
            else:
                keep[span, :] = sum_

        if turn < 3:
            ring[turn][p].start()

    def weight_block(flip):
        slot = flip % 2
        fetched[slot].wait()

        @pl.loop(0, rows // BLOCK)
        def _(i):
            span = pl.ds(pl.multiple_of(i * BLOCK, BLOCK), BLOCK)
            turned = tokens_buf[slot, :, span].T
            for k in range(3):
                term = jnp.dot(turned, grads[flip, k], preferred_element_type=jnp.float32)
                total[k, span, :] = term if flip == 0 else total[k, span, :] + term

        if flip < 2:
            fetched[slot] = fetch_tokens(flip + 2)
            fetched[slot].start()

    def weight_rest(i, part):
        slot = 3 % 2
        if i == 0 and part == 0:
            fetched[slot].wait()
        tops = [top + i * part_rows for top in (0, half)]

        @pl.loop(0, cols // BLOCK)
        def _(j):
            top = pl.multiple_of(j * BLOCK, BLOCK)
            span = pl.ds(pl.multiple_of(part * cols + top, BLOCK), BLOCK)
            turned = [tokens_buf[slot, pl.ds(t, part_rows), span].T for t in tops]
            for k in range(3):
                term = total[k, span, :]
                for t, rows_of in zip(tops, turned):
                    term = term + jnp.dot(
                        rows_of, grads[3, k, pl.ds(t, part_rows)], preferred_element_type=jnp.float32
                    )
                if i == 0:
                    total[k, span, :] = term
                else:
                    rows_buf[part, k, pl.ds(top, BLOCK), :] = term.astype(jnp.bfloat16)

    for p in range(2):
        input_half(0, p)
        pass_half(0, p)
    for p in range(2):
        input_half(1, p)
    weight_block(0)
    side[0].wait_recv()
    side[1].wait_recv()
    for moves in far:
        for move in moves:
            move.start()
    for p in range(2):
        pass_half(1, p)
    for p in range(2):
        input_half(2, p)
    side[2].wait_recv()
    weight_block(1)
    for p in range(2):
        pass_half(2, p)
    for p in range(2):
        input_half(3, p)
        pass_half(3, p)
    keep_copy = pltpu.make_async_copy(keep, keep_out, local.at[6])
    keep_copy.start()
    side[3].wait_recv()
    weight_block(2)
    stores = [
        pltpu.make_async_copy(
            rows_buf.at[part], weight_out.at[:, pl.ds(part * cols, cols)], local.at[part]
        )
        for part in range(2)
    ]
    for i in range(2):
        for move in far[i]:
            move.wait_recv()
        for part in range(2):
            weight_rest(i, part)
            if i == 1:
                stores[part].start()
    for move in ring[2]:
        move.wait_recv()
    for move in (keep_copy, *stores):
        move.wait()
    for moves in (side, *far, *ring, twin[2], twin[3]):
        for move in moves:
            move.wait_send()


def close_kernel(keep_ref, last_ref, rows_ref, input_ref, weight_ref):
    input_ref[...] = (keep_ref[...] + last_ref[...].astype(jnp.float32)).astype(jnp.bfloat16)
    weight_ref[...] = rows_ref[...]


def close_call(keep, last, weight):
    (tokens, cols), (_, rows, local_cols) = keep.shape, weight.shape
    steps = 8
    input_spec = pl.BlockSpec((tokens // steps, cols), lambda i: (i, 0))
    weight_spec = pl.BlockSpec((3, rows // steps, local_cols), lambda i: (0, i, 0))
    return pl.pallas_call(
        close_kernel,
        grid=(steps,),
        in_specs=[input_spec, input_spec, weight_spec],
        out_specs=[input_spec, weight_spec],
        out_shape=[
            jax.ShapeDtypeStruct(keep.shape, jnp.bfloat16),
            jax.ShapeDtypeStruct(weight.shape, weight.dtype),
        ],
        compiler_params=pltpu.CompilerParams(vmem_limit_bytes=62 << 20),
        name="close",
    )(keep, last, weight)


def finish_call(gradient, feats, wall, swap):
    _, tokens, local_cols = gradient.shape
    rows = wall.shape[2]
    cols = rows // 2
    bf16, f32 = jnp.bfloat16, jnp.float32
    anywhere = pl.BlockSpec(memory_space=pl.ANY)
    return pl.pallas_call(
        finish_kernel,
        in_specs=[anywhere] * 4,
        out_specs=[anywhere] * 3,
        out_shape=[
            jax.ShapeDtypeStruct((tokens, cols), f32),
            jax.ShapeDtypeStruct((tokens, cols), bf16),
            jax.ShapeDtypeStruct((3, rows, local_cols), bf16),
        ],
        scratch_shapes=[
            pltpu.VMEM((4, 3, tokens, local_cols), bf16),
            pltpu.VMEM((2, tokens, rows), bf16),
            pltpu.VMEM((2, 3, cols, local_cols), bf16),
            pltpu.VMEM((3, rows, local_cols), f32),
            pltpu.VMEM((tokens, cols), f32),
            pltpu.VMEM((2, tokens, cols), bf16),
            pltpu.VMEM((4, tokens, cols), bf16),
            pltpu.VMEM((3, tokens, cols), bf16),
            pltpu.VMEM((2, tokens, cols), bf16),
            pltpu.SemaphoreType.DMA((22,)),
            pltpu.SemaphoreType.DMA((22,)),
            pltpu.SemaphoreType.DMA((7,)),
        ],
        compiler_params=pltpu.CompilerParams(
            collective_id=1, has_side_effects=True, vmem_limit_bytes=60 << 20
        ),
        name="finish",
    )(gradient, feats, wall, swap)


def fast_body(inputs, projection, cotangent, log_decay, document_starts):
    feats, wall, gradient, swap = gather_call(
        document_starts, log_decay, inputs, projection.transpose(1, 0, 2), cotangent
    )
    input_gradient, weight_gradient = close_call(*finish_call(gradient, feats, wall, swap))
    return (input_gradient, weight_gradient.transpose(1, 0, 2))


def solution(mesh):
    fast = (mesh.shape["seq"], mesh.shape["head"]) == (4, 8)
    placed = (P("seq", "head"), P("seq", None, "head"), P("seq", "head"), P("head", "seq"), P())
    return jax.shard_map(
        fast_body if fast else general_body,
        mesh=mesh,
        in_specs=placed,
        out_specs=(P("seq", "head"), P("seq", None, "head")),
        check_vma=False,
    )
```

```python
import jax
import jax.numpy as jnp
from jax import lax
from jax.experimental import pallas as pl
from jax.experimental.layout import Layout, with_layout_constraint
from jax.experimental.pallas import tpu as pltpu
from jax.sharding import PartitionSpec as P

HEAD_DIM = 128
BLOCK = 256


def hop(array, axis, flip):
    return lax.ppermute(array, axis, [(i, i ^ flip) for i in range(lax.axis_size(axis))])


def gather_states(packed, axis):
    length, place = (lax.axis_size(axis), lax.axis_index(axis))
    if length != 4:
        whole = lax.all_gather(packed, axis)
        return [whole[k] for k in range(length)], jnp.arange(length, dtype=jnp.int32)
    parts = [packed] + [hop(packed, axis, flip) for flip in range(1, length)]
    return parts, place ^ jnp.arange(length, dtype=jnp.int32)


def device_weights(device_decay, owners, axis):
    length, place = (lax.axis_size(axis), lax.axis_index(axis))
    if length == 4:
        slab = jnp.broadcast_to(device_decay[:, None], (device_decay.shape[0], HEAD_DIM))
        hops = [slab] + [hop(slab, axis, flip) for flip in range(1, length)]
        arrived = jnp.stack([part[:, 0] for part in hops])
        mine = owners[None, :] == jnp.arange(length, dtype=jnp.int32)[:, None]
        decays = jnp.sum(jnp.where(mine[:, :, None], arrived[None], 0.0), axis=1)
    else:
        decays = lax.all_gather(device_decay, axis)
    at, other = owners[:, None], jnp.arange(length, dtype=jnp.int32)[None]
    before = (other > at) & (other < place)
    after = (other < at) & (other > place)
    weights = []
    for between, counts in ((before, owners < place), (after, owners > place)):
        product = jnp.prod(jnp.where(between[:, :, None], decays[None], 1.0), axis=1)
        weights.append(jnp.where(counts[:, None], product, 0.0))
    return jnp.stack(weights)


def gather_rows(part, axis):
    length, place, rows = (lax.axis_size(axis), lax.axis_index(axis), part.shape[1])
    if length != 4:
        whole = lax.all_gather(part, axis, axis=1, tiled=True)
        return [(0, 0, whole)]
    half = rows // 2
    low, high = part[:, :half], part[:, half:]
    x_high = hop(high, axis, 1)
    y_low = hop(low, axis, 2)
    x_low = hop(low, axis, 1)
    y_high = hop(high, axis, 2)
    d_low = hop(y_low, axis, 1)
    d_high = hop(x_high, axis, 2)
    return [
        (place, 0, low),
        (place, half, high),
        (place ^ 1, half, x_high),
        (place ^ 2, 0, y_low),
        (place ^ 1, 0, x_low),
        (place ^ 2, half, y_high),
        (place ^ 3, 0, d_low),
        (place ^ 3, half, d_high),
    ]


def scatter_rows(partial, between, source, axis, rows):
    length, place = (lax.axis_size(axis), lax.axis_index(axis))
    if length != 4:
        whole = partial(source, 0, 0, rows * length)
        return [between(source, 0, 1)], lax.psum_scatter(whole, axis, scatter_dimension=1, tiled=True)
    half = rows // 2

    def add(*terms):
        return sum(term.astype(jnp.float32) for term in terms).astype(jnp.bfloat16)

    far_low, far_high = partial(source, place ^ 3, 0, half), partial(source, place ^ 3, half, half)
    source, far_low, far_high = lax.optimization_barrier((source, far_low, far_high))
    far_low, far_high = hop(far_low, axis, 1), hop(far_high, axis, 2)
    beside = between(source, 0, 1)
    source, beside = lax.optimization_barrier((source, beside))
    x_low, y_high = partial(source, place ^ 1, 0, half), partial(source, place ^ 2, half, half)
    source, x_low, y_high = lax.optimization_barrier((source, x_low, y_high))
    x_low, y_high = hop(x_low, axis, 1), hop(y_high, axis, 2)
    x_high = hop(add(partial(source, place ^ 1, half, half), far_high), axis, 1)
    y_low = hop(add(partial(source, place ^ 2, 0, half), far_low), axis, 2)
    own_low, own_high = partial(source, place, 0, half), partial(source, place, half, half)
    whole = jnp.concatenate([add(own_low, x_low, y_low), add(own_high, x_high, y_high)], axis=1)
    return [beside], whole


def running_sum(values):
    inside = jnp.arange(values.shape[-1], dtype=jnp.int32)
    triangle = (inside[:, None] <= inside[None, :]).astype(jnp.float32)
    return jnp.einsum("hbu,ut->hbt", values, triangle, precision=lax.Precision.HIGHEST)


def block_factors(decay_sum, doc_index, doc_begin):
    inside = jnp.arange(doc_index.shape[-1], dtype=jnp.int32)
    causal = inside[:, None] >= inside[None, :]
    same_doc = (doc_index[:, :, None] == doc_index[:, None, :]) & causal[None]
    spread = jnp.minimum(decay_sum[..., :, None] - decay_sum[..., None, :], 0.0)
    pair_weight = jnp.where(same_doc[None], jnp.exp(spread), 0.0)
    to_end = jnp.where(
        (doc_index == doc_index[:, -1:])[None], jnp.exp(decay_sum[..., -1:] - decay_sum), 0.0
    )
    began_flag = doc_index == doc_index[:, :1] - doc_begin[:, :1]
    from_start = jnp.where(began_flag[None], jnp.exp(decay_sum), 0.0)
    return (pair_weight, to_end, from_start, from_start[..., -1])


def dot(left, right, contract):
    return lax.dot_general(
        left, right, ((contract[:1], contract[1:]), ((), ())), preferred_element_type=jnp.float32
    )


def projections(proj_ref, span):
    point_q, point_k = proj_ref[0, span], proj_ref[1, span]
    gate_q, gate_k = jax.nn.sigmoid(point_q), jax.nn.sigmoid(point_k)
    queries = (point_q * gate_q * HEAD_DIM ** (-0.5)).astype(jnp.bfloat16)
    keys = (point_k * gate_k).astype(jnp.bfloat16)
    values = proj_ref[2, span].astype(jnp.bfloat16)
    return (point_q, gate_q, queries), (point_k, gate_k, keys), values


def state_kernel(proj_ref, up_ref, start_ref, end_ref, key_ref, query_ref, total_ref):
    blocks = key_ref.shape[1]
    forward = jnp.zeros((HEAD_DIM, HEAD_DIM), jnp.float32)
    query_states, decays = [], []
    for b in range(blocks):
        span = pl.ds(b * BLOCK, BLOCK)
        (_, _, queries), (_, _, keys), values = projections(proj_ref, span)
        keys_weighted = (keys.astype(jnp.float32) * end_ref[0, span]).astype(jnp.bfloat16)
        queries_weighted = (queries.astype(jnp.float32) * start_ref[0, span]).astype(jnp.bfloat16)
        key_state = dot(keys_weighted, values, (0, 0))
        query_state = dot(queries_weighted, up_ref[span], (0, 0))
        key_ref[0, b] = key_state
        query_ref[0, b] = query_state
        decay = start_ref[0, pl.ds(b * BLOCK + BLOCK - 1, 1)]
        forward = decay * forward + key_state
        query_states.append(query_state)
        decays.append(decay)
    backward = jnp.zeros((HEAD_DIM, HEAD_DIM), jnp.float32)
    for b in reversed(range(blocks)):
        backward = decays[b] * backward + query_states[b]
    total_ref[0, 0] = forward.astype(jnp.bfloat16)
    total_ref[1, 0] = backward.astype(jnp.bfloat16)


def gradient_kernel(
    weight_ref, proj_ref, up_ref, start_ref, end_ref, pair_ref, key_ref, query_ref, *rest
):
    totals, out_ref = rest[:-1], rest[-1]
    blocks = key_ref.shape[1]
    head = pl.program_id(0)
    state = jnp.zeros((HEAD_DIM, HEAD_DIM), jnp.float32)
    reverse = jnp.zeros((HEAD_DIM, HEAD_DIM), jnp.float32)
    for k, total in enumerate(totals):
        state = state + weight_ref[0, k, head] * total[0, 0].astype(jnp.float32)
        reverse = reverse + weight_ref[1, k, head] * total[1, 0].astype(jnp.float32)
    decays = [start_ref[0, pl.ds(b * BLOCK + BLOCK - 1, 1)] for b in range(blocks)]
    after = [None] * blocks
    for b in reversed(range(blocks)):
        after[b] = reverse.astype(jnp.bfloat16)
        reverse = decays[b] * reverse + query_ref[0, b]
    for b in range(blocks):
        before = state.astype(jnp.bfloat16)
        state = decays[b] * state + key_ref[0, b]
        span = pl.ds(b * BLOCK, BLOCK)
        (point_q, gate_q, queries), (point_k, gate_k, keys), values = projections(proj_ref, span)
        upstream = up_ref[span]
        from_start, to_end, pair = start_ref[0, span], end_ref[0, span], pair_ref[0, b]
        query_key = (dot(queries, keys, (1, 1)) * pair).astype(jnp.bfloat16)
        value_score = (dot(upstream, values, (1, 1)) * pair).astype(jnp.bfloat16)
        query_gradient = dot(value_score, keys, (1, 0)) + from_start * dot(
            upstream, before, (1, 1)
        )
        key_gradient = dot(value_score, queries, (0, 0)) + to_end * dot(values, after[b], (1, 1))
        value_gradient = dot(query_key, upstream, (0, 0)) + to_end * dot(keys, after[b], (1, 0))
        slope_q = gate_q * (1.0 + point_q * (1.0 - gate_q)) * HEAD_DIM ** (-0.5)
        slope_k = gate_k * (1.0 + point_k * (1.0 - gate_k))
        out_ref[0, span] = (query_gradient * slope_q).astype(jnp.bfloat16)
        out_ref[1, span] = (key_gradient * slope_k).astype(jnp.bfloat16)
        out_ref[2, span] = value_gradient.astype(jnp.bfloat16)


def input_kernel(gradient_ref, weight_ref, out_ref):
    for first in range(0, out_ref.shape[0], BLOCK):
        span = pl.ds(first, BLOCK)
        total = dot(gradient_ref[0, span], weight_ref[0], (1, 1))
        for k in (1, 2):
            total = total + dot(gradient_ref[k, span], weight_ref[k], (1, 1))
        out_ref[span] = total.astype(jnp.bfloat16)


def general_body(inputs, projection, cotangent, log_decay, document_starts):
    tokens = inputs.shape[0]
    heads_here = log_decay.shape[0]
    local_cols = cotangent.shape[1]
    blocks = tokens // BLOCK
    features = lax.all_gather(inputs, "head", axis=1, tiled=True)
    rows = projection.shape[0]
    blocks_w = gather_rows(projection.transpose(1, 0, 2), "seq")

    def feature_rows(owner, first, count):
        return lax.dynamic_slice_in_dim(features, owner * rows + first, count, axis=1)

    offset = lax.axis_index("seq") * tokens
    positions = offset + jnp.arange(tokens, dtype=jnp.int32)
    doc_index = (
        jnp.sum((document_starts[None, :] <= positions[:, None]).astype(jnp.int32), axis=1) - 1
    )
    doc_begin = jnp.any(document_starts[None, :] == positions[:, None], axis=1).astype(jnp.int32)
    decay_sum = running_sum(log_decay.reshape(heads_here, blocks, BLOCK))
    pair_weight, to_end, from_start, block_decay = block_factors(
        decay_sum, doc_index.reshape(blocks, BLOCK), doc_begin.reshape(blocks, BLOCK)
    )
    lanes = (heads_here, tokens, HEAD_DIM)
    to_end = jnp.broadcast_to(to_end.reshape(heads_here, tokens)[..., None], lanes)
    from_start = jnp.broadcast_to(from_start.reshape(heads_here, tokens)[..., None], lanes)
    device_decay = jnp.prod(block_decay, axis=1)

    zero = jnp.zeros((), jnp.bfloat16)
    if len(blocks_w) > 2:
        owner, first, block = blocks_w[2]
        zero, block = lax.optimization_barrier((zero, block))
        blocks_w[2] = (owner, first, block)
    weights_all = jnp.broadcast_to(zero, (3, features.shape[1], local_cols))

    def place_rows(whole, some):
        for owner, first, block in some:
            whole = lax.dynamic_update_slice_in_dim(whole, block, owner * rows + first, axis=1)
        return whole

    early, late = blocks_w[:6], blocks_w[6:]
    weights_all = place_rows(weights_all, early)
    features, weights_all, from_start, to_end, pair_weight = lax.optimization_barrier(
        (features, weights_all, from_start, to_end, pair_weight)
    )
    projected = None
    for k, (owner, first, block) in enumerate(blocks_w):
        piece = jnp.einsum(
            "td,kdc->ktc",
            feature_rows(owner, first, block.shape[1]),
            block,
            preferred_element_type=jnp.float32,
        )
        projected = piece if projected is None else lax.optimization_barrier(projected) + piece
        if k == min(5, len(blocks_w) - 1):
            projected, device_decay = lax.optimization_barrier((projected, device_decay))
    weights_all = place_rows(weights_all, late)

    proj_spec = pl.BlockSpec((3, tokens, HEAD_DIM), lambda h: (0, 0, h))
    up_spec = pl.BlockSpec((tokens, HEAD_DIM), lambda h: (0, h))
    lane_spec = pl.BlockSpec((1, tokens, HEAD_DIM), lambda h: (h, 0, 0))
    state_spec = pl.BlockSpec((1, blocks, HEAD_DIM, HEAD_DIM), lambda h: (h, 0, 0, 0))
    total_spec = pl.BlockSpec((2, 1, HEAD_DIM, HEAD_DIM), lambda h: (0, h, 0, 0))
    pair_spec = pl.BlockSpec((1, blocks, BLOCK, BLOCK), lambda h: (h, 0, 0, 0))
    states = jax.ShapeDtypeStruct((heads_here, blocks, HEAD_DIM, HEAD_DIM), jnp.float32)
    key_state, query_state, totals = pl.pallas_call(
        state_kernel,
        grid=(heads_here,),
        in_specs=[proj_spec, up_spec, lane_spec, lane_spec],
        out_specs=[state_spec, state_spec, total_spec],
        out_shape=[
            states,
            states,
            jax.ShapeDtypeStruct((2, heads_here, HEAD_DIM, HEAD_DIM), jnp.bfloat16),
        ],
    )(projected, cotangent, from_start, to_end)
    parts, owners = gather_states(totals, "seq")
    weights = device_weights(device_decay, owners, "seq")
    project_gradient = pl.pallas_call(
        gradient_kernel,
        grid=(heads_here,),
        in_specs=[pl.BlockSpec(memory_space=pltpu.SMEM)]
        + [proj_spec, up_spec, lane_spec, lane_spec, pair_spec, state_spec, state_spec]
        + [total_spec] * len(parts),
        out_specs=proj_spec,
        out_shape=jax.ShapeDtypeStruct(projected.shape, jnp.bfloat16),
    )(weights, projected, cotangent, from_start, to_end, pair_weight, key_state, query_state, *parts)

    def weight_partial(gradient, owner, first, count):
        term = jnp.einsum(
            "td,ktc->kdc",
            feature_rows(owner, first, count),
            gradient,
            preferred_element_type=jnp.float32,
        ).astype(jnp.bfloat16)
        return with_layout_constraint(term, Layout(major_to_minor=(0, 1, 2)))

    def input_partial(gradient, part, of):
        columns = features.shape[1]
        tile, count = columns // 8, tokens // of
        return pl.pallas_call(
            input_kernel,
            grid=(columns // tile,),
            in_specs=[
                pl.BlockSpec((3, count, local_cols), lambda i: (0, part, 0)),
                pl.BlockSpec((3, tile, local_cols), lambda i: (0, i, 0)),
            ],
            out_specs=pl.BlockSpec((count, tile), lambda i: (0, i)),
            out_shape=jax.ShapeDtypeStruct((count, columns), jnp.bfloat16),
            cost_estimate=pl.CostEstimate(flops=1, bytes_accessed=1, transcendentals=0),
            compiler_params=pltpu.CompilerParams(vmem_limit_bytes=40 << 20),
        )(gradient, weights_all)

    input_partials, weight_gradient = scatter_rows(
        weight_partial, input_partial, project_gradient, "seq", rows
    )
    input_gradient = lax.psum_scatter(
        input_partials[0], "head", scatter_dimension=1, tiled=True
    )
    weight_gradient = weight_gradient.transpose(1, 0, 2)
    return (input_gradient, weight_gradient)


MESH = pl.DeviceIdType.MESH
PAIR = 2 * HEAD_DIM


def remote_maker(send, recv):
    def remote(index, source, target, device):
        return pltpu.make_async_remote_copy(
            src_ref=source,
            dst_ref=target,
            send_sem=send.at[index],
            recv_sem=recv.at[index],
            device_id=device,
            device_id_type=MESH,
        )

    return remote


def greet(others):
    barrier = pltpu.get_barrier_semaphore()
    for other in others:
        pl.semaphore_signal(barrier, inc=1, device_id=other, device_id_type=MESH)
    pl.semaphore_wait(barrier, len(others))


def gather_kernel(
    starts_ref, log_ref, x_ref, w_ref, up_ref, feats_out, wall_out, grads_out, swap,
    feats, wall, total, grads, upper, decay_rows, decay_cols, decays_out, decays_in, states,
    sums_out, sums_in, send, recv, local,
):
    place, head = lax.axis_index("seq"), lax.axis_index("head")
    z, core = head // 2, head % 2
    tokens, cols = x_ref.shape
    rows = w_ref.shape[1]
    half, near, chunk = tokens // 2, rows // 2, tokens // 8
    blocks = tokens // BLOCK
    x_id, y_id, far_id = (place ^ 1, head), (place ^ 2, head), (place ^ 3, head)
    next_id, last_id = (place, (head + 2) % 8), (place, (head + 6) % 8)
    twin_id = (place, head ^ 1)
    mine = pl.ds(pl.multiple_of(core * cols, cols), cols)
    remote = remote_maker(send, recv)

    own_w = pltpu.make_async_copy(w_ref, wall.at[place], local.at[0])
    own_x = pltpu.make_async_copy(x_ref, feats.at[z, :, mine], local.at[1])
    own_up = pltpu.make_async_copy(up_ref, upper, local.at[8])
    own_w.start()
    own_x.start()
    own_up.start()

    def block(step, part):
        return feats.at[(z + 4 - step) % 4, pl.ds(part * half, half), mine]

    def x_part(step, part):
        return x_ref.at[pl.ds(part * half, half)] if step == 0 else block(step, part)

    ring = [
        [remote(2 * k + p, x_part(k, p), block(k, p), next_id) for p in range(2)] for k in range(3)
    ]
    twin = [
        [remote(6 + 2 * k + p, x_part(k, p), block(k, p), twin_id) for p in range(2)]
        for k in range(4)
    ]
    low, high = pl.ds(0, near), pl.ds(near, near)
    side = [
        remote(14 + i, w_ref.at[:, part], wall.at[place, :, part], device)
        for i, (part, device) in enumerate(((high, x_id), (low, y_id), (low, x_id), (high, y_id)))
    ]

    def patch(owner, top, count, pair):
        return wall.at[owner, :, pl.ds(top, count), pl.ds(pair * PAIR, PAIR)]

    def forward(index, top, count, pair):
        first, second = patch(place ^ 2, top, count, pair), patch(place ^ 1, near + top, count, pair)
        return [remote(index, first, first, x_id), remote(index + 1, second, second, y_id)]

    part = near // 2
    filler = near // 3
    far = [
        forward(18, 0, filler, 0),
        forward(20, filler, near - filler, 0),
        forward(22, 0, part, 1),
        forward(24, part, part, 1),
    ]

    def share(who):
        return pl.ds(pl.multiple_of(who * chunk, chunk), chunk)

    others = ((1, x_id), (2, y_id), (3, far_id))
    mix = [
        remote(25 + flip, feats.at[place ^ flip, share(head)], swap.at[flip - 1, share(head)], device)
        for flip, device in others
    ]

    def shared(step):
        return swap.at[:, share((head + 8 - 2 * step) % 8)]

    ringed = chunk * 5 // 8

    def ring_rows(step):
        top = pl.multiple_of((head + 8 - 2 * step) % 8 * chunk, chunk)
        return pl.ds(top, chunk if step < 2 else ringed)

    spread = [
        [
            remote(
                29 + 3 * k + flip, swap.at[flip, ring_rows(k)], swap.at[flip, ring_rows(k)], next_id
            )
            for flip in range(3)
        ]
        for k in range(3)
    ]
    spread_twin = [remote(38 + k, shared(k), shared(k), twin_id) for k in range(4)]
    direct_rows = pl.ds(
        pl.multiple_of((head + 2) % 8 * chunk + ringed, chunk // 8), chunk - ringed
    )
    direct = [
        remote(41 + flip, feats.at[place ^ flip, direct_rows], swap.at[flip - 1, direct_rows], device)
        for flip, device in others
    ]
    decays = [
        remote(44 + flip, decays_out, decays_in.at[flip - 1], device) for flip, device in others
    ]
    way = (place % 2, place // 2, place // 2)
    sums = [
        [
            remote(
                47 + 3 * pair + flip, sums_out.at[way[flip - 1], pl.ds(2 * pair, 2)],
                sums_in.at[flip - 1, pl.ds(2 * pair, 2)], device,
            )
            for flip, device in others
        ]
        for pair in range(2)
    ]

    greet((x_id, y_id, far_id, next_id, last_id, twin_id))
    ring[0][0].start()
    side[0].start()
    side[1].start()
    ring[0][1].start()
    twin[0][0].start()
    twin[0][1].start()

    def arrived(step, part):
        ring[step][part].wait_recv()
        if step < 2:
            ring[step + 1][part].start()
        twin[step + 1][part].start()

    def multiply(owner, pair, begin, top, count):
        columns = pl.ds(pair * PAIR, PAIR)

        @pl.loop(0, 6)
        def _(i):
            k, span = i // 2, pl.ds(pl.multiple_of(i % 2 * half, half), half)
            term = jnp.dot(
                feats[owner, span, pl.ds(top, count)],
                wall[owner, k, pl.ds(top, count), columns],
                preferred_element_type=jnp.float32,
            )
            total[k, span, columns] = term if begin else total[k, span, columns] + term

    def documents(b, shape, axis):
        at = lax.broadcasted_iota(jnp.int32, shape, axis) + (place * tokens + b * BLOCK)
        return sum((starts_ref[i] <= at).astype(jnp.int32) for i in range(starts_ref.shape[0]))

    def factors(b, lane):
        span = pl.ds(b * BLOCK, BLOCK)
        decay, doc = decay_cols[span, lane], documents(b, (BLOCK, HEAD_DIM), 0)
        last = decay_cols[pl.ds(b * BLOCK + BLOCK - 1, 1), lane]
        first, final = 0, 0
        top = place * tokens + b * BLOCK
        for i in range(starts_ref.shape[0]):
            first = first + (starts_ref[i] < top).astype(jnp.int32)
            final = final + (starts_ref[i] <= top + (BLOCK - 1)).astype(jnp.int32)
        from_start = jnp.where(doc == first, jnp.exp(decay), 0.0)
        to_end = jnp.where(doc == final, jnp.exp(last - decay), 0.0)
        return decay, doc, from_start, to_end

    def project(b, lane):
        span = pl.ds(b * BLOCK, BLOCK)
        point_q, point_k = total[0, span, lane], total[1, span, lane]
        gate_q, gate_k = jax.nn.sigmoid(point_q), jax.nn.sigmoid(point_k)
        queries = (point_q * gate_q * HEAD_DIM ** (-0.5)).astype(jnp.bfloat16)
        keys = (point_k * gate_k).astype(jnp.bfloat16)
        values = total[2, span, lane].astype(jnp.bfloat16)
        return (point_q, gate_q, queries), (point_k, gate_k, keys), values

    def summarize(pair):
        @pl.loop(0, 2)
        def _(i):
            h = 2 * pair + i
            lane = pl.ds(pl.multiple_of(h * HEAD_DIM, HEAD_DIM), HEAD_DIM)
            forward = jnp.zeros((HEAD_DIM, HEAD_DIM), jnp.float32)
            query_states, decays = [], []
            for b in range(blocks):
                _, _, from_start, to_end = factors(b, lane)
                (_, _, queries), (_, _, keys), values = project(b, lane)
                weighted = (keys.astype(jnp.float32) * to_end).astype(jnp.bfloat16)
                key_state = dot(weighted, values, (0, 0))
                weighted = (queries.astype(jnp.float32) * from_start).astype(jnp.bfloat16)
                upstream = upper[pl.ds(b * BLOCK, BLOCK), lane]
                query_state = dot(weighted, upstream, (0, 0))
                states[0, h, b] = key_state
                states[1, h, b] = query_state
                decay = from_start[BLOCK - 1 :]
                forward = decay * forward + key_state
                query_states.append(query_state)
                decays.append(decay)
            backward = jnp.zeros((HEAD_DIM, HEAD_DIM), jnp.float32)
            for b in reversed(range(blocks)):
                backward = decays[b] * backward + query_states[b]
            sums_out[0, h] = forward.astype(jnp.bfloat16)
            sums_out[1, h] = backward.astype(jnp.bfloat16)

        for move in sums[pair]:
            move.start()

    def differentiate(pair):
        for move in sums[pair]:
            move.wait_recv()

        @pl.loop(0, 2)
        def _(i):
            h = 2 * pair + i
            lane = pl.ds(pl.multiple_of(h * HEAD_DIM, HEAD_DIM), HEAD_DIM)
            state = jnp.zeros((HEAD_DIM, HEAD_DIM), jnp.float32)
            reverse = jnp.zeros((HEAD_DIM, HEAD_DIM), jnp.float32)
            for flip in (1, 2, 3):
                owner = place ^ flip
                share = jnp.ones((1, HEAD_DIM), jnp.float32)
                for other in (1, 2, 3):
                    if other != flip:
                        at = place ^ other
                        between = ((at > owner) & (at < place)) | ((at < owner) & (at > place))
                        share = jnp.where(between, decays_in[other - 1, pl.ds(h, 1)] * share, share)
                came = share * sums_in[flip - 1, h].astype(jnp.float32)
                state = jnp.where(owner < place, state + came, state)
                reverse = jnp.where(owner > place, reverse + came, reverse)
            decays = [factors(b, lane)[2][BLOCK - 1 :] for b in range(blocks)]
            behind = [None] * blocks
            for b in reversed(range(blocks)):
                behind[b] = reverse.astype(jnp.bfloat16)
                reverse = decays[b] * reverse + states[1, h, b]
            for b in range(blocks):
                before = state.astype(jnp.bfloat16)
                state = decays[b] * state + states[0, h, b]
                span = pl.ds(b * BLOCK, BLOCK)
                decay, doc, from_start, to_end = factors(b, lane)
                gap = jnp.minimum(
                    jnp.concatenate([decay, decay], axis=1) - decay_rows[pl.ds(h, 1), span], 0.0
                )
                rows_at = lax.broadcasted_iota(jnp.int32, (BLOCK, BLOCK), 0)
                cols_at = lax.broadcasted_iota(jnp.int32, (BLOCK, BLOCK), 1)
                same = jnp.concatenate([doc, doc], axis=1) == documents(b, (1, BLOCK), 1)
                pair_weight = jnp.where(same & (rows_at >= cols_at), jnp.exp(gap), 0.0)
                (point_q, gate_q, queries), (point_k, gate_k, keys), values = project(b, lane)
                upstream = upper[span, lane]
                query_key = (dot(queries, keys, (1, 1)) * pair_weight).astype(jnp.bfloat16)
                value_score = (dot(upstream, values, (1, 1)) * pair_weight).astype(jnp.bfloat16)
                query_gradient = dot(value_score, keys, (1, 0)) + from_start * dot(
                    upstream, before, (1, 1)
                )
                key_gradient = dot(value_score, queries, (0, 0)) + to_end * dot(
                    values, behind[b], (1, 1)
                )
                value_gradient = dot(query_key, upstream, (0, 0)) + to_end * dot(
                    keys, behind[b], (1, 0)
                )
                slope_q = gate_q * (1.0 + point_q * (1.0 - gate_q)) * HEAD_DIM ** (-0.5)
                slope_k = gate_k * (1.0 + point_k * (1.0 - gate_k))
                grads[0, span, lane] = (query_gradient * slope_q).astype(jnp.bfloat16)
                grads[1, span, lane] = (key_gradient * slope_k).astype(jnp.bfloat16)
                grads[2, span, lane] = value_gradient.astype(jnp.bfloat16)

    def prepare():
        before = lax.broadcasted_iota(jnp.int32, (BLOCK, BLOCK), 0) <= lax.broadcasted_iota(
            jnp.int32, (BLOCK, BLOCK), 1
        )
        triangle = before.astype(jnp.float32)
        heads = log_ref.shape[0]
        for b in range(tokens // BLOCK):
            span = pl.ds(b * BLOCK, BLOCK)
            sums_of = lax.dot_general(
                log_ref[:, span], triangle, (((1,), (0,)), ((), ())),
                precision=lax.Precision.HIGHEST, preferred_element_type=jnp.float32,
            )
            decay_rows[pl.ds(0, heads), span] = sums_of
            for h in range(heads):
                wide = jnp.broadcast_to(sums_of[h : h + 1], (HEAD_DIM, BLOCK))
                decay_cols[span, pl.ds(h * HEAD_DIM, HEAD_DIM)] = wide.T
        decays_out[...] = jnp.ones_like(decays_out)
        for h in range(heads):
            product = jnp.ones((1, HEAD_DIM), jnp.float32)
            for b in range(tokens // BLOCK):
                from_start = factors(b, pl.ds(h * HEAD_DIM, HEAD_DIM))[2]
                product = product * from_start[BLOCK - 1 :]
            decays_out[pl.ds(h, 1)] = product

    prepare()
    for move in decays:
        move.start()
    arrived(0, 0)
    arrived(0, 1)
    arrived(1, 0)
    side[0].wait_recv()
    side[1].wait_recv()
    for move in (side[2], side[3], *far[0]):
        move.start()
    arrived(1, 1)
    own_w.wait()
    own_x.wait()
    own_up.wait()
    arrived(2, 0)
    arrived(2, 1)
    for pair in twin:
        for move in pair:
            move.wait_recv()
    for move in (*mix, *far[1], *far[2]):
        move.start()
    feats_copy = pltpu.make_async_copy(feats.at[place], feats_out, local.at[2])
    feats_copy.start()
    multiply(place, 0, True, 0, rows)
    multiply(place, 1, True, 0, rows)
    for flip in range(2):
        mix[flip].wait_recv()
        spread[0][flip].start()
    side[2].wait_recv()
    side[3].wait_recv()
    multiply(place ^ 1, 0, False, 0, rows)
    multiply(place ^ 2, 0, False, 0, rows)
    mix[2].wait_recv()
    spread[0][2].start()
    spread_twin[0].start()
    multiply(place ^ 1, 1, False, 0, rows)
    multiply(place ^ 2, 1, False, 0, rows)
    near_copies = [
        pltpu.make_async_copy(wall.at[place ^ f], wall_out.at[place ^ f], local.at[3 + f])
        for f in range(3)
    ]
    for move in near_copies:
        move.start()
    for move in decays:
        move.wait_recv()
    def spread_on(step):
        for flip in range(3):
            spread[step][flip].wait_recv()
            spread[step + 1][flip].start()
        spread_twin[step + 1].start()

    for move in (*far[0], *far[1]):
        move.wait_recv()
    multiply(place ^ 3, 0, False, 0, rows)
    spread_on(0)
    summarize(0)
    for move in far[3]:
        move.start()
    for move in far[2]:
        move.wait_recv()
    multiply(place ^ 3, 1, False, 0, part)
    multiply(place ^ 3, 1, False, near, part)
    differentiate(0)
    spread_on(1)
    for move in far[3]:
        move.wait_recv()
    multiply(place ^ 3, 1, False, part, part)
    multiply(place ^ 3, 1, False, near + part, part)
    summarize(1)
    for move in direct:
        move.start()
    far_copy = pltpu.make_async_copy(wall.at[place ^ 3], wall_out.at[place ^ 3], local.at[6])
    far_copy.start()
    differentiate(1)
    grads_copy = pltpu.make_async_copy(grads, grads_out, local.at[7])
    grads_copy.start()
    for move in (*spread[2], *direct):
        move.wait_recv()
    spread_twin[3].start()
    for move in spread_twin:
        move.wait_recv()
    for move in (feats_copy, *near_copies, far_copy, grads_copy):
        move.wait()
    for moves in (*ring, *twin, side, *far, mix, *spread, spread_twin, direct, decays, *sums):
        for move in moves:
            move.wait_send()


def gather_call(starts, log_decay, inputs, weights, cotangent):
    (tokens, cols), (_, rows, local_cols) = inputs.shape, weights.shape
    bf16, f32 = jnp.bfloat16, jnp.float32
    blocks = tokens // BLOCK
    shapes = [
        ((tokens, 2 * cols), bf16),
        ((4, 3, rows, local_cols), bf16),
        ((3, tokens, local_cols), bf16),
        ((3, tokens, 2 * cols), bf16),
    ]
    buffers = [
        ((4, tokens, 2 * cols), bf16),
        ((4, 3, rows, local_cols), bf16),
        ((3, tokens, local_cols), f32),
        ((3, tokens, local_cols), bf16),
        ((tokens, local_cols), bf16),
        ((8, tokens), f32),
        ((tokens, local_cols), f32),
        ((8, HEAD_DIM), f32),
        ((3, 8, HEAD_DIM), f32),
        ((2, 4, blocks, HEAD_DIM, HEAD_DIM), f32),
        ((2, 4, HEAD_DIM, HEAD_DIM), bf16),
        ((3, 4, HEAD_DIM, HEAD_DIM), bf16),
    ]
    anywhere = pl.BlockSpec(memory_space=pl.ANY)
    return pl.pallas_call(
        gather_kernel,
        in_specs=[pl.BlockSpec(memory_space=pltpu.SMEM), pl.BlockSpec(memory_space=pltpu.VMEM)]
        + [anywhere] * 3,
        out_specs=[anywhere] * 4,
        out_shape=[jax.ShapeDtypeStruct(*shape) for shape in shapes],
        scratch_shapes=[pltpu.VMEM(*shape) for shape in buffers]
        + [
            pltpu.SemaphoreType.DMA((54,)),
            pltpu.SemaphoreType.DMA((54,)),
            pltpu.SemaphoreType.DMA((9,)),
        ],
        compiler_params=pltpu.CompilerParams(
            collective_id=0, has_side_effects=True, vmem_limit_bytes=58 << 20
        ),
        name="gather",
    )(starts, log_decay, inputs, weights, cotangent)


def finish_kernel(
    grad_ref, feats_ref, wall_ref, swap_ref, keep_out, last_out, weight_out,
    grads, tokens_buf, rows_buf, total, keep, twin_out, twin_in, ring_out, ring_in,
    send, recv, local,
):
    place, head = lax.axis_index("seq"), lax.axis_index("head")
    z, core = head // 2, head % 2
    _, tokens, local_cols = grad_ref.shape
    rows, cols = total.shape[1], keep.shape[1]
    half, chunk = tokens // 2, tokens // 8
    x_id, y_id = (place ^ 1, head), (place ^ 2, head)
    next_id, last_id = (place, (head + 2) % 8), (place, (head + 6) % 8)
    twin_id = (place, head ^ 1)
    remote = remote_maker(send, recv)
    low, high = pl.ds(0, half), pl.ds(half, half)

    def fetch_rows(turn, part):
        owner = (z + 7 - turn) % 4
        side = pl.multiple_of((core if part else 1 - core) * cols, cols)
        return pltpu.make_async_copy(
            wall_ref.at[owner, :, pl.ds(side, cols)], rows_buf.at[part], local.at[part]
        )

    def fetch_tokens(flip):
        source = feats_ref if flip == 0 else swap_ref.at[flip - 1]
        return pltpu.make_async_copy(source, tokens_buf.at[flip % 2], local.at[2 + flip])

    own = pltpu.make_async_copy(grad_ref, grads.at[0], local.at[6])
    own.start()
    fetched_rows = [fetch_rows(0, 0), fetch_rows(0, 1)]
    for move in fetched_rows:
        move.start()
    fetched = [fetch_tokens(0), fetch_tokens(1)]
    for move in fetched:
        move.start()
    side = [
        remote(i, grad_ref.at[:, part], grads.at[flip, :, part], device)
        for i, (part, flip, device) in enumerate(
            ((high, 1, x_id), (low, 2, y_id), (low, 1, x_id), (high, 2, y_id))
        )
    ]
    part_rows = half // 2
    far = [
        [
            remote(
                4 + 2 * i + j, grads.at[flip, :, pl.ds(top + i * part_rows, part_rows)],
                grads.at[3, :, pl.ds(top + i * part_rows, part_rows)], device,
            )
            for j, (flip, top, device) in enumerate(((2, 0, x_id), (1, half, y_id)))
        ]
        for i in range(2)
    ]
    twin = [
        [
            remote(8 + 2 * k + p, twin_out.at[k % 2, part], twin_in.at[k, part], twin_id)
            for p, part in enumerate((low, high))
        ]
        for k in range(4)
    ]
    ring = [
        [
            remote(
                16 + 2 * k + p, ring_out.at[k, part],
                ring_in.at[k, part] if k < 2 else last_out.at[part], next_id,
            )
            for p, part in enumerate((low, high))
        ]
        for k in range(3)
    ]
    greet((x_id, y_id, next_id, last_id, twin_id))
    for move in side:
        move.start()
    own.wait()

    def back(part, p, target):
        @pl.loop(0, 2)
        def _(i):
            quarter = tokens // 4
            span = pl.ds(pl.multiple_of(p * half + i * quarter, quarter), quarter)
            term = None
            for k in range(3):
                piece = dot(grads[0, k, span, :], rows_buf[part, k], (1, 1))
                term = piece if term is None else term + piece
            target[span, :] = term.astype(target.dtype)

    def input_half(turn, p):
        if p == 0:
            for move in fetched_rows:
                move.wait()
        if turn >= 2:
            twin[turn - 2][p].wait_send()
        back(0, p, twin_out.at[turn % 2])
        twin[turn][p].start()
        back(1, p, keep)
        if p == 1 and turn < 3:
            for part in range(2):
                fetched_rows[part] = fetch_rows(turn + 1, part)
                fetched_rows[part].start()

    def pass_half(turn, p):
        twin[turn][p].wait_recv()
        if turn in (1, 2):
            ring[turn - 1][p].wait_recv()

        @pl.loop(0, 2)
        def _(i):
            quarter = tokens // 4
            span = pl.ds(pl.multiple_of(p * half + i * quarter, quarter), quarter)
            sum_ = keep[span, :] + twin_in[turn, span, :].astype(jnp.float32)
            if turn in (1, 2):
                sum_ = sum_ + ring_in[turn - 1, span, :].astype(jnp.float32)
            if turn < 3:
                ring_out[turn, span, :] = sum_.astype(jnp.bfloat16)
            else:
                keep[span, :] = sum_

        if turn < 3:
            ring[turn][p].start()

    def weight_block(flip):
        slot = flip % 2
        fetched[slot].wait()

        @pl.loop(0, rows // BLOCK)
        def _(i):
            span = pl.ds(pl.multiple_of(i * BLOCK, BLOCK), BLOCK)
            turned = tokens_buf[slot, :, span].T
            for k in range(3):
                term = jnp.dot(turned, grads[flip, k], preferred_element_type=jnp.float32)
                total[k, span, :] = term if flip == 0 else total[k, span, :] + term

        if flip < 2:
            fetched[slot] = fetch_tokens(flip + 2)
            fetched[slot].start()

    def weight_rest(i, part):
        slot = 3 % 2
        if i == 0 and part == 0:
            fetched[slot].wait()
        tops = [top + i * part_rows for top in (0, half)]

        @pl.loop(0, cols // BLOCK)
        def _(j):
            top = pl.multiple_of(j * BLOCK, BLOCK)
            span = pl.ds(pl.multiple_of(part * cols + top, BLOCK), BLOCK)
            turned = [tokens_buf[slot, pl.ds(t, part_rows), span].T for t in tops]
            for k in range(3):
                term = total[k, span, :]
                for t, rows_of in zip(tops, turned):
                    term = term + jnp.dot(
                        rows_of, grads[3, k, pl.ds(t, part_rows)], preferred_element_type=jnp.float32
                    )
                if i == 0:
                    total[k, span, :] = term
                else:
                    rows_buf[part, k, pl.ds(top, BLOCK), :] = term.astype(jnp.bfloat16)

    for p in range(2):
        input_half(0, p)
        pass_half(0, p)
    for p in range(2):
        input_half(1, p)
    weight_block(0)
    side[0].wait_recv()
    side[1].wait_recv()
    for moves in far:
        for move in moves:
            move.start()
    for p in range(2):
        pass_half(1, p)
    for p in range(2):
        input_half(2, p)
    side[2].wait_recv()
    weight_block(1)
    for p in range(2):
        pass_half(2, p)
    for p in range(2):
        input_half(3, p)
        pass_half(3, p)
    keep_copy = pltpu.make_async_copy(keep, keep_out, local.at[6])
    keep_copy.start()
    side[3].wait_recv()
    weight_block(2)
    stores = [
        pltpu.make_async_copy(
            rows_buf.at[part], weight_out.at[:, pl.ds(part * cols, cols)], local.at[part]
        )
        for part in range(2)
    ]
    for i in range(2):
        for move in far[i]:
            move.wait_recv()
        for part in range(2):
            weight_rest(i, part)
            if i == 1:
                stores[part].start()
    for move in ring[2]:
        move.wait_recv()
    for move in (keep_copy, *stores):
        move.wait()
    for moves in (side, *far, *ring, twin[2], twin[3]):
        for move in moves:
            move.wait_send()


def close_kernel(keep_ref, last_ref, rows_ref, input_ref, weight_ref):
    input_ref[...] = (keep_ref[...] + last_ref[...].astype(jnp.float32)).astype(jnp.bfloat16)
    weight_ref[...] = rows_ref[...]


def close_call(keep, last, weight):
    (tokens, cols), (_, rows, local_cols) = keep.shape, weight.shape
    steps = 2
    input_spec = pl.BlockSpec((tokens // steps, cols), lambda i: (i, 0))
    weight_spec = pl.BlockSpec((3, rows // steps, local_cols), lambda i: (0, i, 0))
    return pl.pallas_call(
        close_kernel,
        grid=(steps,),
        in_specs=[input_spec, input_spec, weight_spec],
        out_specs=[input_spec, weight_spec],
        out_shape=[
            jax.ShapeDtypeStruct(keep.shape, jnp.bfloat16),
            jax.ShapeDtypeStruct(weight.shape, weight.dtype),
        ],
        compiler_params=pltpu.CompilerParams(vmem_limit_bytes=62 << 20),
        name="close",
    )(keep, last, weight)


def finish_call(gradient, feats, wall, swap):
    _, tokens, local_cols = gradient.shape
    rows = wall.shape[2]
    cols = rows // 2
    bf16, f32 = jnp.bfloat16, jnp.float32
    anywhere = pl.BlockSpec(memory_space=pl.ANY)
    return pl.pallas_call(
        finish_kernel,
        in_specs=[anywhere] * 4,
        out_specs=[anywhere] * 3,
        out_shape=[
            jax.ShapeDtypeStruct((tokens, cols), f32),
            jax.ShapeDtypeStruct((tokens, cols), bf16),
            jax.ShapeDtypeStruct((3, rows, local_cols), bf16),
        ],
        scratch_shapes=[
            pltpu.VMEM((4, 3, tokens, local_cols), bf16),
            pltpu.VMEM((2, tokens, rows), bf16),
            pltpu.VMEM((2, 3, cols, local_cols), bf16),
            pltpu.VMEM((3, rows, local_cols), f32),
            pltpu.VMEM((tokens, cols), f32),
            pltpu.VMEM((2, tokens, cols), bf16),
            pltpu.VMEM((4, tokens, cols), bf16),
            pltpu.VMEM((3, tokens, cols), bf16),
            pltpu.VMEM((2, tokens, cols), bf16),
            pltpu.SemaphoreType.DMA((22,)),
            pltpu.SemaphoreType.DMA((22,)),
            pltpu.SemaphoreType.DMA((7,)),
        ],
        compiler_params=pltpu.CompilerParams(
            collective_id=1, has_side_effects=True, vmem_limit_bytes=60 << 20
        ),
        name="finish",
    )(gradient, feats, wall, swap)


def fast_body(inputs, projection, cotangent, log_decay, document_starts):
    feats, wall, gradient, swap = gather_call(
        document_starts, log_decay, inputs, projection.transpose(1, 0, 2), cotangent
    )
    input_gradient, weight_gradient = close_call(*finish_call(gradient, feats, wall, swap))
    return (input_gradient, weight_gradient.transpose(1, 0, 2))


def solution(mesh):
    fast = (mesh.shape["seq"], mesh.shape["head"]) == (4, 8)
    placed = (P("seq", "head"), P("seq", None, "head"), P("seq", "head"), P("head", "seq"), P())
    return jax.shard_map(
        fast_body if fast else general_body,
        mesh=mesh,
        in_specs=placed,
        out_specs=(P("seq", "head"), P("seq", None, "head")),
        check_vma=False,
    )
```
